32 devices in a mesh: groups: 2 (over x), seq: 16 (over z, y, core).
Axes of the slice: x: 2, y: 2, z: 4, core: 2. Of those that a mesh axis runs over, the one named last changes fastest.
Arguments:
- tokens: bfloat16 [96, 5120], P(('groups', 'seq')), parts along dimension 0, may hold values from -6 to 6
- modulation: float32 [6, 5120], replicated, may hold values from -2.5 to 2.5
- w_qkv: bfloat16 [3, 5120, 2560], P(None, None, 'seq'), may hold values from -0.078125 to 0.078125
- norm_gains: float32 [2, 2560], replicated, may hold values from 0.56 to 12
- cache_kv: bfloat16 [2, 2, 96, 2560], P(None, None, ('groups', 'seq')), parts along dimension 2, may hold values from -17 to 17
- w_out: bfloat16 [2560, 5120], P(None, 'seq'), may hold values from -0.125 to 0.125
- w_up: bfloat16 [5120, 13824], P(None, 'seq'), may hold values from -0.078125 to 0.078125
- w_down: bfloat16 [13824, 5120], P('seq'), may hold values from -0.0546875 to 0.0546875
Outputs:
- block_out: bfloat16 [96, 5120], P(('groups', 'seq')), parts along dimension 0
The draws below stay inside these ranges and needn't reach their ends.
There are 2 independent parts, one for each index of `groups`. The reference program is written for one: setup_inputs(seed, part) draws one part's arguments, and reference() takes and returns one part's arrays. A program takes and returns all parts, laid end to end along the dimension named above; an argument that names none is the same for every part. Nothing has to cross between parts.
All inputs are finite; a program needn't handle non-finite values.
Results may differ from the reference program's by a relative error of at most 0.017.
The reference program's roundings to bfloat16 on the way (of `normed`, `qkv`, `weights`, `attended`, `projected`, `normed2` and `hidden`) count: a program that leaves them out, or rounds other values in their place, can miss the bound.
Values may be sent and summed in bfloat16 or wider, within the bound.
A program may use at most 128 MiB of HBM per device.

```python
import math
import jax
import jax.numpy as jnp
from jax import lax

D = 5120
FF = 13824
HEAD_DIM = 128
HEADS = 20
FRAMES = 2
ATTN = 2560
TOKENS = 48


def draw_norm_gains(key, part):
    key_one, key_two = jax.random.split(jax.random.fold_in(key, 11))
    lower, upper = (0.7, 1.6)
    head_scale = jnp.exp(jax.random.uniform(key_one, (2, HEADS, 1), jnp.float32, math.log(lower), math.log(upper)))
    channel = jax.random.uniform(key_two, (2, HEADS, HEAD_DIM), jnp.float32, 0.8, 1.2)
    return (head_scale * channel).reshape(2, HEADS * HEAD_DIM)


def draw_cache_kv(key, part):
    key_one, key_two, key_three = jax.random.split(jax.random.fold_in(key, 23), 3)
    shape = (FRAMES, TOKENS, HEADS, HEAD_DIM)
    head_scale = jnp.exp(jax.random.uniform(key_one, (1, 1, HEADS, 1), jnp.float32, math.log(0.7), math.log(1.6)))
    keys = jnp.clip(jax.random.normal(key_two, shape, jnp.float32), -4.0, 4.0) * head_scale
    values = jnp.clip(jax.random.normal(key_three, shape, jnp.float32), -4.0, 4.0)
    stacked = jnp.stack([keys, values]).reshape(2, FRAMES, TOKENS, HEADS * HEAD_DIM)
    return stacked.astype(jnp.bfloat16)


def levels(rng, dims, cuts, least, top_value):
    loudness, own = 1.0, jax.random.fold_in(rng, 6)
    for position, parts in cuts:
        heights = jnp.exp(jax.random.uniform(jax.random.fold_in(own, position), (parts,), jnp.float32, least / len(cuts), top_value / len(cuts)))
        loudness = loudness * jnp.repeat(heights, dims[position] // parts).reshape([-1 if axis == position else 1 for axis in range(len(dims))])
    return loudness


def scatter_about(own_key, shape, scale, reach, shards=(), dtype=jnp.bfloat16):
    values = scale * jax.random.normal(own_key, shape, jnp.float32)
    if shards:
        values = values * levels(own_key, shape, shards, -0.22, 0.18)
    return jnp.clip(values, -reach, reach).astype(dtype)


def setup_inputs(seed: int = 0, part: int = 0) -> dict:
    key_of = jax.random.split(jax.random.key(seed), 9)
    part_splits = jax.random.split(jax.random.fold_in(key_of[8], part), 9)
    return {
        "tokens": scatter_about(part_splits[0], (TOKENS, D), 1.0, 6.0, ((0, 16),)),
        "modulation": scatter_about(key_of[1], (6, D), 0.6, 2.5, (), jnp.float32),
        "w_qkv": scatter_about(key_of[2], (3, D, ATTN), D ** -0.5, 0.078125, ((2, 16),)),
        "norm_gains": draw_norm_gains(jax.random.fold_in(key_of[8], 71), part),
        "cache_kv": draw_cache_kv(jax.random.fold_in(jax.random.fold_in(key_of[8], part), 71), part),
        "w_out": scatter_about(key_of[5], (ATTN, D), ATTN ** -0.5, 0.125, ((1, 16),)),
        "w_up": scatter_about(key_of[6], (D, FF), D ** -0.5, 0.078125, ((1, 16),)),
        "w_down": scatter_about(key_of[7], (FF, D), FF ** -0.5, 0.0546875, ((0, 16),)),
    }


def layer_norm(values):
    center = values - lax.optimization_barrier(jnp.mean(values, axis=-1, keepdims=True))
    spread = lax.optimization_barrier(jnp.mean(center * center, axis=-1, keepdims=True))
    return center * lax.rsqrt(spread + 1e-06)

def rms_norm(values, gain):
    return values * lax.rsqrt(lax.optimization_barrier(jnp.mean(values * values, axis=-1, keepdims=True)) + 1e-06) * gain

def reference(tokens, modulation, w_qkv, norm_gains, cache_kv, w_out, w_up, w_down):
    residual = tokens.astype(jnp.float32)
    normed = (layer_norm(residual) * (1.0 + modulation[1]) + modulation[0]).astype(jnp.bfloat16)
    qkv = [jnp.dot(normed, w_qkv[index], preferred_element_type=jnp.float32).astype(jnp.bfloat16) for index in range(3)]
    queries = rms_norm(qkv[0].astype(jnp.float32), norm_gains[0]).astype(jnp.bfloat16)
    keys_now = rms_norm(qkv[1].astype(jnp.float32), norm_gains[1]).astype(jnp.bfloat16)
    keys = jnp.concatenate([cache_kv[0].reshape(FRAMES * TOKENS, ATTN), keys_now], axis=0)
    values = jnp.concatenate([cache_kv[1].reshape(FRAMES * TOKENS, ATTN), qkv[2]], axis=0)
    scale = 1.0 / math.sqrt(HEAD_DIM)
    query_heads = queries.reshape(TOKENS, HEADS, HEAD_DIM).transpose(1, 0, 2)
    key_heads = keys.reshape(-1, HEADS, HEAD_DIM).transpose(1, 0, 2)
    value_heads = values.reshape(-1, HEADS, HEAD_DIM).transpose(1, 0, 2)

    def one_head(operands):
        query_h, key_h, value_h = operands
        scores = jnp.dot(query_h, key_h.T, preferred_element_type=jnp.float32) * scale
        peak = lax.optimization_barrier(jnp.max(scores, axis=-1, keepdims=True))
        expo = jnp.exp(scores - peak)
        total = lax.optimization_barrier(jnp.sum(expo, axis=-1, keepdims=True))
        weights = expo.astype(jnp.bfloat16)
        return jnp.dot(weights, value_h, preferred_element_type=jnp.float32) / total
    heads_out = lax.map(one_head, (query_heads, key_heads, value_heads))
    attended = heads_out.transpose(1, 0, 2).reshape(TOKENS, ATTN).astype(jnp.bfloat16)
    projected = jnp.dot(attended, w_out, preferred_element_type=jnp.float32).astype(jnp.bfloat16)
    residual = residual + modulation[2] * projected.astype(jnp.float32)
    normed2 = (layer_norm(residual) * (1.0 + modulation[4]) + modulation[3]).astype(jnp.bfloat16)
    hidden = jax.nn.gelu(jnp.dot(normed2, w_up, preferred_element_type=jnp.float32), approximate=True).astype(jnp.bfloat16)
    feed = jnp.dot(hidden, w_down, preferred_element_type=jnp.float32)
    return (residual + modulation[5] * feed).astype(jnp.bfloat16)
```

```python
import math

import jax
import jax.numpy as jnp
from jax import lax
from jax.experimental import pallas as pl
from jax.experimental.pallas import tpu as pltpu
from jax.sharding import PartitionSpec as P

HEAD_DIM = 128
HEADS = 20
SLOT = 16
MESH = pl.DeviceIdType.MESH
NT = (((1,), (1,)), ((), ()))
NN = (((1,), (0,)), ((), ()))
F32 = jnp.float32
BF16 = jnp.bfloat16


def factors(n):
    chips = n // 2
    near = 1
    while (2 * near) * (2 * near) <= chips:
        near *= 2
    return chips // near, near


def loop(low, high, fn):
    if high - low <= 8:
        for i in range(low, high):
            fn(i)
        return

    def step(i, c):
        fn(i)
        return c

    lax.fori_loop(low, high, step, 0)


def xor(value, k, size):
    total, bit = 0, 1
    while bit < size:
        digit = lax.rem(lax.div(value, bit), 2)
        other = (k // bit) % 2
        if isinstance(other, int):
            digit = 1 - digit if other else digit
        else:
            digit = lax.rem(digit + other, 2)
        total = total + bit * digit
        bit *= 2
    return total


def remote_copy(src, dst, send, recv, device):
    return pltpu.make_async_remote_copy(
        src_ref=src, dst_ref=dst, send_sem=send, recv_sem=recv, device_id={"seq": device}, device_id_type=MESH
    )


def fold(x):
    total = x[:, :128]
    for k in range(1, x.shape[1] // 128):
        total = total + x[:, 128 * k : 128 * (k + 1)]
    return total


def gelu(x):
    return 0.5 * x * (1.0 + jnp.tanh(math.sqrt(2.0 / math.pi) * (x + 0.044715 * (x * x * x))))


def fused(n, tokens, modulation, wq, gains, cache, wo, wu, wd):
    far, near = factors(n)
    own_rows, features = tokens.shape
    rows = n * own_rows
    width = HEADS * HEAD_DIM
    cols = wq.shape[1]
    wide = math.lcm(cols, HEAD_DIM)
    gs = wide // cols
    blocks = n // gs
    heads = wide // HEAD_DIM
    frames = cache.shape[2]
    held = frames * own_rows
    span = gs // (2 * near)
    part_rows = rows // (2 * span)
    oc = wo.shape[0]
    fl = wu.shape[0]
    chunks = features // wide
    pack = own_rows * chunks
    group = wide // oc
    scale = 1.0 / math.sqrt(HEAD_DIM)
    assert held <= SLOT // 2 and rows // group == pack and gs % (2 * near) == 0 and far % blocks == 0

    def body(
        tok, mod, wq_h, gains_h, cache_h, wo_h, wu_h, wd_h, out,
        tok_v, mod_v, gains_v, cache_v, wq_v, wo_v, wu_v, wd_v,
        t32, pack32, gt, normed, c32, cown, kv, qacc, qk, sq, q32, att,
        gp, res, hacc, hid, p16, got1, sum1, got2, sum2, got3,
        lsem, tsend, trecv, csend, crecv, qsend, qrecv, ssend, srecv, asend, arecv, psend, precv,
        rsend, r1, r2, r3,
    ):
        me = lax.axis_index("seq")
        a, b, c = lax.div(me, 2 * near), lax.rem(lax.div(me, 2), near), lax.rem(me, 2)
        block, place = lax.div(me, gs), lax.rem(me, gs)
        base = block * gs
        part = lax.rem(a, span) * 2 + c

        def dev(a2, b2, c2):
            return (a2 * near + b2) * 2 + c2

        def fetch(k, src, dst):
            copy = pltpu.make_async_copy(src, dst, lsem.at[k])
            copy.start()
            return copy

        get_tok = fetch(0, tok, tok_v)
        get_cache = fetch(1, cache_h, cache_v)
        get_mod = fetch(2, mod, mod_v)
        get_gains = fetch(3, gains_h, gains_v)
        get_wq = fetch(4, wq_h, wq_v)
        get_wo = fetch(5, wo_h, wo_v)
        get_wu = fetch(6, wu_h, wu_v)
        get_wd = fetch(7, wd_h, wd_v)

        barrier = pltpu.get_barrier_semaphore()

        def signal(i, carry):
            pl.semaphore_signal(barrier, inc=1, device_id={"seq": lax.rem(me + i, n)}, device_id_type=MESH)
            return carry

        lax.fori_loop(1, n, signal, 0)

        def at_pack(d):
            return pl.ds(pl.multiple_of(d * pack, 8), pack)

        def put(d, x):
            for l in range(heads):
                t32[l, at_pack(d), :] = x[:, HEAD_DIM * l : HEAD_DIM * (l + 1)]

        def take(d):
            return jnp.concatenate([t32[l, at_pack(d), :] for l in range(heads)], axis=1)

        def lanes(k):
            return pl.ds(pl.multiple_of(k * wide, wide), wide)

        get_tok.wait()
        for k in range(chunks):
            pack32[own_rows * k : own_rows * (k + 1), :] = tok_v[:, wide * k : wide * (k + 1)].astype(F32)
        put(me, pack32[...])
        gt[me] = pack32[...].astype(BF16)
        get_cache.wait()
        c32[...] = jnp.zeros_like(c32)
        for side in range(2):
            for r in range(own_rows):
                at = SLOT // 2 * side + frames * r
                c32[at : at + frames, :] = cache_v[side, r].astype(F32)
        for k in range(blocks):
            cown[k] = c32[:, wide * k : wide * (k + 1)].astype(BF16)
        kv[me] = c32[:, lanes(block)].astype(BF16)

        pl.semaphore_wait(barrier, n - 1)

        def gather(dst, send, recv, own_part=None):
            def far_copy(i):
                a2 = xor(a, i, far)
                src = dst.at[me] if own_part is None else own_part.at[lax.div(a2 * 2 * near, gs)]
                return remote_copy(src, dst.at[me], send.at[0, i], recv.at[me], dev(a2, b, c))

            def near_copy(i, j):
                row = dev(xor(a, i, far), b, c)
                return remote_copy(
                    dst.at[row], dst.at[row], send.at[1, i * near + j], recv.at[row], dev(a, xor(b, j, near), c)
                )

            def core_copy(i, j):
                row = dev(xor(a, i, far), xor(b, j, near), c)
                return remote_copy(dst.at[row], dst.at[row], send.at[2, i * near + j], recv.at[row], dev(a, b, 1 - c))

            def arrived(row):
                remote_copy(dst.at[row], dst.at[row], send.at[0, 0], recv.at[row], me).wait_recv()

            def begin():
                loop(1, far, lambda i: far_copy(i).start())

            def begin_near():
                loop(1, near, lambda j: near_copy(0, j).start())
                core_copy(0, 0).start()

            def forward(use):
                def one(i):
                    row = dev(xor(a, i, far), b, c)
                    arrived(row)
                    loop(1, near, lambda j: near_copy(i, j).start())
                    core_copy(i, 0).start()
                    use(row)

                loop(1, far, one)

            def across(use):
                def one(m):
                    i, j = m % far, 1 + m // far
                    row = dev(xor(a, i, far), xor(b, j, near), c)
                    arrived(row)
                    core_copy(i, j).start()
                    use(row)

                loop(0, far * (near - 1), one)

            def finish(use):
                def one(m):
                    row = dev(xor(a, m % far, far), xor(b, m // far, near), 1 - c)
                    arrived(row)
                    use(row)

                loop(0, far * near, one)

            def drain():
                loop(1, far, lambda i: far_copy(i).wait_send())
                loop(0, far * (near - 1), lambda m: near_copy(m % far, 1 + m // far).wait_send())
                loop(0, far * near, lambda m: core_copy(m % far, m // far).wait_send())

            return begin, begin_near, forward, across, finish, drain

        nothing = lambda row: None
        t_begin, t_near, t_forward, t_across, t_finish, t_drain = gather(gt, tsend, trecv)
        c_begin, c_near, c_forward, c_across, c_finish, c_drain = gather(kv, csend, crecv, cown)

        def ingest(row):
            put(row, gt[row].astype(F32))

        t_begin()
        t_near()
        c_begin()
        t_forward(ingest)
        t_across(ingest)
        c_near()
        t_finish(ingest)
        c_forward(nothing)

        def token_chunk(k):
            return jnp.concatenate(
                [
                    jnp.concatenate(
                        [t32[l, pl.ds(own_rows * k + r, n, stride=pack), :] for r in range(own_rows)], axis=0
                    )
                    for l in range(heads)
                ],
                axis=1,
            )

        def layer_norm(chunk, shift, gain):
            total = jnp.zeros((rows, 128), F32)
            for k in range(chunks):
                total = total + fold(chunk(k))
            mean = jnp.sum(total, axis=-1, keepdims=True) * (1.0 / features)
            total = jnp.zeros((rows, 128), F32)
            for k in range(chunks):
                center = chunk(k) - mean
                total = total + fold(center * center)
            inverse = lax.rsqrt(jnp.sum(total, axis=-1, keepdims=True) * (1.0 / features) + 1e-06)
            for k in range(chunks):
                s = slice(wide * k, wide * (k + 1))
                normed[:, s] = (
                    (chunk(k) - mean) * inverse * (1.0 + mod_v[gain : gain + 1, s]) + mod_v[shift : shift + 1, s]
                ).astype(BF16)

        get_mod.wait()
        layer_norm(token_chunk, 0, 1)

        get_wq.wait()
        depth = features // 4
        qacc[...] = jnp.zeros_like(qacc)

        def project(k, carry):
            s = pl.ds(pl.multiple_of(k * depth, depth), depth)
            x = normed[:, s]
            if cols % 16 == 0:
                qacc[...] += lax.dot_general(
                    x, wq_v[:, :, s].reshape(3 * cols, depth), NT, preferred_element_type=F32
                )
            else:
                for i in range(3):
                    qacc[:, cols * i : cols * (i + 1)] += lax.dot_general(
                        x, wq_v[i, :, s], NT, preferred_element_type=F32
                    )
            return carry

        lax.fori_loop(0, 4, project, 0)
        rounded = qacc[...].astype(BF16)
        qk[place] = rounded

        def peer(i):
            return remote_copy(
                qk.at[place], qk.at[place], qsend.at[i], qrecv.at[place], base + xor(place, i, gs)
            )

        loop(1, gs, lambda i: peer(gs - i).start())
        exact = rounded.astype(F32)
        lane = lax.broadcasted_iota(jnp.int32, (8, 3 * cols), 1)
        line = lax.broadcasted_iota(jnp.int32, (8, 3 * cols), 0)
        pick = jnp.where((lane >= line * cols) & (lane < line * cols + cols), 1.0, 0.0)
        sums = lax.dot_general(
            pick, exact * exact, NT, preferred_element_type=F32, precision=lax.Precision.HIGHEST
        )
        sq[me] = sums[:2]

        def spread(i):
            return remote_copy(sq.at[me], sq.at[me], ssend.at[i], srecv.at[me], lax.rem(me + i, n))

        loop(1, n, lambda i: spread(i).start())
        c_across(nothing)

        def squares_in(i):
            row = lax.rem(me + i, n)
            remote_copy(sq.at[row], sq.at[row], ssend.at[i], srecv.at[row], me).wait_recv()

        loop(1, n, squares_in)
        both = lax.rsqrt(jnp.sum(sq[...], axis=0) * (1.0 / width) + 1e-06)
        eye = jnp.where(
            lax.broadcasted_iota(jnp.int32, (rows, rows), 0) == lax.broadcasted_iota(jnp.int32, (rows, rows), 1),
            1.0,
            0.0,
        )
        inverse = lax.dot_general(eye, both, NT, preferred_element_type=F32, precision=lax.Precision.HIGHEST)

        def peer_in(i):
            row = xor(place, i, gs)
            remote_copy(qk.at[row], qk.at[row], qsend.at[i], qrecv.at[row], me).wait_recv()

        loop(1, gs, peer_in)
        get_gains.wait()

        def whole(i):
            return jnp.concatenate([qk[p, :, cols * i : cols * (i + 1)].astype(F32) for p in range(gs)], axis=1)

        q32[...] = whole(0) * inverse[:, 0:1] * gains_v[0:1, lanes(block)]
        keys = (whole(1) * inverse[:, 1:2] * gains_v[1:2, lanes(block)]).astype(BF16)
        values = whole(2).astype(BF16)
        queries = q32[pl.ds(pl.multiple_of(part * part_rows, 8), part_rows), :].astype(BF16)

        c_finish(nothing)
        spot = lax.rem(lax.broadcasted_iota(jnp.int32, (part_rows, n * SLOT), 1), SLOT)
        for h in range(heads):
            s = slice(HEAD_DIM * h, HEAD_DIM * (h + 1))
            cached = kv[:, :, s].reshape(n * SLOT, HEAD_DIM)
            old = lax.dot_general(queries[:, s], cached, NT, preferred_element_type=F32) * scale
            new = lax.dot_general(queries[:, s], keys[:, s], NT, preferred_element_type=F32) * scale
            old = jnp.where(spot < held, old, -jnp.inf)
            peak = jnp.maximum(jnp.max(old, axis=-1, keepdims=True), jnp.max(new, axis=-1, keepdims=True))
            old, new = jnp.exp(old - peak), jnp.exp(new - peak)
            total = jnp.sum(old, axis=-1, keepdims=True) + jnp.sum(new, axis=-1, keepdims=True)
            moved = pltpu.roll(old, SLOT // 2, axis=1).astype(BF16)
            summed = lax.dot_general(moved, cached, NN, preferred_element_type=F32) + lax.dot_general(
                new.astype(BF16), values[:, s], NN, preferred_element_type=F32
            )
            att[a, c, :, s] = (summed / total).astype(BF16)

        def att_far(i):
            return remote_copy(
                att.at[a, c], att.at[a, c], asend.at[0, i], arecv.at[a, c], dev(xor(a, i, far), b, c)
            )

        def att_core(i):
            a2 = xor(a, i, far)
            return remote_copy(
                att.at[a2, c], att.at[a2, c], asend.at[1, i], arecv.at[a2, c], dev(a, b, 1 - c)
            )

        def att_in(a2, c2):
            remote_copy(att.at[a2, c2], att.at[a2, c2], asend.at[0, 0], arecv.at[a2, c2], me).wait_recv()

        loop(1, far, lambda i: att_far(far - i).start())
        att_core(0).start()

        def att_pass(i):
            att_in(xor(a, i, far), c)
            att_core(i).start()

        loop(1, far, att_pass)
        loop(0, far, lambda i: att_in(xor(a, i, far), 1 - c))

        get_wo.wait()
        projected = jnp.zeros((rows, oc), F32)
        for k in range(blocks):
            x = att[span * k : span * (k + 1)].astype(F32).reshape(rows, wide).astype(BF16)
            projected = projected + lax.dot_general(
                x, wo_v[:, wide * k : wide * (k + 1)], NT, preferred_element_type=F32
            )
        gp[me] = jnp.concatenate([projected[pack * g : pack * (g + 1)] for g in range(group)], axis=1).astype(BF16)

        p_begin, p_near, p_forward, p_across, p_finish, p_drain = gather(gp, psend, precv)
        p_begin()
        p_near()
        p_forward(nothing)
        p_across(nothing)
        p_finish(nothing)

        for k in range(chunks):
            pieces = [gp[group * k + j].astype(F32) for j in range(group)]
            s = slice(wide * k, wide * (k + 1))
            full = jnp.concatenate(
                [
                    jnp.concatenate([piece[:, oc * g : oc * (g + 1)] for piece in pieces], axis=1)
                    for g in range(group)
                ],
                axis=0,
            )
            res[:, s] = token_chunk(k) + mod_v[2:3, s] * full
        layer_norm(lambda k: res[:, wide * k : wide * (k + 1)], 3, 4)

        get_wu.wait()
        deep = features // 2
        hacc[...] = lax.dot_general(normed[:, :deep], wu_v[:, :deep], NT, preferred_element_type=F32)
        hacc[...] += lax.dot_general(normed[:, deep:], wu_v[:, deep:], NT, preferred_element_type=F32)
        hid[...] = gelu(hacc[...]).astype(BF16)
        get_wd.wait()
        for k in range(chunks):
            part_sum = lax.dot_general(
                hid[...], wd_v[:, wide * k : wide * (k + 1)], NN, preferred_element_type=F32
            )
            for r in range(own_rows):
                for l in range(heads):
                    t32[l, pl.ds(own_rows * k + r, n, stride=pack), :] = part_sum[
                        n * r : n * (r + 1), HEAD_DIM * l : HEAD_DIM * (l + 1)
                    ]

        def copy1(m):
            i, j = far - 1 - m // near, near - 1 - m % near
            chip = xor(a, i, far) * near + xor(b, j, near)
            return chip, remote_copy(p16.at[chip], got1.at[chip], rsend.at[0, m], r1.at[chip], dev(a, b, 1 - c))

        def hand(m):
            chip, copy = copy1(m)
            p16[chip] = take(2 * chip + 1 - c).astype(BF16)
            copy.start()

        loop(0, far * near, hand)

        def pair(chip):
            remote_copy(got1.at[chip], got1.at[chip], rsend.at[0, 0], r1.at[chip], me).wait_recv()
            return take(2 * chip + c) + got1[chip].astype(F32)

        def copy2(m):
            i, j = far - 1 - m // (near - 1), near - 1 - m % (near - 1)
            a2, b2 = xor(a, i, far), xor(b, j, near)
            chip = a2 * near + b2
            at = a2 * near + b
            return chip, remote_copy(sum1.at[chip], got2.at[at], rsend.at[1, m], r2.at[at], dev(a, b2, c))

        def second(m):
            chip, copy = copy2(m)
            sum1[chip] = pair(chip).astype(BF16)
            copy.start()

        loop(0, far * (near - 1), second)

        def collect(i):
            a2 = xor(a, i, far)
            total = pair(a2 * near + b)
            for j in range(1, near):
                at = a2 * near + xor(b, j, near)
                remote_copy(got2.at[at], got2.at[at], rsend.at[1, 0], r2.at[at], me).wait_recv()
                total = total + got2[at].astype(F32)
            return a2, total

        def copy3(i):
            a2 = xor(a, i, far)
            return remote_copy(sum2.at[a2], got3.at[a], rsend.at[2, i], r3.at[a], dev(a2, b, c))

        def third(m):
            i = far - m
            a2, total = collect(i)
            sum2[a2] = total.astype(BF16)
            copy3(i).start()

        loop(1, far, third)
        _, total = collect(0)
        for i in range(1, far):
            a2 = xor(a, i, far)
            remote_copy(got3.at[a2], got3.at[a2], rsend.at[2, 0], r3.at[a2], me).wait_recv()
            total = total + got3[a2].astype(F32)
        pack32[...] = total
        for k in range(chunks):
            s = slice(wide * k, wide * (k + 1))
            feed = pack32[own_rows * k : own_rows * (k + 1), :]
            own = jnp.concatenate([res[pl.ds(me + n * r, 1), s] for r in range(own_rows)], axis=0)
            out[:, s] = (own + mod_v[5:6, s] * feed).astype(BF16)

        t_drain()
        c_drain()
        p_drain()
        loop(1, gs, lambda i: peer(i).wait_send())
        loop(1, n, lambda i: spread(i).wait_send())
        loop(1, far, lambda i: att_far(i).wait_send())
        loop(0, far, lambda i: att_core(i).wait_send())
        loop(0, far * near, lambda m: copy1(m)[1].wait_send())
        loop(0, far * (near - 1), lambda m: copy2(m)[1].wait_send())
        loop(1, far, lambda i: copy3(i).wait_send())

    def vmem(shape, dtype):
        return pltpu.VMEM(shape, dtype)

    dma = pltpu.SemaphoreType.DMA
    chips = far * near
    packed = (pack, wide)
    return pl.pallas_call(
        body,
        out_shape=jax.ShapeDtypeStruct(tokens.shape, BF16),
        in_specs=[pl.BlockSpec(memory_space=pl.ANY)] * 8,
        out_specs=pl.BlockSpec(memory_space=pltpu.VMEM),
        scratch_shapes=[
            vmem(tokens.shape, BF16),
            vmem(modulation.shape, F32),
            vmem(gains.shape, F32),
            vmem(cache.shape, BF16),
            vmem(wq.shape, BF16),
            vmem(wo.shape, BF16),
            vmem(wu.shape, BF16),
            vmem(wd.shape, BF16),
            vmem((heads, n * pack, HEAD_DIM), F32),
            vmem(packed, F32),
            vmem((n,) + packed, BF16),
            vmem((rows, features), BF16),
            vmem((SLOT, width), F32),
            vmem((blocks, SLOT, wide), BF16),
            vmem((n, SLOT, wide), BF16),
            vmem((rows, 3 * cols), F32),
            vmem((gs, rows, 3 * cols), BF16),
            vmem((n, 2, rows), F32),
            vmem((rows, wide), F32),
            vmem((far, 2, part_rows, wide), BF16),
            vmem((n,) + packed, BF16),
            vmem((rows, features), F32),
            vmem((rows, fl), F32),
            vmem((rows, fl), BF16),
            vmem((chips,) + packed, BF16),
            vmem((chips,) + packed, BF16),
            vmem((chips,) + packed, BF16),
            vmem((chips,) + packed, BF16),
            vmem((far,) + packed, BF16),
            vmem((far,) + packed, BF16),
            dma((8,)),
            dma((3, chips)),
            dma((n,)),
            dma((3, chips)),
            dma((n,)),
            dma((gs,)),
            dma((gs,)),
            dma((n,)),
            dma((n,)),
            dma((2, far)),
            dma((far, 2)),
            dma((3, chips)),
            dma((n,)),
            dma((3, chips)),
            dma((chips,)),
            dma((chips,)),
            dma((far,)),
        ],
        compiler_params=pltpu.CompilerParams(
            collective_id=0, has_side_effects=True, vmem_limit_bytes=60 * 1024 * 1024
        ),
        name="block",
    )(tokens, modulation, wq, gains, cache, wo, wu, wd)


def solution(mesh):
    n = mesh.shape["seq"]
    in_specs = (
        P(("groups", "seq"), None),
        P(),
        P(None, None, "seq"),
        P(),
        P(None, None, ("groups", "seq"), None),
        P(None, "seq"),
        P(None, "seq"),
        P("seq", None),
    )
    out_specs = P(("groups", "seq"), None)

    def step(tokens, modulation, w_qkv, norm_gains, cache_kv, w_out, w_up, w_down):
        return fused(
            n,
            tokens,
            modulation,
            jnp.swapaxes(w_qkv, 1, 2),
            norm_gains,
            jnp.swapaxes(cache_kv, 1, 2),
            w_out.T,
            w_up.T,
            w_down,
        )

    return jax.shard_map(step, mesh=mesh, in_specs=in_specs, out_specs=out_specs, check_vma=False)
```

```python
import math

import jax
import jax.numpy as jnp
from jax import lax
from jax.experimental import pallas as pl
from jax.experimental.pallas import tpu as pltpu
from jax.sharding import PartitionSpec as P

HEAD_DIM = 128
HEADS = 20
SLOT = 16
MESH = pl.DeviceIdType.MESH
NT = (((1,), (1,)), ((), ()))
NN = (((1,), (0,)), ((), ()))
F32 = jnp.float32
BF16 = jnp.bfloat16


def factors(n):
    chips = n // 2
    near = 1
    while (2 * near) * (2 * near) <= chips:
        near *= 2
    return chips // near, near


def loop(low, high, fn):
    if high - low <= 8:
        for i in range(low, high):
            fn(i)
        return

    def step(i, c):
        fn(i)
        return c

    lax.fori_loop(low, high, step, 0)


def xor(value, k, size):
    total, bit = 0, 1
    while bit < size:
        digit = lax.rem(lax.div(value, bit), 2)
        other = (k // bit) % 2
        if isinstance(other, int):
            digit = 1 - digit if other else digit
        else:
            digit = lax.rem(digit + other, 2)
        total = total + bit * digit
        bit *= 2
    return total


def remote_copy(src, dst, send, recv, device):
    return pltpu.make_async_remote_copy(
        src_ref=src, dst_ref=dst, send_sem=send, recv_sem=recv, device_id={"seq": device}, device_id_type=MESH
    )


def fold(x):
    total = x[:, :128]
    for k in range(1, x.shape[1] // 128):
        total = total + x[:, 128 * k : 128 * (k + 1)]
    return total


def gelu(x):
    return 0.5 * x * (1.0 + jnp.tanh(math.sqrt(2.0 / math.pi) * (x + 0.044715 * (x * x * x))))


def fused(n, tokens, modulation, wq, gains, cache, wo, wu, wd):
    far, near = factors(n)
    own_rows, features = tokens.shape
    rows = n * own_rows
    width = HEADS * HEAD_DIM
    cols = wq.shape[1]
    wide = math.lcm(cols, HEAD_DIM)
    gs = wide // cols
    blocks = n // gs
    heads = wide // HEAD_DIM
    frames = cache.shape[2]
    held = frames * own_rows
    span = gs // (2 * near)
    part_rows = rows // (2 * span)
    oc = wo.shape[0]
    fl = wu.shape[0]
    chunks = features // wide
    pack = own_rows * chunks
    group = wide // oc
    scale = 1.0 / math.sqrt(HEAD_DIM)
    tall = -(-rows // 128) * 128
    assert held <= SLOT // 2 and rows // group == pack and gs % (2 * near) == 0 and far % blocks == 0

    def body(
        tok, mod, wq_h, gains_h, cache_h, wo_h, wu_h, wd_h, out,
        tok_v, mod_v, gains_v, cache_v, wq_v, wo_v, wu_v, wd_v,
        t32, pack32, gt, normed, c32, cown, kv, qacc, qk, sq, q32, att,
        gp, res, hacc, hid, p16, got1, sum1, got2, sum2, got3,
        lsem, tsend, trecv, csend, crecv, qsend, qrecv, ssend, srecv, asend, arecv, psend, precv,
        rsend, r1, r2, r3,
    ):
        me = lax.axis_index("seq")
        a, b, c = lax.div(me, 2 * near), lax.rem(lax.div(me, 2), near), lax.rem(me, 2)
        block, place = lax.div(me, gs), lax.rem(me, gs)
        base = block * gs
        part = lax.rem(a, span) * 2 + c

        def dev(a2, b2, c2):
            return (a2 * near + b2) * 2 + c2

        def fetch(k, src, dst):
            copy = pltpu.make_async_copy(src, dst, lsem.at[k])
            copy.start()
            return copy

        barrier = pltpu.get_barrier_semaphore()

        partners = [dev(xor(a, i, far), b, c) for i in range(1, far)]
        partners += [dev(a, xor(b, j, near), c) for j in range(1, near)]
        partners += [dev(xor(a, far - 1, far), xor(b, j, near), c) for j in range(1, near)]
        partners += [dev(a, b, 1 - c)]
        for partner in partners:
            pl.semaphore_signal(barrier, inc=1, device_id={"seq": partner}, device_id_type=MESH)

        get_tok = fetch(0, tok, tok_v)
        get_cache = fetch(1, cache_h, cache_v)
        get_mod = fetch(2, mod, mod_v)
        get_gains = fetch(3, gains_h, gains_v)
        get_wq = fetch(4, wq_h, wq_v)
        get_wo = fetch(5, wo_h, wo_v)
        get_wu = fetch(6, wu_h, wu_v)
        get_wd = fetch(7, wd_h, wd_v)

        def at_pack(d):
            return pl.ds(pl.multiple_of(d * pack, 8), pack)

        def put(d, x):
            for l in range(heads):
                t32[l, at_pack(d), :] = x[:, HEAD_DIM * l : HEAD_DIM * (l + 1)]

        def take(d):
            return jnp.concatenate([t32[l, at_pack(d), :] for l in range(heads)], axis=1)

        def lanes(k):
            return pl.ds(pl.multiple_of(k * wide, wide), wide)

        get_tok.wait()
        for k in range(chunks):
            pack32[own_rows * k : own_rows * (k + 1), :] = tok_v[:, wide * k : wide * (k + 1)].astype(F32)
        put(me, pack32[...])
        gt[me] = pack32[...].astype(BF16)
        get_cache.wait()
        c32[...] = jnp.zeros_like(c32)
        for side in range(2):
            for r in range(own_rows):
                at = SLOT // 2 * side + frames * r
                c32[at : at + frames, :] = cache_v[side, r].astype(F32)
        for k in range(blocks):
            cown[k] = c32[:, wide * k : wide * (k + 1)].astype(BF16)
        kv[me] = c32[:, lanes(block)].astype(BF16)

        pl.semaphore_wait(barrier, len(partners))

        def gather(dst, send, recv, own_part=None):
            def far_copy(i):
                a2 = xor(a, i, far)
                src = dst.at[me] if own_part is None else own_part.at[lax.div(a2 * 2 * near, gs)]
                return remote_copy(src, dst.at[me], send.at[0, i], recv.at[me], dev(a2, b, c))

            def across_copy(j):
                b2 = xor(b, j, near)
                a2 = xor(a, far - 1, far)
                src = dst.at[me] if own_part is None else own_part.at[lax.div(a2 * 2 * near, gs)]
                at = (far - 1) * near + j
                return remote_copy(src, dst.at[me], send.at[1, at], recv.at[me], dev(a2, b2, c))

            def near_copy(i, j):
                row = dev(xor(a, i, far), b, c)
                return remote_copy(
                    dst.at[row], dst.at[row], send.at[1, i * near + j], recv.at[row], dev(a, xor(b, j, near), c)
                )

            def core_copy(i, j):
                row = dev(xor(a, i, far), xor(b, j, near), c)
                return remote_copy(dst.at[row], dst.at[row], send.at[2, i * near + j], recv.at[row], dev(a, b, 1 - c))

            def arrived(row):
                remote_copy(dst.at[row], dst.at[row], send.at[0, 0], recv.at[row], me).wait_recv()

            def begin():
                loop(1, far, lambda i: far_copy(far - 1 - i if i < far - 1 else i).start())
                loop(1, near, lambda j: across_copy(j).start())

            def begin_near():
                loop(1, near, lambda j: near_copy(0, j).start())
                core_copy(0, 0).start()

            def forward(use):
                def one(i):
                    row = dev(xor(a, i, far), b, c)
                    arrived(row)
                    if not isinstance(i, int) or i < far - 1:
                        loop(1, near, lambda j: near_copy(i, j).start())
                    core_copy(i, 0).start()
                    use(row)

                loop(1, far, one)

            def across(use):
                def one(m):
                    i, j = m % far, 1 + m // far
                    row = dev(xor(a, i, far), xor(b, j, near), c)
                    arrived(row)
                    core_copy(i, j).start()
                    use(row)

                loop(0, far * (near - 1), one)

            def finish(use):
                def one(m):
                    row = dev(xor(a, m % far, far), xor(b, m // far, near), 1 - c)
                    arrived(row)
                    use(row)

                loop(0, far * near, one)

            def drain():
                loop(1, far, lambda i: far_copy(i).wait_send())
                loop(0, (far - 1) * (near - 1), lambda m: near_copy(m % (far - 1), 1 + m // (far - 1)).wait_send())
                loop(1, near, lambda j: across_copy(j).wait_send())
                loop(0, far * near, lambda m: core_copy(m % far, m // far).wait_send())

            return begin, begin_near, forward, across, finish, drain

        nothing = lambda row: None
        t_begin, t_near, t_forward, t_across, t_finish, t_drain = gather(gt, tsend, trecv)
        c_begin, c_near, c_forward, c_across, c_finish, c_drain = gather(kv, csend, crecv, cown)

        def ingest(row):
            put(row, gt[row].astype(F32))

        t_begin()
        t_near()
        c_begin()
        t_forward(ingest)
        t_across(ingest)
        c_near()
        c_forward(nothing)
        t_finish(ingest)

        def token_chunk(k):
            return jnp.concatenate(
                [
                    jnp.concatenate(
                        [t32[l, pl.ds(own_rows * k + r, n, stride=pack), :] for r in range(own_rows)], axis=0
                    )
                    for l in range(heads)
                ],
                axis=1,
            )

        def layer_norm(chunk, shift, gain):
            total = jnp.zeros((rows, 128), F32)
            for k in range(chunks):
                total = total + fold(chunk(k))
            mean = jnp.sum(total, axis=-1, keepdims=True) * (1.0 / features)
            total = jnp.zeros((rows, 128), F32)
            for k in range(chunks):
                center = chunk(k) - mean
                total = total + fold(center * center)
            inverse = lax.rsqrt(jnp.sum(total, axis=-1, keepdims=True) * (1.0 / features) + 1e-06)
            for k in range(chunks):
                s = slice(wide * k, wide * (k + 1))
                normed[:, s] = (
                    (chunk(k) - mean) * inverse * (1.0 + mod_v[gain : gain + 1, s]) + mod_v[shift : shift + 1, s]
                ).astype(BF16)

        get_mod.wait()
        layer_norm(token_chunk, 0, 1)

        get_wq.wait()
        depth = features // 4
        qacc[...] = jnp.zeros_like(qacc)

        def project(k, carry):
            s = pl.ds(pl.multiple_of(k * depth, depth), depth)
            x = normed[:, s]
            if cols % 16 == 0:
                qacc[...] += lax.dot_general(
                    x, wq_v[:, :, s].reshape(3 * cols, depth), NT, preferred_element_type=F32
                )
            else:
                for i in range(3):
                    qacc[:, cols * i : cols * (i + 1)] += lax.dot_general(
                        x, wq_v[i, :, s], NT, preferred_element_type=F32
                    )
            return carry

        lax.fori_loop(0, 4, project, 0)
        c_across(nothing)
        rounded = qacc[...].astype(BF16)
        qk[place] = rounded

        def peer(i):
            return remote_copy(
                qk.at[place], qk.at[place], qsend.at[i], qrecv.at[place], base + xor(place, i, gs)
            )

        loop(1, gs, lambda i: peer(gs - i).start())
        exact = rounded.astype(F32)
        square = exact * exact
        lane = lax.broadcasted_iota(jnp.int32, (rows, 128), 1)
        sums = jnp.where(
            lane == 0,
            jnp.sum(square[:, :cols], axis=-1, keepdims=True),
            jnp.sum(square[:, cols : 2 * cols], axis=-1, keepdims=True),
        )
        if tall > rows:
            sums = jnp.concatenate([sums, jnp.zeros((tall - rows, 128), F32)], axis=0)
        sums = sums.T
        sq[me] = sums[:2, :rows]

        def spread(i):
            return remote_copy(sq.at[me], sq.at[me], ssend.at[i], srecv.at[me], lax.rem(me + i, n))

        loop(1, n, lambda i: spread(i).start())

        def squares_in(i):
            row = lax.rem(me + i, n)
            remote_copy(sq.at[row], sq.at[row], ssend.at[i], srecv.at[row], me).wait_recv()

        loop(1, n, squares_in)
        both = lax.rsqrt(jnp.sum(sq[...], axis=0) * (1.0 / width) + 1e-06)
        if tall > rows:
            both = jnp.concatenate([both, jnp.zeros((2, tall - rows), F32)], axis=1)
        inverse = jnp.concatenate([both, jnp.zeros((6, tall), F32)], axis=0).T[:rows]

        def peer_in(i):
            row = xor(place, i, gs)
            remote_copy(qk.at[row], qk.at[row], qsend.at[i], qrecv.at[row], me).wait_recv()

        loop(1, gs, peer_in)
        get_gains.wait()

        def whole(i):
            return jnp.concatenate([qk[p, :, cols * i : cols * (i + 1)].astype(F32) for p in range(gs)], axis=1)

        q32[...] = whole(0) * inverse[:, 0:1] * gains_v[0:1, lanes(block)]
        keys = (whole(1) * inverse[:, 1:2] * gains_v[1:2, lanes(block)]).astype(BF16)
        values = whole(2).astype(BF16)
        queries = q32[pl.ds(pl.multiple_of(part * part_rows, 8), part_rows), :].astype(BF16)

        c_finish(nothing)
        spot = lax.rem(lax.broadcasted_iota(jnp.int32, (part_rows, n * SLOT), 1), SLOT)
        columns = [slice(HEAD_DIM * h, HEAD_DIM * (h + 1)) for h in range(heads)]
        cached = [kv[:, :, s].reshape(n * SLOT, HEAD_DIM) for s in columns]
        scores = []
        for h, s in enumerate(columns):
            old = lax.dot_general(queries[:, s], cached[h], NT, preferred_element_type=F32) * scale
            new = lax.dot_general(queries[:, s], keys[:, s], NT, preferred_element_type=F32) * scale
            scores.append((jnp.where(spot < held, old, -jnp.inf), new))
        weights = []
        for old, new in scores:
            peak = jnp.maximum(jnp.max(old, axis=-1, keepdims=True), jnp.max(new, axis=-1, keepdims=True))
            old, new = jnp.exp(old - peak), jnp.exp(new - peak)
            total = jnp.sum(old, axis=-1, keepdims=True) + jnp.sum(new, axis=-1, keepdims=True)
            weights.append((pltpu.roll(old, SLOT // 2, axis=1).astype(BF16), new.astype(BF16), total))
        outs = []
        for h, s in enumerate(columns):
            old, new, total = weights[h]
            summed = lax.dot_general(old, cached[h], NN, preferred_element_type=F32) + lax.dot_general(
                new, values[:, s], NN, preferred_element_type=F32
            )
            outs.append((summed / total).astype(BF16))
        att[a, c] = jnp.concatenate(outs, axis=1)

        def att_far(i):
            return remote_copy(
                att.at[a, c], att.at[a, c], asend.at[0, i], arecv.at[a, c], dev(xor(a, i, far), b, c)
            )

        def att_core(i):
            a2 = xor(a, i, far)
            return remote_copy(
                att.at[a2, c], att.at[a2, c], asend.at[1, i], arecv.at[a2, c], dev(a, b, 1 - c)
            )

        def att_in(a2, c2):
            remote_copy(att.at[a2, c2], att.at[a2, c2], asend.at[0, 0], arecv.at[a2, c2], me).wait_recv()

        loop(1, far, lambda i: att_far(far - i).start())
        att_core(0).start()

        def att_pass(i):
            att_in(xor(a, i, far), c)
            att_core(i).start()

        loop(1, far, att_pass)
        loop(0, far, lambda i: att_in(xor(a, i, far), 1 - c))

        get_wo.wait()
        projected = jnp.zeros((rows, oc), F32)
        for k in range(blocks):
            x = att[span * k : span * (k + 1)].astype(F32).reshape(rows, wide).astype(BF16)
            projected = projected + lax.dot_general(
                x, wo_v[:, wide * k : wide * (k + 1)], NT, preferred_element_type=F32
            )
        gp[me] = jnp.concatenate([projected[pack * g : pack * (g + 1)] for g in range(group)], axis=1).astype(BF16)

        p_begin, p_near, p_forward, p_across, p_finish, p_drain = gather(gp, psend, precv)
        p_begin()
        p_near()
        p_forward(nothing)
        p_across(nothing)
        p_finish(nothing)

        for k in range(chunks):
            pieces = [gp[group * k + j].astype(F32) for j in range(group)]
            s = slice(wide * k, wide * (k + 1))
            full = jnp.concatenate(
                [
                    jnp.concatenate([piece[:, oc * g : oc * (g + 1)] for piece in pieces], axis=1)
                    for g in range(group)
                ],
                axis=0,
            )
            res[:, s] = token_chunk(k) + mod_v[2:3, s] * full
        layer_norm(lambda k: res[:, wide * k : wide * (k + 1)], 3, 4)

        get_wu.wait()
        deep = features // 2
        hacc[...] = lax.dot_general(normed[:, :deep], wu_v[:, :deep], NT, preferred_element_type=F32)
        hacc[...] += lax.dot_general(normed[:, deep:], wu_v[:, deep:], NT, preferred_element_type=F32)
        hid[...] = gelu(hacc[...]).astype(BF16)
        get_wd.wait()
        for k in range(chunks):
            part_sum = lax.dot_general(
                hid[...], wd_v[:, wide * k : wide * (k + 1)], NN, preferred_element_type=F32
            )
            for r in range(own_rows):
                for l in range(heads):
                    t32[l, pl.ds(own_rows * k + r, n, stride=pack), :] = part_sum[
                        n * r : n * (r + 1), HEAD_DIM * l : HEAD_DIM * (l + 1)
                    ]

        def copy1(m):
            i, j = far - 1 - m // near, near - 1 - m % near
            chip = xor(a, i, far) * near + xor(b, j, near)
            return chip, remote_copy(p16.at[chip], got1.at[chip], rsend.at[0, m], r1.at[chip], dev(a, b, 1 - c))

        def hand(m):
            chip, copy = copy1(m)
            p16[chip] = take(2 * chip + 1 - c).astype(BF16)
            copy.start()

        loop(0, far * near, hand)

        def pair(chip):
            remote_copy(got1.at[chip], got1.at[chip], rsend.at[0, 0], r1.at[chip], me).wait_recv()
            return take(2 * chip + c) + got1[chip].astype(F32)

        def copy2(m):
            i, j = far - 1 - m // (near - 1), near - 1 - m % (near - 1)
            a2, b2 = xor(a, i, far), xor(b, j, near)
            chip = a2 * near + b2
            at = a2 * near + b
            return chip, remote_copy(sum1.at[chip], got2.at[at], rsend.at[1, m], r2.at[at], dev(a, b2, c))

        def second(m):
            chip, copy = copy2(m)
            sum1[chip] = pair(chip).astype(BF16)
            copy.start()

        loop(0, far * (near - 1), second)

        def collect(i):
            a2 = xor(a, i, far)
            total = pair(a2 * near + b)
            for j in range(1, near):
                at = a2 * near + xor(b, j, near)
                remote_copy(got2.at[at], got2.at[at], rsend.at[1, 0], r2.at[at], me).wait_recv()
                total = total + got2[at].astype(F32)
            return a2, total

        def copy3(i):
            a2 = xor(a, i, far)
            return remote_copy(sum2.at[a2], got3.at[a], rsend.at[2, i], r3.at[a], dev(a2, b, c))

        def third(m):
            i = far - m
            a2, total = collect(i)
            sum2[a2] = total.astype(BF16)
            copy3(i).start()

        loop(1, far, third)
        _, total = collect(0)
        for i in range(1, far):
            a2 = xor(a, i, far)
            remote_copy(got3.at[a2], got3.at[a2], rsend.at[2, 0], r3.at[a2], me).wait_recv()
            total = total + got3[a2].astype(F32)
        pack32[...] = total
        for k in range(chunks):
            s = slice(wide * k, wide * (k + 1))
            feed = pack32[own_rows * k : own_rows * (k + 1), :]
            own = jnp.concatenate([res[pl.ds(me + n * r, 1), s] for r in range(own_rows)], axis=0)
            out[:, s] = (own + mod_v[5:6, s] * feed).astype(BF16)

        t_drain()
        c_drain()
        p_drain()
        loop(1, gs, lambda i: peer(i).wait_send())
        loop(1, n, lambda i: spread(i).wait_send())
        loop(1, far, lambda i: att_far(i).wait_send())
        loop(0, far, lambda i: att_core(i).wait_send())
        loop(0, far * near, lambda m: copy1(m)[1].wait_send())
        loop(0, far * (near - 1), lambda m: copy2(m)[1].wait_send())
        loop(1, far, lambda i: copy3(i).wait_send())

    def vmem(shape, dtype):
        return pltpu.VMEM(shape, dtype)

    dma = pltpu.SemaphoreType.DMA
    chips = far * near
    packed = (pack, wide)
    return pl.pallas_call(
        body,
        out_shape=jax.ShapeDtypeStruct(tokens.shape, BF16),
        in_specs=[pl.BlockSpec(memory_space=pl.ANY)] * 8,
        out_specs=pl.BlockSpec(memory_space=pltpu.VMEM),
        scratch_shapes=[
            vmem(tokens.shape, BF16),
            vmem(modulation.shape, F32),
            vmem(gains.shape, F32),
            vmem(cache.shape, BF16),
            vmem(wq.shape, BF16),
            vmem(wo.shape, BF16),
            vmem(wu.shape, BF16),
            vmem(wd.shape, BF16),
            vmem((heads, n * pack, HEAD_DIM), F32),
            vmem(packed, F32),
            vmem((n,) + packed, BF16),
            vmem((rows, features), BF16),
            vmem((SLOT, width), F32),
            vmem((blocks, SLOT, wide), BF16),
            vmem((n, SLOT, wide), BF16),
            vmem((rows, 3 * cols), F32),
            vmem((gs, rows, 3 * cols), BF16),
            vmem((n, 2, rows), F32),
            vmem((rows, wide), F32),
            vmem((far, 2, part_rows, wide), BF16),
            vmem((n,) + packed, BF16),
            vmem((rows, features), F32),
            vmem((rows, fl), F32),
            vmem((rows, fl), BF16),
            vmem((chips,) + packed, BF16),
            vmem((chips,) + packed, BF16),
            vmem((chips,) + packed, BF16),
            vmem((chips,) + packed, BF16),
            vmem((far,) + packed, BF16),
            vmem((far,) + packed, BF16),
            dma((8,)),
            dma((3, chips)),
            dma((n,)),
            dma((3, chips)),
            dma((n,)),
            dma((gs,)),
            dma((gs,)),
            dma((n,)),
            dma((n,)),
            dma((2, far)),
            dma((far, 2)),
            dma((3, chips)),
            dma((n,)),
            dma((3, chips)),
            dma((chips,)),
            dma((chips,)),
            dma((far,)),
        ],
        compiler_params=pltpu.CompilerParams(
            collective_id=0, has_side_effects=True, vmem_limit_bytes=60 * 1024 * 1024
        ),
        name="block",
    )(tokens, modulation, wq, gains, cache, wo, wu, wd)


def solution(mesh):
    n = mesh.shape["seq"]
    in_specs = (
        P(("groups", "seq"), None),
        P(),
        P(None, None, "seq"),
        P(),
        P(None, None, ("groups", "seq"), None),
        P(None, "seq"),
        P(None, "seq"),
        P("seq", None),
    )
    out_specs = P(("groups", "seq"), None)

    def step(tokens, modulation, w_qkv, norm_gains, cache_kv, w_out, w_up, w_down):
        return fused(
            n,
            tokens,
            modulation,
            jnp.swapaxes(w_qkv, 1, 2),
            norm_gains,
            jnp.swapaxes(cache_kv, 1, 2),
            w_out.T,
            w_up.T,
            w_down,
        )

    return jax.shard_map(step, mesh=mesh, in_specs=in_specs, out_specs=out_specs, check_vma=False)
```

```python
import math

import jax
import jax.numpy as jnp
from jax import lax
from jax.experimental import pallas as pl
from jax.experimental.pallas import tpu as pltpu
from jax.sharding import PartitionSpec as P

HEAD_DIM = 128
HEADS = 20
SLOT = 16
MESH = pl.DeviceIdType.MESH
NT = (((1,), (1,)), ((), ()))
NN = (((1,), (0,)), ((), ()))
F32 = jnp.float32
BF16 = jnp.bfloat16


def factors(n):
    chips = n // 2
    near = 1
    while (2 * near) * (2 * near) <= chips:
        near *= 2
    return chips // near, near


def loop(low, high, fn):
    if high - low <= 8:
        for i in range(low, high):
            fn(i)
        return

    def step(i, c):
        fn(i)
        return c

    lax.fori_loop(low, high, step, 0)


def xor(value, k, size):
    total, bit = 0, 1
    while bit < size:
        digit = lax.rem(lax.div(value, bit), 2)
        other = (k // bit) % 2
        if isinstance(other, int):
            digit = 1 - digit if other else digit
        else:
            digit = lax.rem(digit + other, 2)
        total = total + bit * digit
        bit *= 2
    return total


def remote_copy(src, dst, send, recv, device):
    return pltpu.make_async_remote_copy(
        src_ref=src, dst_ref=dst, send_sem=send, recv_sem=recv, device_id={"seq": device}, device_id_type=MESH
    )


def fold(x):
    total = x[:, :128]
    for k in range(1, x.shape[1] // 128):
        total = total + x[:, 128 * k : 128 * (k + 1)]
    return total


def gelu(x):
    return 0.5 * x * (1.0 + jnp.tanh(math.sqrt(2.0 / math.pi) * (x + 0.044715 * (x * x * x))))


def fused(n, tokens, modulation, wq, gains, cache, wo, wu, wd):
    far, near = factors(n)
    own_rows, features = tokens.shape
    rows = n * own_rows
    width = HEADS * HEAD_DIM
    cols = wq.shape[1]
    wide = math.lcm(cols, HEAD_DIM)
    gs = wide // cols
    blocks = n // gs
    heads = wide // HEAD_DIM
    frames = cache.shape[2]
    held = frames * own_rows
    span = gs // (2 * near)
    part_rows = rows // (2 * span)
    oc = wo.shape[0]
    fl = wu.shape[0]
    chunks = features // wide
    pack = own_rows * chunks
    group = wide // oc
    scale = 1.0 / math.sqrt(HEAD_DIM)
    tall = -(-rows // 128) * 128
    assert held <= SLOT // 2 and rows // group == pack and gs % (2 * near) == 0 and far % blocks == 0

    def body(
        tok, mod, wq_h, gains_h, cache_h, wo_h, wu_h, wd_h, out,
        tok_v, mod_v, gains_v, cache_v, wq_v, wo_v, wu_v, wd_v,
        t32, pack32, gt, normed, c32, cown, kv, qacc, qk, sq, st, q32, att,
        gp, res, hacc, hid, p16, got1, sum1, got2, sum2, got3,
        lsem, tsend, trecv, csend, crecv, qsend, qrecv, ssend, srecv, asend, arecv, psend, precv, usend, urecv,
        rsend, r1, r2, r3,
    ):
        me = lax.axis_index("seq")
        a, b, c = lax.div(me, 2 * near), lax.rem(lax.div(me, 2), near), lax.rem(me, 2)
        block, place = lax.div(me, gs), lax.rem(me, gs)
        base = block * gs
        part = lax.rem(a, span) * 2 + c

        def dev(a2, b2, c2):
            return (a2 * near + b2) * 2 + c2

        def fetch(k, src, dst):
            copy = pltpu.make_async_copy(src, dst, lsem.at[k])
            copy.start()
            return copy

        barrier = pltpu.get_barrier_semaphore()

        partners = [dev(xor(a, i, far), b, c) for i in range(1, far)]
        partners += [dev(a, xor(b, j, near), c) for j in range(1, near)]
        partners += [dev(xor(a, far - 1, far), xor(b, j, near), c) for j in range(1, near)]
        partners += [dev(a, b, 1 - c)]
        for partner in partners:
            pl.semaphore_signal(barrier, inc=1, device_id={"seq": partner}, device_id_type=MESH)

        get_tok = fetch(0, tok, tok_v)
        get_cache = fetch(1, cache_h, cache_v)
        get_mod = fetch(2, mod, mod_v)
        get_gains = fetch(3, gains_h, gains_v)
        get_wq = fetch(4, wq_h, wq_v)
        get_wo = fetch(5, wo_h, wo_v)
        get_wu = fetch(6, wu_h, wu_v)
        get_wd = fetch(7, wd_h, wd_v)

        def at_pack(d):
            return pl.ds(pl.multiple_of(d * pack, 8), pack)

        def put(d, x):
            for l in range(heads):
                t32[l, at_pack(d), :] = x[:, HEAD_DIM * l : HEAD_DIM * (l + 1)]

        def take(d):
            return jnp.concatenate([t32[l, at_pack(d), :] for l in range(heads)], axis=1)

        def lanes(k):
            return pl.ds(pl.multiple_of(k * wide, wide), wide)

        get_tok.wait()
        for k in range(chunks):
            pack32[own_rows * k : own_rows * (k + 1), :] = tok_v[:, wide * k : wide * (k + 1)].astype(F32)
        put(me, pack32[...])
        gt[me] = pack32[...].astype(BF16)
        get_cache.wait()
        c32[...] = jnp.zeros_like(c32)
        for side in range(2):
            for r in range(own_rows):
                at = SLOT // 2 * side + frames * r
                c32[at : at + frames, :] = cache_v[side, r].astype(F32)
        for k in range(blocks):
            cown[k] = c32[:, wide * k : wide * (k + 1)].astype(BF16)
        kv[me] = c32[:, lanes(block)].astype(BF16)

        pl.semaphore_wait(barrier, len(partners))

        def gather(dst, send, recv, own_part=None):
            def far_copy(i):
                a2 = xor(a, i, far)
                src = dst.at[me] if own_part is None else own_part.at[lax.div(a2 * 2 * near, gs)]
                return remote_copy(src, dst.at[me], send.at[0, i], recv.at[me], dev(a2, b, c))

            def across_copy(j):
                b2 = xor(b, j, near)
                a2 = xor(a, far - 1, far)
                src = dst.at[me] if own_part is None else own_part.at[lax.div(a2 * 2 * near, gs)]
                at = (far - 1) * near + j
                return remote_copy(src, dst.at[me], send.at[1, at], recv.at[me], dev(a2, b2, c))

            def near_copy(i, j):
                row = dev(xor(a, i, far), b, c)
                return remote_copy(
                    dst.at[row], dst.at[row], send.at[1, i * near + j], recv.at[row], dev(a, xor(b, j, near), c)
                )

            def core_copy(i, j):
                row = dev(xor(a, i, far), xor(b, j, near), c)
                return remote_copy(dst.at[row], dst.at[row], send.at[2, i * near + j], recv.at[row], dev(a, b, 1 - c))

            def arrived(row):
                remote_copy(dst.at[row], dst.at[row], send.at[0, 0], recv.at[row], me).wait_recv()

            def begin():
                loop(1, far, lambda i: far_copy(far - 1 - i if i < far - 1 else i).start())
                loop(1, near, lambda j: across_copy(j).start())

            def begin_near():
                loop(1, near, lambda j: near_copy(0, j).start())
                core_copy(0, 0).start()

            def forward(use, low=1, high=far):
                def one(i):
                    row = dev(xor(a, i, far), b, c)
                    arrived(row)
                    if not isinstance(i, int) or i < far - 1:
                        loop(1, near, lambda j: near_copy(i, j).start())
                    core_copy(i, 0).start()
                    use(row)

                loop(low, high, one)

            def across(use, low=0, high=far * (near - 1)):
                def one(m):
                    i, j = m % far, 1 + m // far
                    row = dev(xor(a, i, far), xor(b, j, near), c)
                    arrived(row)
                    core_copy(i, j).start()
                    use(row)

                loop(low, high, one)

            def finish(use):
                def one(m):
                    row = dev(xor(a, m % far, far), xor(b, m // far, near), 1 - c)
                    arrived(row)
                    use(row)

                loop(0, far * near, one)

            def drain():
                loop(1, far, lambda i: far_copy(i).wait_send())
                loop(0, (far - 1) * (near - 1), lambda m: near_copy(m % (far - 1), 1 + m // (far - 1)).wait_send())
                loop(1, near, lambda j: across_copy(j).wait_send())
                loop(0, far * near, lambda m: core_copy(m % far, m // far).wait_send())

            return begin, begin_near, forward, across, finish, drain

        nothing = lambda row: None
        t_begin, t_near, t_forward, t_across, t_finish, t_drain = gather(gt, tsend, trecv)
        c_begin, c_near, c_forward, c_across, c_finish, c_drain = gather(kv, csend, crecv, cown)

        def ingest(row):
            put(row, gt[row].astype(F32))

        t_begin()
        t_near()
        c_begin()
        t_forward(ingest)
        t_across(ingest)
        c_near()
        c_forward(nothing)
        t_finish(ingest)

        def token_chunk(k):
            return jnp.concatenate(
                [
                    jnp.concatenate(
                        [t32[l, pl.ds(own_rows * k + r, n, stride=pack), :] for r in range(own_rows)], axis=0
                    )
                    for l in range(heads)
                ],
                axis=1,
            )

        def to_lines(first, second):
            x = jnp.where(lax.broadcasted_iota(jnp.int32, (rows, 128), 1) == 0, first, second)
            if tall > rows:
                x = jnp.concatenate([x, jnp.zeros((tall - rows, 128), F32)], axis=0)
            return x.T[:2, :rows]

        def to_columns(x):
            if tall > rows:
                x = jnp.concatenate([x, jnp.zeros((2, tall - rows), F32)], axis=1)
            return jnp.concatenate([x, jnp.zeros((6, tall), F32)], axis=0).T[:rows]

        def layer_norm(chunk, shift, gain):
            total = jnp.zeros((rows, 128), F32)
            for k in range(chunks):
                total = total + fold(chunk(k))
            mean = jnp.sum(total, axis=-1, keepdims=True) * (1.0 / features)
            total = jnp.zeros((rows, 128), F32)
            for k in range(chunks):
                center = chunk(k) - mean
                total = total + fold(center * center)
            inverse = lax.rsqrt(jnp.sum(total, axis=-1, keepdims=True) * (1.0 / features) + 1e-06)
            for k in range(chunks):
                s = slice(wide * k, wide * (k + 1))
                normed[:, s] = (
                    (chunk(k) - mean) * inverse * (1.0 + mod_v[gain : gain + 1, s]) + mod_v[shift : shift + 1, s]
                ).astype(BF16)

        get_mod.wait()
        layer_norm(token_chunk, 0, 1)

        get_wq.wait()
        depth = features // 4
        qacc[...] = jnp.zeros_like(qacc)

        def project(k, carry):
            s = pl.ds(pl.multiple_of(k * depth, depth), depth)
            x = normed[:, s]
            if cols % 16 == 0:
                qacc[...] += lax.dot_general(
                    x, wq_v[:, :, s].reshape(3 * cols, depth), NT, preferred_element_type=F32
                )
            else:
                for i in range(3):
                    qacc[:, cols * i : cols * (i + 1)] += lax.dot_general(
                        x, wq_v[i, :, s], NT, preferred_element_type=F32
                    )
            return carry

        lax.fori_loop(0, 4, project, 0)
        c_across(nothing)
        rounded = qacc[...].astype(BF16)
        qk[place] = rounded

        def peer(i):
            return remote_copy(
                qk.at[place], qk.at[place], qsend.at[i], qrecv.at[place], base + xor(place, i, gs)
            )

        loop(1, gs, lambda i: peer(gs - i).start())
        exact = rounded.astype(F32)
        square = exact * exact
        sq[me] = to_lines(
            jnp.sum(square[:, :cols], axis=-1, keepdims=True), jnp.sum(square[:, cols : 2 * cols], axis=-1, keepdims=True)
        )

        def spread(i):
            return remote_copy(sq.at[me], sq.at[me], ssend.at[i], srecv.at[me], lax.rem(me + i, n))

        loop(1, n, lambda i: spread(i).start())

        def squares_in(i):
            row = lax.rem(me + i, n)
            remote_copy(sq.at[row], sq.at[row], ssend.at[i], srecv.at[row], me).wait_recv()

        loop(1, n, squares_in)
        both = lax.rsqrt(jnp.sum(sq[...], axis=0) * (1.0 / width) + 1e-06)
        inverse = to_columns(both)

        def peer_in(i):
            row = xor(place, i, gs)
            remote_copy(qk.at[row], qk.at[row], qsend.at[i], qrecv.at[row], me).wait_recv()

        loop(1, gs, peer_in)
        get_gains.wait()

        def whole(i):
            return jnp.concatenate([qk[p, :, cols * i : cols * (i + 1)].astype(F32) for p in range(gs)], axis=1)

        q32[...] = whole(0) * inverse[:, 0:1] * gains_v[0:1, lanes(block)]
        keys = (whole(1) * inverse[:, 1:2] * gains_v[1:2, lanes(block)]).astype(BF16)
        values = whole(2).astype(BF16)
        queries = q32[pl.ds(pl.multiple_of(part * part_rows, 8), part_rows), :].astype(BF16)

        c_finish(nothing)
        spot = lax.rem(lax.broadcasted_iota(jnp.int32, (part_rows, n * SLOT), 1), SLOT)
        columns = [slice(HEAD_DIM * h, HEAD_DIM * (h + 1)) for h in range(heads)]
        cached = [kv[:, :, s].reshape(n * SLOT, HEAD_DIM) for s in columns]
        scores = []
        for h, s in enumerate(columns):
            old = lax.dot_general(queries[:, s], cached[h], NT, preferred_element_type=F32) * scale
            new = lax.dot_general(queries[:, s], keys[:, s], NT, preferred_element_type=F32) * scale
            scores.append((jnp.where(spot < held, old, -jnp.inf), new))
        weights = []
        for old, new in scores:
            peak = jnp.maximum(jnp.max(old, axis=-1, keepdims=True), jnp.max(new, axis=-1, keepdims=True))
            old, new = jnp.exp(old - peak), jnp.exp(new - peak)
            total = jnp.sum(old, axis=-1, keepdims=True) + jnp.sum(new, axis=-1, keepdims=True)
            weights.append((pltpu.roll(old, SLOT // 2, axis=1).astype(BF16), new.astype(BF16), total))
        outs = []
        for h, s in enumerate(columns):
            old, new, total = weights[h]
            summed = lax.dot_general(old, cached[h], NN, preferred_element_type=F32) + lax.dot_general(
                new, values[:, s], NN, preferred_element_type=F32
            )
            outs.append((summed / total).astype(BF16))
        att[a, c] = jnp.concatenate(outs, axis=1)

        def att_far(i):
            return remote_copy(
                att.at[a, c], att.at[a, c], asend.at[0, i], arecv.at[a, c], dev(xor(a, i, far), b, c)
            )

        def att_core(i):
            a2 = xor(a, i, far)
            return remote_copy(
                att.at[a2, c], att.at[a2, c], asend.at[1, i], arecv.at[a2, c], dev(a, b, 1 - c)
            )

        def att_in(a2, c2):
            remote_copy(att.at[a2, c2], att.at[a2, c2], asend.at[0, 0], arecv.at[a2, c2], me).wait_recv()

        loop(1, far, lambda i: att_far(far - i).start())
        att_core(0).start()

        mine = lax.div(me, group)
        turn = lax.rem(wide - lax.rem(me, group) * oc, wide)

        def own_columns(x):
            return pltpu.roll(x, turn, axis=1)[:, :oc]

        own_tokens = own_columns(token_chunk(mine))
        own_gate = own_columns(jnp.broadcast_to(mod_v[2:3, lanes(mine)], (8, wide)))[0:1]

        def att_pass(i):
            att_in(xor(a, i, far), c)
            att_core(i).start()

        def head_block(first, s):
            x = att[pl.ds(first, span)].astype(F32).reshape(rows, wide).astype(BF16)
            return lax.dot_general(x, wo_v[:, s], NT, preferred_element_type=F32)

        get_wo.wait()
        projected = jnp.zeros((rows, oc), F32)
        if span == 1 and far <= 8:
            for i in range(far):
                if i + 1 < far:
                    att_pass(i + 1)
                a2 = xor(a, i, far)
                att_in(a2, 1 - c)
                projected = projected + head_block(a2, lanes(a2))
        else:
            loop(1, far, att_pass)
            loop(0, far, lambda i: att_in(xor(a, i, far), 1 - c))
            for k in range(blocks):
                projected = projected + head_block(span * k, slice(wide * k, wide * (k + 1)))
        projected = projected.astype(BF16).astype(F32)
        gp[me] = jnp.concatenate([projected[pack * g : pack * (g + 1)] for g in range(group)], axis=1).astype(BF16)

        p_begin, p_near, p_forward, p_across, p_finish, p_drain = gather(gp, psend, precv)

        partly = own_tokens + own_gate * projected
        mean = jnp.sum(partly, axis=-1, keepdims=True) * (1.0 / oc)
        partly = partly - mean
        square = jnp.sum(partly * partly, axis=-1, keepdims=True)
        st[me] = to_lines(mean, square)

        def tell(i):
            return remote_copy(st.at[me], st.at[me], usend.at[i], urecv.at[me], lax.rem(me + i, n))

        loop(1, n, lambda i: tell(i).start())

        p_begin()
        p_near()

        def told(i):
            row = lax.rem(me + i, n)
            remote_copy(st.at[row], st.at[row], usend.at[i], urecv.at[row], me).wait_recv()

        def statistics():
            loop(1, n, told)
            means, squares = st[:, 0], st[:, 1]
            middle = jnp.sum(means, axis=0, keepdims=True) * (1.0 / n)
            apart = means - middle
            spread_ = jnp.sum(squares + oc * (apart * apart), axis=0, keepdims=True) * (1.0 / features)
            both = to_columns(jnp.concatenate([middle, lax.rsqrt(spread_ + 1e-06)], axis=0))
            return both[:, 0:1], both[:, 1:2]

        def residual_chunk(k):
            pieces = [gp[group * k + j].astype(F32) for j in range(group)]
            full = jnp.concatenate(
                [
                    jnp.concatenate([piece[:, oc * g : oc * (g + 1)] for piece in pieces], axis=1)
                    for g in range(group)
                ],
                axis=0,
            )
            return token_chunk(k) + mod_v[2:3, lanes(k)] * full

        def grow(k, first, middle, inverse):
            s = lanes(k)
            x = residual_chunk(k)
            res[:, s] = x
            x = ((x - middle) * inverse * (1.0 + mod_v[4:5, s]) + mod_v[3:4, s]).astype(BF16)
            y = lax.dot_general(x, wu_v[:, s], NT, preferred_element_type=F32)
            hacc[...] = y if first else hacc[...] + y

        if group == 2 and far == 4:

            def chunk_of(i, j, first=False):
                a2, b2 = xor(a, i, far), xor(b, j, near)
                row = dev(a2, b2, 1 - c)
                remote_copy(gp.at[row], gp.at[row], psend.at[0, 0], precv.at[row], me).wait_recv()
                grow(a2 * near + b2, first, *stats)

            p_forward(nothing, 1, 3)
            p_across(nothing, 0, 1)
            p_forward(nothing, 3, 4)
            stats = statistics()
            get_wu.wait()
            chunk_of(0, 0, True)
            chunk_of(1, 0)
            chunk_of(0, 1)
            p_across(nothing, 3, 4)
            chunk_of(2, 0)
            p_across(nothing, 1, 2)
            chunk_of(3, 0)
            p_across(nothing, 2, 3)
            chunk_of(3, 1)
            chunk_of(1, 1)
            chunk_of(2, 1)
        else:
            p_forward(nothing)
            p_across(nothing)
            p_finish(nothing)
            stats = statistics()
            get_wu.wait()
            hacc[...] = jnp.zeros_like(hacc)
            lax.fori_loop(0, chunks, lambda k, carry: (grow(k, False, *stats), carry)[1], 0)

        hid[...] = gelu(hacc[...]).astype(BF16)
        get_wd.wait()
        for k in range(chunks):
            part_sum = lax.dot_general(
                hid[...], wd_v[:, wide * k : wide * (k + 1)], NN, preferred_element_type=F32
            )
            for r in range(own_rows):
                for l in range(heads):
                    t32[l, pl.ds(own_rows * k + r, n, stride=pack), :] = part_sum[
                        n * r : n * (r + 1), HEAD_DIM * l : HEAD_DIM * (l + 1)
                    ]

        def copy1(m):
            i, j = far - 1 - m // near, near - 1 - m % near
            chip = xor(a, i, far) * near + xor(b, j, near)
            return chip, remote_copy(p16.at[chip], got1.at[chip], rsend.at[0, m], r1.at[chip], dev(a, b, 1 - c))

        def hand(m):
            chip, copy = copy1(m)
            p16[chip] = take(2 * chip + 1 - c).astype(BF16)
            copy.start()

        loop(0, far * near, hand)

        def pair(chip):
            remote_copy(got1.at[chip], got1.at[chip], rsend.at[0, 0], r1.at[chip], me).wait_recv()
            return take(2 * chip + c) + got1[chip].astype(F32)

        def copy2(m):
            i, j = far - 1 - m // (near - 1), near - 1 - m % (near - 1)
            a2, b2 = xor(a, i, far), xor(b, j, near)
            chip = a2 * near + b2
            at = a2 * near + b
            return chip, remote_copy(sum1.at[chip], got2.at[at], rsend.at[1, m], r2.at[at], dev(a, b2, c))

        def second(m):
            chip, copy = copy2(m)
            sum1[chip] = pair(chip).astype(BF16)
            copy.start()

        loop(0, far * (near - 1), second)

        def collect(i):
            a2 = xor(a, i, far)
            total = pair(a2 * near + b)
            for j in range(1, near):
                at = a2 * near + xor(b, j, near)
                remote_copy(got2.at[at], got2.at[at], rsend.at[1, 0], r2.at[at], me).wait_recv()
                total = total + got2[at].astype(F32)
            return a2, total

        def copy3(i):
            a2 = xor(a, i, far)
            return remote_copy(sum2.at[a2], got3.at[a], rsend.at[2, i], r3.at[a], dev(a2, b, c))

        def third(m):
            i = far - m
            a2, total = collect(i)
            sum2[a2] = total.astype(BF16)
            copy3(i).start()

        loop(1, far, third)
        _, total = collect(0)
        for i in range(1, far):
            a2 = xor(a, i, far)
            remote_copy(got3.at[a2], got3.at[a2], rsend.at[2, 0], r3.at[a2], me).wait_recv()
            total = total + got3[a2].astype(F32)
        pack32[...] = total
        for k in range(chunks):
            s = slice(wide * k, wide * (k + 1))
            feed = pack32[own_rows * k : own_rows * (k + 1), :]
            own = jnp.concatenate([res[pl.ds(me + n * r, 1), s] for r in range(own_rows)], axis=0)
            out[:, s] = (own + mod_v[5:6, s] * feed).astype(BF16)

        t_drain()
        c_drain()
        p_drain()
        loop(1, gs, lambda i: peer(i).wait_send())
        loop(1, n, lambda i: spread(i).wait_send())
        loop(1, n, lambda i: tell(i).wait_send())
        loop(1, far, lambda i: att_far(i).wait_send())
        loop(0, far, lambda i: att_core(i).wait_send())
        loop(0, far * near, lambda m: copy1(m)[1].wait_send())
        loop(0, far * (near - 1), lambda m: copy2(m)[1].wait_send())
        loop(1, far, lambda i: copy3(i).wait_send())

    def vmem(shape, dtype):
        return pltpu.VMEM(shape, dtype)

    dma = pltpu.SemaphoreType.DMA
    chips = far * near
    packed = (pack, wide)
    return pl.pallas_call(
        body,
        out_shape=jax.ShapeDtypeStruct(tokens.shape, BF16),
        in_specs=[pl.BlockSpec(memory_space=pl.ANY)] * 8,
        out_specs=pl.BlockSpec(memory_space=pltpu.VMEM),
        scratch_shapes=[
            vmem(tokens.shape, BF16),
            vmem(modulation.shape, F32),
            vmem(gains.shape, F32),
            vmem(cache.shape, BF16),
            vmem(wq.shape, BF16),
            vmem(wo.shape, BF16),
            vmem(wu.shape, BF16),
            vmem(wd.shape, BF16),
            vmem((heads, n * pack, HEAD_DIM), F32),
            vmem(packed, F32),
            vmem((n,) + packed, BF16),
            vmem((rows, features), BF16),
            vmem((SLOT, width), F32),
            vmem((blocks, SLOT, wide), BF16),
            vmem((n, SLOT, wide), BF16),
            vmem((rows, 3 * cols), F32),
            vmem((gs, rows, 3 * cols), BF16),
            vmem((n, 2, rows), F32),
            vmem((n, 2, rows), F32),
            vmem((rows, wide), F32),
            vmem((far, 2, part_rows, wide), BF16),
            vmem((n,) + packed, BF16),
            vmem((rows, features), F32),
            vmem((rows, fl), F32),
            vmem((rows, fl), BF16),
            vmem((chips,) + packed, BF16),
            vmem((chips,) + packed, BF16),
            vmem((chips,) + packed, BF16),
            vmem((chips,) + packed, BF16),
            vmem((far,) + packed, BF16),
            vmem((far,) + packed, BF16),
            dma((8,)),
            dma((3, chips)),
            dma((n,)),
            dma((3, chips)),
            dma((n,)),
            dma((gs,)),
            dma((gs,)),
            dma((n,)),
            dma((n,)),
            dma((2, far)),
            dma((far, 2)),
            dma((3, chips)),
            dma((n,)),
            dma((n,)),
            dma((n,)),
            dma((3, chips)),
            dma((chips,)),
            dma((chips,)),
            dma((far,)),
        ],
        compiler_params=pltpu.CompilerParams(
            collective_id=0, has_side_effects=True, vmem_limit_bytes=60 * 1024 * 1024
        ),
        name="block",
    )(tokens, modulation, wq, gains, cache, wo, wu, wd)


def solution(mesh):
    n = mesh.shape["seq"]
    in_specs = (
        P(("groups", "seq"), None),
        P(),
        P(None, None, "seq"),
        P(),
        P(None, None, ("groups", "seq"), None),
        P(None, "seq"),
        P(None, "seq"),
        P("seq", None),
    )
    out_specs = P(("groups", "seq"), None)

    def step(tokens, modulation, w_qkv, norm_gains, cache_kv, w_out, w_up, w_down):
        return fused(
            n,
            tokens,
            modulation,
            jnp.swapaxes(w_qkv, 1, 2),
            norm_gains,
            jnp.swapaxes(cache_kv, 1, 2),
            w_out.T,
            w_up.T,
            w_down,
        )

    return jax.shard_map(step, mesh=mesh, in_specs=in_specs, out_specs=out_specs, check_vma=False)
```

```python
import math

import jax
import jax.numpy as jnp
from jax import lax
from jax.experimental import pallas as pl
from jax.experimental.pallas import tpu as pltpu
from jax.sharding import PartitionSpec as P

HEAD_DIM = 128
HEADS = 20
SLOT = 16
MESH = pl.DeviceIdType.MESH
NT = (((1,), (1,)), ((), ()))
NN = (((1,), (0,)), ((), ()))
F32 = jnp.float32
BF16 = jnp.bfloat16


def factors(n):
    chips = n // 2
    near = 1
    while (2 * near) * (2 * near) <= chips:
        near *= 2
    return chips // near, near


def loop(low, high, fn):
    if high - low <= 8:
        for i in range(low, high):
            fn(i)
        return

    def step(i, c):
        fn(i)
        return c

    lax.fori_loop(low, high, step, 0)


def xor(value, k, size):
    total, bit = 0, 1
    while bit < size:
        digit = lax.rem(lax.div(value, bit), 2)
        other = (k // bit) % 2
        if isinstance(other, int):
            digit = 1 - digit if other else digit
        else:
            digit = lax.rem(digit + other, 2)
        total = total + bit * digit
        bit *= 2
    return total


def remote_copy(src, dst, send, recv, device):
    return pltpu.make_async_remote_copy(
        src_ref=src, dst_ref=dst, send_sem=send, recv_sem=recv, device_id={"seq": device}, device_id_type=MESH
    )


def fold(x):
    total = x[:, :128]
    for k in range(1, x.shape[1] // 128):
        total = total + x[:, 128 * k : 128 * (k + 1)]
    return total


def gelu(x):
    return 0.5 * x * (1.0 + jnp.tanh(math.sqrt(2.0 / math.pi) * (x + 0.044715 * (x * x * x))))


def fused(n, tokens, modulation, wq, gains, cache, wo, wu, wd):
    far, near = factors(n)
    own_rows, features = tokens.shape
    rows = n * own_rows
    width = HEADS * HEAD_DIM
    cols = wq.shape[1]
    wide = math.lcm(cols, HEAD_DIM)
    gs = wide // cols
    blocks = n // gs
    heads = wide // HEAD_DIM
    frames = cache.shape[2]
    held = frames * own_rows
    span = gs // (2 * near)
    part_rows = rows // (2 * span)
    oc = wo.shape[0]
    fl = wu.shape[0]
    chunks = features // wide
    splits = [(0, heads // 2), (heads // 2, heads)]
    pack = own_rows * chunks
    group = wide // oc
    scale = 1.0 / math.sqrt(HEAD_DIM)
    tall = -(-rows // 128) * 128
    assert held <= SLOT // 2 and rows // group == pack and gs % (2 * near) == 0 and far % blocks == 0

    def body(
        tok, mod, wq_h, gains_h, cache_h, wo_h, wu_h, wd_h, out,
        tok_v, mod_v, gains_v, cache_v, wq_v, wo_v, wu_v, wd_v,
        t32, pack32, gt, normed, c32, cown, kv, qacc, qk, sq, st, q32, att,
        gp, res, hacc, hid,
        lsem, tsend, trecv, csend, crecv, qsend, qrecv, ssend, srecv, asend, arecv, psend, precv, usend, urecv,
        rsend, r1, r2, r3, *reduces,
    ):
        me = lax.axis_index("seq")
        a, b, c = lax.div(me, 2 * near), lax.rem(lax.div(me, 2), near), lax.rem(me, 2)
        block, place = lax.div(me, gs), lax.rem(me, gs)
        base = block * gs
        part = lax.rem(a, span) * 2 + c

        def dev(a2, b2, c2):
            return (a2 * near + b2) * 2 + c2

        def fetch(k, src, dst):
            copy = pltpu.make_async_copy(src, dst, lsem.at[k])
            copy.start()
            return copy

        barrier = pltpu.get_barrier_semaphore()

        partners = [dev(xor(a, i, far), b, c) for i in range(1, far)]
        partners += [dev(a, xor(b, j, near), c) for j in range(1, near)]
        partners += [dev(xor(a, far - 1, far), xor(b, j, near), c) for j in range(1, near)]
        partners += [dev(a, b, 1 - c)]
        for partner in partners:
            pl.semaphore_signal(barrier, inc=1, device_id={"seq": partner}, device_id_type=MESH)

        get_tok = fetch(0, tok, tok_v)
        get_cache = fetch(1, cache_h, cache_v)
        get_mod = fetch(2, mod, mod_v)
        get_gains = fetch(3, gains_h, gains_v)
        get_wq = fetch(4, wq_h, wq_v)
        get_wo = fetch(5, wo_h, wo_v)
        get_wu = fetch(6, wu_h, wu_v)
        get_wd = fetch(7, wd_h, wd_v)

        def at_pack(d):
            return pl.ds(pl.multiple_of(d * pack, 8), pack)

        def put(d, x):
            for l in range(heads):
                t32[l, at_pack(d), :] = x[:, HEAD_DIM * l : HEAD_DIM * (l + 1)]

        def take(d):
            return jnp.concatenate([t32[l, at_pack(d), :] for l in range(heads)], axis=1)

        def lanes(k):
            return pl.ds(pl.multiple_of(k * wide, wide), wide)

        get_tok.wait()
        for k in range(chunks):
            pack32[own_rows * k : own_rows * (k + 1), :] = tok_v[:, wide * k : wide * (k + 1)].astype(F32)
        put(me, pack32[...])
        gt[me] = pack32[...].astype(BF16)
        get_cache.wait()
        c32[...] = jnp.zeros_like(c32)
        for side in range(2):
            for r in range(own_rows):
                at = SLOT // 2 * side + frames * r
                c32[at : at + frames, :] = cache_v[side, r].astype(F32)
        for k in range(blocks):
            cown[k] = c32[:, wide * k : wide * (k + 1)].astype(BF16)
        kv[me] = c32[:, lanes(block)].astype(BF16)

        pl.semaphore_wait(barrier, len(partners))

        def gather(dst, send, recv, own_part=None):
            def far_copy(i):
                a2 = xor(a, i, far)
                src = dst.at[me] if own_part is None else own_part.at[lax.div(a2 * 2 * near, gs)]
                return remote_copy(src, dst.at[me], send.at[0, i], recv.at[me], dev(a2, b, c))

            def across_copy(j):
                b2 = xor(b, j, near)
                a2 = xor(a, far - 1, far)
                src = dst.at[me] if own_part is None else own_part.at[lax.div(a2 * 2 * near, gs)]
                at = (far - 1) * near + j
                return remote_copy(src, dst.at[me], send.at[1, at], recv.at[me], dev(a2, b2, c))

            def near_copy(i, j):
                row = dev(xor(a, i, far), b, c)
                return remote_copy(
                    dst.at[row], dst.at[row], send.at[1, i * near + j], recv.at[row], dev(a, xor(b, j, near), c)
                )

            def core_copy(i, j):
                row = dev(xor(a, i, far), xor(b, j, near), c)
                return remote_copy(dst.at[row], dst.at[row], send.at[2, i * near + j], recv.at[row], dev(a, b, 1 - c))

            def arrived(row):
                remote_copy(dst.at[row], dst.at[row], send.at[0, 0], recv.at[row], me).wait_recv()

            def begin():
                loop(1, far, lambda i: far_copy(far - 1 - i if i < far - 1 else i).start())
                loop(1, near, lambda j: across_copy(j).start())

            def begin_near():
                loop(1, near, lambda j: near_copy(0, j).start())
                core_copy(0, 0).start()

            def forward(use, low=1, high=far):
                def one(i):
                    row = dev(xor(a, i, far), b, c)
                    arrived(row)
                    if not isinstance(i, int) or i < far - 1:
                        loop(1, near, lambda j: near_copy(i, j).start())
                    core_copy(i, 0).start()
                    use(row)

                loop(low, high, one)

            def across(use, low=0, high=far * (near - 1)):
                def one(m):
                    i, j = m % far, 1 + m // far
                    row = dev(xor(a, i, far), xor(b, j, near), c)
                    arrived(row)
                    core_copy(i, j).start()
                    use(row)

                loop(low, high, one)

            def finish(use):
                def one(m):
                    row = dev(xor(a, m % far, far), xor(b, m // far, near), 1 - c)
                    arrived(row)
                    use(row)

                loop(0, far * near, one)

            def drain():
                loop(1, far, lambda i: far_copy(i).wait_send())
                loop(0, (far - 1) * (near - 1), lambda m: near_copy(m % (far - 1), 1 + m // (far - 1)).wait_send())
                loop(1, near, lambda j: across_copy(j).wait_send())
                loop(0, far * near, lambda m: core_copy(m % far, m // far).wait_send())

            return begin, begin_near, forward, across, finish, drain

        nothing = lambda row: None
        t_begin, t_near, t_forward, t_across, t_finish, t_drain = gather(gt, tsend, trecv)
        c_begin, c_near, c_forward, c_across, c_finish, c_drain = gather(kv, csend, crecv, cown)

        def ingest(row):
            put(row, gt[row].astype(F32))

        t_begin()
        t_near()
        c_begin()
        t_forward(ingest)
        t_across(ingest)
        c_near()
        c_forward(nothing)
        t_finish(ingest)

        def token_chunk(k):
            return jnp.concatenate(
                [
                    jnp.concatenate(
                        [t32[l, pl.ds(own_rows * k + r, n, stride=pack), :] for r in range(own_rows)], axis=0
                    )
                    for l in range(heads)
                ],
                axis=1,
            )

        def to_lines(first, second):
            x = jnp.where(lax.broadcasted_iota(jnp.int32, (rows, 128), 1) == 0, first, second)
            if tall > rows:
                x = jnp.concatenate([x, jnp.zeros((tall - rows, 128), F32)], axis=0)
            return x.T[:2, :rows]

        def to_columns(x):
            if tall > rows:
                x = jnp.concatenate([x, jnp.zeros((2, tall - rows), F32)], axis=1)
            return jnp.concatenate([x, jnp.zeros((6, tall), F32)], axis=0).T[:rows]

        def layer_norm(chunk, shift, gain):
            total = jnp.zeros((rows, 128), F32)
            for k in range(chunks):
                total = total + fold(chunk(k))
            mean = jnp.sum(total, axis=-1, keepdims=True) * (1.0 / features)
            total = jnp.zeros((rows, 128), F32)
            for k in range(chunks):
                center = chunk(k) - mean
                total = total + fold(center * center)
            inverse = lax.rsqrt(jnp.sum(total, axis=-1, keepdims=True) * (1.0 / features) + 1e-06)
            for k in range(chunks):
                s = slice(wide * k, wide * (k + 1))
                normed[:, s] = (
                    (chunk(k) - mean) * inverse * (1.0 + mod_v[gain : gain + 1, s]) + mod_v[shift : shift + 1, s]
                ).astype(BF16)

        get_mod.wait()
        layer_norm(token_chunk, 0, 1)

        get_wq.wait()
        depth = features // 4
        qacc[...] = jnp.zeros_like(qacc)

        def project(k, carry):
            s = pl.ds(pl.multiple_of(k * depth, depth), depth)
            x = normed[:, s]
            if cols % 16 == 0:
                qacc[...] += lax.dot_general(
                    x, wq_v[:, :, s].reshape(3 * cols, depth), NT, preferred_element_type=F32
                )
            else:
                for i in range(3):
                    qacc[:, cols * i : cols * (i + 1)] += lax.dot_general(
                        x, wq_v[i, :, s], NT, preferred_element_type=F32
                    )
            return carry

        lax.fori_loop(0, 4, project, 0)
        c_across(nothing)
        rounded = qacc[...].astype(BF16)
        qk[place] = rounded

        def peer(i):
            return remote_copy(
                qk.at[place], qk.at[place], qsend.at[i], qrecv.at[place], base + xor(place, i, gs)
            )

        loop(1, gs, lambda i: peer(gs - i).start())
        exact = rounded.astype(F32)
        square = exact * exact
        sq[me] = to_lines(
            jnp.sum(square[:, :cols], axis=-1, keepdims=True), jnp.sum(square[:, cols : 2 * cols], axis=-1, keepdims=True)
        )

        def spread(i):
            return remote_copy(sq.at[me], sq.at[me], ssend.at[i], srecv.at[me], lax.rem(me + i, n))

        loop(1, n, lambda i: spread(i).start())

        def squares_in(i):
            row = lax.rem(me + i, n)
            remote_copy(sq.at[row], sq.at[row], ssend.at[i], srecv.at[row], me).wait_recv()

        loop(1, n, squares_in)
        both = lax.rsqrt(jnp.sum(sq[...], axis=0) * (1.0 / width) + 1e-06)
        inverse = to_columns(both)

        def peer_in(i):
            row = xor(place, i, gs)
            remote_copy(qk.at[row], qk.at[row], qsend.at[i], qrecv.at[row], me).wait_recv()

        loop(1, gs, peer_in)
        get_gains.wait()

        def whole(i):
            return jnp.concatenate([qk[p, :, cols * i : cols * (i + 1)].astype(F32) for p in range(gs)], axis=1)

        q32[...] = whole(0) * inverse[:, 0:1] * gains_v[0:1, lanes(block)]
        keys = (whole(1) * inverse[:, 1:2] * gains_v[1:2, lanes(block)]).astype(BF16)
        values = whole(2).astype(BF16)
        queries = q32[pl.ds(pl.multiple_of(part * part_rows, 8), part_rows), :].astype(BF16)

        c_finish(nothing)
        spot = lax.rem(lax.broadcasted_iota(jnp.int32, (part_rows, n * SLOT), 1), SLOT)
        columns = [slice(HEAD_DIM * h, HEAD_DIM * (h + 1)) for h in range(heads)]
        cached = [kv[:, :, s].reshape(n * SLOT, HEAD_DIM) for s in columns]
        scores = []
        for h, s in enumerate(columns):
            old = lax.dot_general(queries[:, s], cached[h], NT, preferred_element_type=F32) * scale
            new = lax.dot_general(queries[:, s], keys[:, s], NT, preferred_element_type=F32) * scale
            scores.append((jnp.where(spot < held, old, -jnp.inf), new))
        weights = []
        for old, new in scores:
            peak = jnp.maximum(jnp.max(old, axis=-1, keepdims=True), jnp.max(new, axis=-1, keepdims=True))
            old, new = jnp.exp(old - peak), jnp.exp(new - peak)
            total = jnp.sum(old, axis=-1, keepdims=True) + jnp.sum(new, axis=-1, keepdims=True)
            weights.append((pltpu.roll(old, SLOT // 2, axis=1).astype(BF16), new.astype(BF16), total))
        outs = []
        for h, s in enumerate(columns):
            old, new, total = weights[h]
            summed = lax.dot_general(old, cached[h], NN, preferred_element_type=F32) + lax.dot_general(
                new, values[:, s], NN, preferred_element_type=F32
            )
            outs.append((summed / total).astype(BF16))
        att[a, c] = jnp.concatenate(outs, axis=1)

        def att_far(i):
            return remote_copy(
                att.at[a, c], att.at[a, c], asend.at[0, i], arecv.at[a, c], dev(xor(a, i, far), b, c)
            )

        def att_core(i):
            a2 = xor(a, i, far)
            return remote_copy(
                att.at[a2, c], att.at[a2, c], asend.at[1, i], arecv.at[a2, c], dev(a, b, 1 - c)
            )

        def att_in(a2, c2):
            remote_copy(att.at[a2, c2], att.at[a2, c2], asend.at[0, 0], arecv.at[a2, c2], me).wait_recv()

        loop(1, far, lambda i: att_far(far - i).start())
        att_core(0).start()

        mine = lax.div(me, group)
        turn = lax.rem(wide - lax.rem(me, group) * oc, wide)

        def own_columns(x):
            return pltpu.roll(x, turn, axis=1)[:, :oc]

        own_tokens = own_columns(token_chunk(mine))
        own_gate = own_columns(jnp.broadcast_to(mod_v[2:3, lanes(mine)], (8, wide)))[0:1]

        def att_pass(i):
            att_in(xor(a, i, far), c)
            att_core(i).start()

        def head_block(first, s):
            x = att[pl.ds(first, span)].astype(F32).reshape(rows, wide).astype(BF16)
            return lax.dot_general(x, wo_v[:, s], NT, preferred_element_type=F32)

        get_wo.wait()
        projected = jnp.zeros((rows, oc), F32)
        if span == 1 and far <= 8:
            for i in range(far):
                if i + 1 < far:
                    att_pass(i + 1)
                a2 = xor(a, i, far)
                att_in(a2, 1 - c)
                projected = projected + head_block(a2, lanes(a2))
        else:
            loop(1, far, att_pass)
            loop(0, far, lambda i: att_in(xor(a, i, far), 1 - c))
            for k in range(blocks):
                projected = projected + head_block(span * k, slice(wide * k, wide * (k + 1)))
        projected = projected.astype(BF16).astype(F32)
        gp[me] = jnp.concatenate([projected[pack * g : pack * (g + 1)] for g in range(group)], axis=1).astype(BF16)

        p_begin, p_near, p_forward, p_across, p_finish, p_drain = gather(gp, psend, precv)

        partly = own_tokens + own_gate * projected
        mean = jnp.sum(partly, axis=-1, keepdims=True) * (1.0 / oc)
        partly = partly - mean
        square = jnp.sum(partly * partly, axis=-1, keepdims=True)
        st[me] = to_lines(mean, square)

        def tell(i):
            return remote_copy(st.at[me], st.at[me], usend.at[i], urecv.at[me], lax.rem(me + i, n))

        loop(1, n, lambda i: tell(i).start())

        p_begin()
        p_near()

        def told(i):
            row = lax.rem(me + i, n)
            remote_copy(st.at[row], st.at[row], usend.at[i], urecv.at[row], me).wait_recv()

        def statistics():
            loop(1, n, told)
            means, squares = st[:, 0], st[:, 1]
            middle = jnp.sum(means, axis=0, keepdims=True) * (1.0 / n)
            apart = means - middle
            spread_ = jnp.sum(squares + oc * (apart * apart), axis=0, keepdims=True) * (1.0 / features)
            both = to_columns(jnp.concatenate([middle, lax.rsqrt(spread_ + 1e-06)], axis=0))
            return both[:, 0:1], both[:, 1:2]

        def residual_chunk(k):
            pieces = [gp[group * k + j].astype(F32) for j in range(group)]
            full = jnp.concatenate(
                [
                    jnp.concatenate([piece[:, oc * g : oc * (g + 1)] for piece in pieces], axis=1)
                    for g in range(group)
                ],
                axis=0,
            )
            return token_chunk(k) + mod_v[2:3, lanes(k)] * full

        def grow(k, first, middle, inverse):
            s = lanes(k)
            x = residual_chunk(k)
            res[:, s] = x
            x = ((x - middle) * inverse * (1.0 + mod_v[4:5, s]) + mod_v[3:4, s]).astype(BF16)
            y = lax.dot_general(x, wu_v[:, s], NT, preferred_element_type=F32)
            hacc[...] = y if first else hacc[...] + y

        if group == 2 and far == 4:

            def chunk_of(i, j, first=False):
                a2, b2 = xor(a, i, far), xor(b, j, near)
                row = dev(a2, b2, 1 - c)
                remote_copy(gp.at[row], gp.at[row], psend.at[0, 0], precv.at[row], me).wait_recv()
                grow(a2 * near + b2, first, *stats)

            p_forward(nothing, 1, 3)
            p_across(nothing, 0, 1)
            p_forward(nothing, 3, 4)
            stats = statistics()
            get_wu.wait()
            chunk_of(0, 0, True)
            chunk_of(1, 0)
            chunk_of(0, 1)
            p_across(nothing, 3, 4)
            chunk_of(2, 0)
            p_across(nothing, 1, 2)
            chunk_of(3, 0)
            p_across(nothing, 2, 3)
            chunk_of(3, 1)
            chunk_of(1, 1)
            chunk_of(2, 1)
        else:
            p_forward(nothing)
            p_across(nothing)
            p_finish(nothing)
            stats = statistics()
            get_wu.wait()
            hacc[...] = jnp.zeros_like(hacc)
            lax.fori_loop(0, chunks, lambda k, carry: (grow(k, False, *stats), carry)[1], 0)

        hid[...] = gelu(hacc[...]).astype(BF16)
        get_wd.wait()

        def part_of(q):
            first, last = splits[q]
            p16, got1, sum1, got2, sum2, got3 = reduces[6 * q : 6 * q + 6]
            span_l = range(first, last)

            def own_sum(d):
                return jnp.concatenate([t32[l, at_pack(d), :] for l in span_l], axis=1)

            def down():
                for k in range(chunks):
                    s = slice(wide * k + HEAD_DIM * first, wide * k + HEAD_DIM * last)
                    y = lax.dot_general(hid[...], wd_v[:, s], NN, preferred_element_type=F32)
                    for r in range(own_rows):
                        for l in span_l:
                            at = HEAD_DIM * (l - first)
                            t32[l, pl.ds(own_rows * k + r, n, stride=pack), :] = y[
                                n * r : n * (r + 1), at : at + HEAD_DIM
                            ]

            def copy1(m):
                i, j = far - 1 - m // near, near - 1 - m % near
                chip = xor(a, i, far) * near + xor(b, j, near)
                return chip, remote_copy(
                    p16.at[chip], got1.at[chip], rsend.at[q, 0, m], r1.at[q, chip], dev(a, b, 1 - c)
                )

            def hand(m):
                chip, copy = copy1(m)
                p16[chip] = own_sum(2 * chip + 1 - c).astype(BF16)
                copy.start()

            def pair(chip):
                remote_copy(got1.at[chip], got1.at[chip], rsend.at[q, 0, 0], r1.at[q, chip], me).wait_recv()
                return own_sum(2 * chip + c) + got1[chip].astype(F32)

            def copy_straight(j):
                a2, b2 = xor(a, far - 1, far), xor(b, j, near)
                chip = a2 * near + b2
                at = a * near + b
                return chip, remote_copy(
                    sum1.at[chip], got3.at[at], rsend.at[q, 3, j], r3.at[q, at], dev(a2, b2, c)
                )

            def straight(j):
                chip, copy = copy_straight(j)
                sum1[chip] = pair(chip).astype(BF16)
                copy.start()

            def copy2(m):
                i, j = far - 2 - m // (near - 1), near - 1 - m % (near - 1)
                a2, b2 = xor(a, i, far), xor(b, j, near)
                chip = a2 * near + b2
                at = a2 * near + b
                return chip, remote_copy(sum1.at[chip], got2.at[at], rsend.at[q, 1, m], r2.at[q, at], dev(a, b2, c))

            def second(m):
                chip, copy = copy2(m)
                sum1[chip] = pair(chip).astype(BF16)
                copy.start()

            def collect(i):
                a2 = xor(a, i, far)
                total = pair(a2 * near + b)
                for j in range(1, near):
                    at = a2 * near + xor(b, j, near)
                    remote_copy(got2.at[at], got2.at[at], rsend.at[q, 1, 0], r2.at[q, at], me).wait_recv()
                    total = total + got2[at].astype(F32)
                return a2, total

            def copy3(i):
                a2 = xor(a, i, far)
                at = a * near + b
                return remote_copy(sum2.at[a2], got3.at[at], rsend.at[q, 2, i], r3.at[q, at], dev(a2, b, c))

            def third(m):
                i = far - 1 - m
                a2, total = collect(i)
                sum2[a2] = total.astype(BF16)
                copy3(i).start()

            def last_sum():
                _, total = collect(0)
                for i in range(1, far):
                    for j in range(near if i == far - 1 else 1):
                        at = xor(a, i, far) * near + xor(b, j, near)
                        remote_copy(got3.at[at], got3.at[at], rsend.at[q, 2, 0], r3.at[q, at], me).wait_recv()
                        total = total + got3[at].astype(F32)
                pack32[:, HEAD_DIM * first : HEAD_DIM * last] = total

            def drain():
                loop(0, far * near, lambda m: copy1(m)[1].wait_send())
                loop(0, near, lambda j: copy_straight(j)[1].wait_send())
                loop(0, (far - 1) * (near - 1), lambda m: copy2(m)[1].wait_send())
                loop(1, far - 1, lambda i: copy3(i).wait_send())

            stages = [
                down,
                lambda: loop(0, far * near, hand),
                lambda: (loop(0, near, straight), loop(0, (far - 1) * (near - 1), second)),
                lambda: loop(1, far - 1, third),
                last_sum,
            ]
            return stages, drain

        todo = [part_of(q) for q in range(len(splits))]
        for stages, _ in todo:
            stages[0]()
            stages[1]()
        for step in range(2, 5):
            for stages, _ in todo:
                stages[step]()
        for k in range(chunks):
            s = slice(wide * k, wide * (k + 1))
            feed = pack32[own_rows * k : own_rows * (k + 1), :]
            own = jnp.concatenate([res[pl.ds(me + n * r, 1), s] for r in range(own_rows)], axis=0)
            out[:, s] = (own + mod_v[5:6, s] * feed).astype(BF16)

        t_drain()
        c_drain()
        p_drain()
        loop(1, gs, lambda i: peer(i).wait_send())
        loop(1, n, lambda i: spread(i).wait_send())
        loop(1, n, lambda i: tell(i).wait_send())
        loop(1, far, lambda i: att_far(i).wait_send())
        loop(0, far, lambda i: att_core(i).wait_send())
        for _, drain in todo:
            drain()

    def vmem(shape, dtype):
        return pltpu.VMEM(shape, dtype)

    dma = pltpu.SemaphoreType.DMA
    chips = far * near
    packed = (pack, wide)
    return pl.pallas_call(
        body,
        out_shape=jax.ShapeDtypeStruct(tokens.shape, BF16),
        in_specs=[pl.BlockSpec(memory_space=pl.ANY)] * 8,
        out_specs=pl.BlockSpec(memory_space=pltpu.VMEM),
        scratch_shapes=[
            vmem(tokens.shape, BF16),
            vmem(modulation.shape, F32),
            vmem(gains.shape, F32),
            vmem(cache.shape, BF16),
            vmem(wq.shape, BF16),
            vmem(wo.shape, BF16),
            vmem(wu.shape, BF16),
            vmem(wd.shape, BF16),
            vmem((heads, n * pack, HEAD_DIM), F32),
            vmem(packed, F32),
            vmem((n,) + packed, BF16),
            vmem((rows, features), BF16),
            vmem((SLOT, width), F32),
            vmem((blocks, SLOT, wide), BF16),
            vmem((n, SLOT, wide), BF16),
            vmem((rows, 3 * cols), F32),
            vmem((gs, rows, 3 * cols), BF16),
            vmem((n, 2, rows), F32),
            vmem((n, 2, rows), F32),
            vmem((rows, wide), F32),
            vmem((far, 2, part_rows, wide), BF16),
            vmem((n,) + packed, BF16),
            vmem((rows, features), F32),
            vmem((rows, fl), F32),
            vmem((rows, fl), BF16),
            dma((8,)),
            dma((3, chips)),
            dma((n,)),
            dma((3, chips)),
            dma((n,)),
            dma((gs,)),
            dma((gs,)),
            dma((n,)),
            dma((n,)),
            dma((2, far)),
            dma((far, 2)),
            dma((3, chips)),
            dma((n,)),
            dma((n,)),
            dma((n,)),
            dma((len(splits), 4, chips)),
            dma((len(splits), chips)),
            dma((len(splits), chips)),
            dma((len(splits), chips)),
        ]
        + [
            vmem((lines, pack, HEAD_DIM * (last - first)), BF16)
            for first, last in splits
            for lines in (chips, chips, chips, chips, far, chips)
        ],
        compiler_params=pltpu.CompilerParams(
            collective_id=0, has_side_effects=True, vmem_limit_bytes=60 * 1024 * 1024
        ),
        name="block",
    )(tokens, modulation, wq, gains, cache, wo, wu, wd)


def solution(mesh):
    n = mesh.shape["seq"]
    in_specs = (
        P(("groups", "seq"), None),
        P(),
        P(None, None, "seq"),
        P(),
        P(None, None, ("groups", "seq"), None),
        P(None, "seq"),
        P(None, "seq"),
        P("seq", None),
    )
    out_specs = P(("groups", "seq"), None)

    def step(tokens, modulation, w_qkv, norm_gains, cache_kv, w_out, w_up, w_down):
        return fused(
            n,
            tokens,
            modulation,
            jnp.swapaxes(w_qkv, 1, 2),
            norm_gains,
            jnp.swapaxes(cache_kv, 1, 2),
            w_out.T,
            w_up.T,
            w_down,
        )

    return jax.shard_map(step, mesh=mesh, in_specs=in_specs, out_specs=out_specs, check_vma=False)
```

```python
import math

import jax
import jax.numpy as jnp
from jax import lax
from jax.experimental import pallas as pl
from jax.experimental.pallas import tpu as pltpu
from jax.sharding import PartitionSpec as P

HEAD_DIM = 128
HEADS = 20
SLOT = 16
MESH = pl.DeviceIdType.MESH
NT = (((1,), (1,)), ((), ()))
NN = (((1,), (0,)), ((), ()))
F32 = jnp.float32
BF16 = jnp.bfloat16


def factors(n):
    chips = n // 2
    near = 1
    while (2 * near) * (2 * near) <= chips:
        near *= 2
    return chips // near, near


def loop(low, high, fn):
    if high - low <= 8:
        for i in range(low, high):
            fn(i)
        return

    def step(i, c):
        fn(i)
        return c

    lax.fori_loop(low, high, step, 0)


def xor(value, k, size):
    total, bit = 0, 1
    while bit < size:
        digit = lax.rem(lax.div(value, bit), 2)
        other = (k // bit) % 2
        if isinstance(other, int):
            digit = 1 - digit if other else digit
        else:
            digit = lax.rem(digit + other, 2)
        total = total + bit * digit
        bit *= 2
    return total


def remote_copy(src, dst, send, recv, device):
    return pltpu.make_async_remote_copy(
        src_ref=src, dst_ref=dst, send_sem=send, recv_sem=recv, device_id={"seq": device}, device_id_type=MESH
    )


def fold(x):
    total = x[:, :128]
    for k in range(1, x.shape[1] // 128):
        total = total + x[:, 128 * k : 128 * (k + 1)]
    return total


def gelu(x):
    return 0.5 * x * (1.0 + jnp.tanh(math.sqrt(2.0 / math.pi) * (x + 0.044715 * (x * x * x))))


def fused(n, tokens, modulation, wq, gains, cache, wo, wu, wd):
    far, near = factors(n)
    own_rows, features = tokens.shape
    rows = n * own_rows
    width = HEADS * HEAD_DIM
    cols = wq.shape[1]
    wide = math.lcm(cols, HEAD_DIM)
    gs = wide // cols
    blocks = n // gs
    heads = wide // HEAD_DIM
    frames = cache.shape[2]
    held = frames * own_rows
    span = gs // (2 * near)
    part_rows = rows // (2 * span)
    oc = wo.shape[0]
    fl = wu.shape[0]
    chunks = features // wide
    splits = [(0, heads // 2), (heads // 2, heads)]
    pack = own_rows * chunks
    group = wide // oc
    scale = 1.0 / math.sqrt(HEAD_DIM)
    tall = -(-rows // 128) * 128
    assert held <= SLOT // 2 and rows // group == pack and gs % (2 * near) == 0 and far % blocks == 0

    def body(
        tok, mod, wq_h, gains_h, cache_h, wo_h, wu_h, wd_h, out,
        tok_v, mod_v, gains_v, cache_v, wq_v, wo_v, wu_v, wd_v,
        t32, pack32, gt, normed, c32, cown, kv, qacc, qk, sq, st, q32, att,
        gp, res, hacc, hid, own_pack, gate_pack,
        lsem, tsend, trecv, csend, crecv, qsend, qrecv, ssend, srecv, asend, arecv, psend, precv, usend, urecv,
        rsend, r1, r2, r3, *reduces,
    ):
        me = lax.axis_index("seq")
        a, b, c = lax.div(me, 2 * near), lax.rem(lax.div(me, 2), near), lax.rem(me, 2)
        block, place = lax.div(me, gs), lax.rem(me, gs)
        base = block * gs
        part = lax.rem(a, span) * 2 + c

        def dev(a2, b2, c2):
            return (a2 * near + b2) * 2 + c2

        def fetch(k, src, dst):
            copy = pltpu.make_async_copy(src, dst, lsem.at[k])
            copy.start()
            return copy

        barrier = pltpu.get_barrier_semaphore()

        partners = [dev(xor(a, i, far), b, c) for i in range(1, far)]
        partners += [dev(a, xor(b, j, near), c) for j in range(1, near)]
        partners += [dev(xor(a, far - 1, far), xor(b, j, near), c) for j in range(1, near)]
        partners += [dev(a, b, 1 - c)]
        for partner in partners:
            pl.semaphore_signal(barrier, inc=1, device_id={"seq": partner}, device_id_type=MESH)

        get_tok = fetch(0, tok, tok_v)
        get_cache = fetch(1, cache_h, cache_v)
        get_mod = fetch(2, mod, mod_v)
        get_gains = fetch(3, gains_h, gains_v)
        get_wq = fetch(4, wq_h, wq_v)
        get_wo = fetch(5, wo_h, wo_v)
        get_wu = fetch(6, wu_h, wu_v)
        get_wd = fetch(7, wd_h, wd_v)

        def at_pack(d):
            return pl.ds(pl.multiple_of(d * pack, 8), pack)

        def put(d, x):
            for l in range(heads):
                t32[l, at_pack(d), :] = x[:, HEAD_DIM * l : HEAD_DIM * (l + 1)]

        def take(d):
            return jnp.concatenate([t32[l, at_pack(d), :] for l in range(heads)], axis=1)

        def lanes(k):
            return pl.ds(pl.multiple_of(k * wide, wide), wide)

        get_tok.wait()
        for k in range(chunks):
            pack32[own_rows * k : own_rows * (k + 1), :] = tok_v[:, wide * k : wide * (k + 1)].astype(F32)
        put(me, pack32[...])
        gt[me] = pack32[...].astype(BF16)
        get_cache.wait()
        c32[...] = jnp.zeros_like(c32)
        for side in range(2):
            for r in range(own_rows):
                at = SLOT // 2 * side + frames * r
                c32[at : at + frames, :] = cache_v[side, r].astype(F32)
        for k in range(blocks):
            cown[k] = c32[:, wide * k : wide * (k + 1)].astype(BF16)
        kv[me] = c32[:, lanes(block)].astype(BF16)

        pl.semaphore_wait(barrier, len(partners))

        def gather(dst, send, recv, own_part=None):
            def far_copy(i):
                a2 = xor(a, i, far)
                src = dst.at[me] if own_part is None else own_part.at[lax.div(a2 * 2 * near, gs)]
                return remote_copy(src, dst.at[me], send.at[0, i], recv.at[me], dev(a2, b, c))

            def across_copy(j):
                b2 = xor(b, j, near)
                a2 = xor(a, far - 1, far)
                src = dst.at[me] if own_part is None else own_part.at[lax.div(a2 * 2 * near, gs)]
                at = (far - 1) * near + j
                return remote_copy(src, dst.at[me], send.at[1, at], recv.at[me], dev(a2, b2, c))

            def near_copy(i, j):
                row = dev(xor(a, i, far), b, c)
                return remote_copy(
                    dst.at[row], dst.at[row], send.at[1, i * near + j], recv.at[row], dev(a, xor(b, j, near), c)
                )

            def core_copy(i, j):
                row = dev(xor(a, i, far), xor(b, j, near), c)
                return remote_copy(dst.at[row], dst.at[row], send.at[2, i * near + j], recv.at[row], dev(a, b, 1 - c))

            def arrived(row):
                remote_copy(dst.at[row], dst.at[row], send.at[0, 0], recv.at[row], me).wait_recv()

            def begin():
                loop(1, far, lambda i: far_copy(far - 1 - i if i < far - 1 else i).start())
                loop(1, near, lambda j: across_copy(j).start())

            def begin_near():
                loop(1, near, lambda j: near_copy(0, j).start())
                core_copy(0, 0).start()

            def forward(use, low=1, high=far):
                def one(i):
                    row = dev(xor(a, i, far), b, c)
                    arrived(row)
                    if not isinstance(i, int) or i < far - 1:
                        loop(1, near, lambda j: near_copy(i, j).start())
                    core_copy(i, 0).start()
                    use(row)

                loop(low, high, one)

            def across(use, low=0, high=far * (near - 1)):
                def one(m):
                    i, j = m % far, 1 + m // far
                    row = dev(xor(a, i, far), xor(b, j, near), c)
                    arrived(row)
                    core_copy(i, j).start()
                    use(row)

                loop(low, high, one)

            def finish(use):
                def one(m):
                    row = dev(xor(a, m % far, far), xor(b, m // far, near), 1 - c)
                    arrived(row)
                    use(row)

                loop(0, far * near, one)

            def drain():
                loop(1, far, lambda i: far_copy(i).wait_send())
                loop(0, (far - 1) * (near - 1), lambda m: near_copy(m % (far - 1), 1 + m // (far - 1)).wait_send())
                loop(1, near, lambda j: across_copy(j).wait_send())
                loop(0, far * near, lambda m: core_copy(m % far, m // far).wait_send())

            return begin, begin_near, forward, across, finish, drain

        nothing = lambda row: None
        t_begin, t_near, t_forward, t_across, t_finish, t_drain = gather(gt, tsend, trecv)
        c_begin, c_near, c_forward, c_across, c_finish, c_drain = gather(kv, csend, crecv, cown)

        def ingest(row):
            put(row, gt[row].astype(F32))

        t_begin()
        t_near()
        c_begin()
        t_forward(ingest)
        t_across(ingest)
        c_near()
        c_forward(nothing)
        t_finish(ingest)

        def token_chunk(k):
            return jnp.concatenate(
                [
                    jnp.concatenate(
                        [t32[l, pl.ds(own_rows * k + r, n, stride=pack), :] for r in range(own_rows)], axis=0
                    )
                    for l in range(heads)
                ],
                axis=1,
            )

        def to_lines(first, second):
            x = jnp.where(lax.broadcasted_iota(jnp.int32, (rows, 128), 1) == 0, first, second)
            if tall > rows:
                x = jnp.concatenate([x, jnp.zeros((tall - rows, 128), F32)], axis=0)
            return x.T[:2, :rows]

        def to_columns(x):
            if tall > rows:
                x = jnp.concatenate([x, jnp.zeros((2, tall - rows), F32)], axis=1)
            return jnp.concatenate([x, jnp.zeros((6, tall), F32)], axis=0).T[:rows]

        def layer_norm(chunk, shift, gain):
            total = jnp.zeros((rows, 128), F32)
            for k in range(chunks):
                total = total + fold(chunk(k))
            mean = jnp.sum(total, axis=-1, keepdims=True) * (1.0 / features)
            total = jnp.zeros((rows, 128), F32)
            for k in range(chunks):
                center = chunk(k) - mean
                total = total + fold(center * center)
            inverse = lax.rsqrt(jnp.sum(total, axis=-1, keepdims=True) * (1.0 / features) + 1e-06)
            for k in range(chunks):
                s = slice(wide * k, wide * (k + 1))
                normed[:, s] = (
                    (chunk(k) - mean) * inverse * (1.0 + mod_v[gain : gain + 1, s]) + mod_v[shift : shift + 1, s]
                ).astype(BF16)

        get_mod.wait()
        layer_norm(token_chunk, 0, 1)

        get_wq.wait()
        depth = features // 4
        qacc[...] = jnp.zeros_like(qacc)

        def project(k, carry):
            s = pl.ds(pl.multiple_of(k * depth, depth), depth)
            x = normed[:, s]
            if cols % 16 == 0:
                qacc[...] += lax.dot_general(
                    x, wq_v[:, :, s].reshape(3 * cols, depth), NT, preferred_element_type=F32
                )
            else:
                for i in range(3):
                    qacc[:, cols * i : cols * (i + 1)] += lax.dot_general(
                        x, wq_v[i, :, s], NT, preferred_element_type=F32
                    )
            return carry

        lax.fori_loop(0, 4, project, 0)
        c_across(nothing)
        rounded = qacc[...].astype(BF16)
        qk[place] = rounded

        def peer(i):
            return remote_copy(
                qk.at[place], qk.at[place], qsend.at[i], qrecv.at[place], base + xor(place, i, gs)
            )

        loop(1, gs, lambda i: peer(gs - i).start())
        exact = rounded.astype(F32)
        square = exact * exact
        sq[me] = to_lines(
            jnp.sum(square[:, :cols], axis=-1, keepdims=True), jnp.sum(square[:, cols : 2 * cols], axis=-1, keepdims=True)
        )

        def spread(i):
            return remote_copy(sq.at[me], sq.at[me], ssend.at[i], srecv.at[me], lax.rem(me + i, n))

        loop(1, n, lambda i: spread(i).start())

        def squares_in(i):
            row = lax.rem(me + i, n)
            remote_copy(sq.at[row], sq.at[row], ssend.at[i], srecv.at[row], me).wait_recv()

        t_drain()
        loop(1, n, squares_in)
        both = lax.rsqrt(jnp.sum(sq[...], axis=0) * (1.0 / width) + 1e-06)
        inverse = to_columns(both)

        def peer_in(i):
            row = xor(place, i, gs)
            remote_copy(qk.at[row], qk.at[row], qsend.at[i], qrecv.at[row], me).wait_recv()

        loop(1, gs, peer_in)
        get_gains.wait()

        def whole(i):
            return jnp.concatenate([qk[p, :, cols * i : cols * (i + 1)].astype(F32) for p in range(gs)], axis=1)

        q32[...] = whole(0) * inverse[:, 0:1] * gains_v[0:1, lanes(block)]
        keys = (whole(1) * inverse[:, 1:2] * gains_v[1:2, lanes(block)]).astype(BF16)
        values = whole(2).astype(BF16)
        queries = q32[pl.ds(pl.multiple_of(part * part_rows, 8), part_rows), :].astype(BF16)

        c_finish(nothing)
        spot = lax.rem(lax.broadcasted_iota(jnp.int32, (part_rows, n * SLOT), 1), SLOT)
        columns = [slice(HEAD_DIM * h, HEAD_DIM * (h + 1)) for h in range(heads)]
        cached = [kv[:, :, s].reshape(n * SLOT, HEAD_DIM) for s in columns]
        scores = []
        for h, s in enumerate(columns):
            old = lax.dot_general(queries[:, s], cached[h], NT, preferred_element_type=F32) * scale
            new = lax.dot_general(queries[:, s], keys[:, s], NT, preferred_element_type=F32) * scale
            scores.append((jnp.where(spot < held, old, -jnp.inf), new))
        weights = []
        for old, new in scores:
            peak = jnp.maximum(jnp.max(old, axis=-1, keepdims=True), jnp.max(new, axis=-1, keepdims=True))
            old, new = jnp.exp(old - peak), jnp.exp(new - peak)
            total = jnp.sum(old, axis=-1, keepdims=True) + jnp.sum(new, axis=-1, keepdims=True)
            weights.append((pltpu.roll(old, SLOT // 2, axis=1).astype(BF16), new.astype(BF16), total))
        outs = []
        for h, s in enumerate(columns):
            old, new, total = weights[h]
            summed = lax.dot_general(old, cached[h], NN, preferred_element_type=F32) + lax.dot_general(
                new, values[:, s], NN, preferred_element_type=F32
            )
            outs.append((summed / total).astype(BF16))
        att[a, c] = jnp.concatenate(outs, axis=1)

        def att_far(i):
            return remote_copy(
                att.at[a, c], att.at[a, c], asend.at[0, i], arecv.at[a, c], dev(xor(a, i, far), b, c)
            )

        def att_core(i):
            a2 = xor(a, i, far)
            return remote_copy(
                att.at[a2, c], att.at[a2, c], asend.at[1, i], arecv.at[a2, c], dev(a, b, 1 - c)
            )

        def att_in(a2, c2):
            remote_copy(att.at[a2, c2], att.at[a2, c2], asend.at[0, 0], arecv.at[a2, c2], me).wait_recv()

        loop(1, far, lambda i: att_far(far - i).start())
        att_core(0).start()

        c_drain()
        loop(1, gs, lambda i: peer(i).wait_send())
        loop(1, n, lambda i: spread(i).wait_send())

        mine = lax.div(me, group)
        turn = lax.rem(wide - lax.rem(me, group) * oc, wide)

        def own_columns(x):
            return pltpu.roll(x, turn, axis=1)[:, :oc]

        own_tokens = own_columns(token_chunk(mine))
        own_gate = own_columns(jnp.broadcast_to(mod_v[2:3, lanes(mine)], (8, wide)))[0:1]

        def att_pass(i):
            att_in(xor(a, i, far), c)
            att_core(i).start()

        def head_block(first, s):
            x = att[pl.ds(first, span)].astype(F32).reshape(rows, wide).astype(BF16)
            return lax.dot_general(x, wo_v[:, s], NT, preferred_element_type=F32)

        get_wo.wait()
        projected = jnp.zeros((rows, oc), F32)
        if span == 1 and far <= 8:
            for i in range(far):
                if i + 1 < far:
                    att_pass(i + 1)
                a2 = xor(a, i, far)
                att_in(a2, 1 - c)
                projected = projected + head_block(a2, lanes(a2))
        else:
            loop(1, far, att_pass)
            loop(0, far, lambda i: att_in(xor(a, i, far), 1 - c))
            for k in range(blocks):
                projected = projected + head_block(span * k, slice(wide * k, wide * (k + 1)))
        projected = projected.astype(BF16).astype(F32)
        gp[me] = jnp.concatenate([projected[pack * g : pack * (g + 1)] for g in range(group)], axis=1).astype(BF16)

        p_begin, p_near, p_forward, p_across, p_finish, p_drain = gather(gp, psend, precv)

        partly = own_tokens + own_gate * projected
        mean = jnp.sum(partly, axis=-1, keepdims=True) * (1.0 / oc)
        partly = partly - mean
        square = jnp.sum(partly * partly, axis=-1, keepdims=True)
        st[me] = to_lines(mean, square)

        def tell(i):
            return remote_copy(st.at[me], st.at[me], usend.at[i], urecv.at[me], lax.rem(me + i, n))

        loop(1, n, lambda i: tell(i).start())

        p_begin()
        p_near()
        loop(1, far, lambda i: att_far(i).wait_send())
        loop(0, far, lambda i: att_core(i).wait_send())

        def told(i):
            row = lax.rem(me + i, n)
            remote_copy(st.at[row], st.at[row], usend.at[i], urecv.at[row], me).wait_recv()

        def statistics():
            loop(1, n, told)
            means, squares = st[:, 0], st[:, 1]
            middle = jnp.sum(means, axis=0, keepdims=True) * (1.0 / n)
            apart = means - middle
            spread_ = jnp.sum(squares + oc * (apart * apart), axis=0, keepdims=True) * (1.0 / features)
            both = to_columns(jnp.concatenate([middle, lax.rsqrt(spread_ + 1e-06)], axis=0))
            return both[:, 0:1], both[:, 1:2]

        def residual_chunk(k):
            pieces = [gp[group * k + j].astype(F32) for j in range(group)]
            full = jnp.concatenate(
                [
                    jnp.concatenate([piece[:, oc * g : oc * (g + 1)] for piece in pieces], axis=1)
                    for g in range(group)
                ],
                axis=0,
            )
            return token_chunk(k) + mod_v[2:3, lanes(k)] * full

        def grow(k, first, middle, inverse):
            s = lanes(k)
            x = residual_chunk(k)
            res[:, s] = x
            x = ((x - middle) * inverse * (1.0 + mod_v[4:5, s]) + mod_v[3:4, s]).astype(BF16)
            y = lax.dot_general(x, wu_v[:, s], NT, preferred_element_type=F32)
            hacc[...] = y if first else hacc[...] + y

        if group == 2 and far == 4:

            def chunk_of(i, j, first=False):
                a2, b2 = xor(a, i, far), xor(b, j, near)
                row = dev(a2, b2, 1 - c)
                remote_copy(gp.at[row], gp.at[row], psend.at[0, 0], precv.at[row], me).wait_recv()
                grow(a2 * near + b2, first, *stats)

            p_forward(nothing, 1, 3)
            p_across(nothing, 0, 1)
            p_forward(nothing, 3, 4)
            stats = statistics()
            get_wu.wait()
            chunk_of(0, 0, True)
            chunk_of(1, 0)
            chunk_of(0, 1)
            p_across(nothing, 3, 4)
            chunk_of(2, 0)
            p_across(nothing, 1, 2)
            chunk_of(3, 0)
            p_across(nothing, 2, 3)
            chunk_of(3, 1)
            chunk_of(1, 1)
            chunk_of(2, 1)
        else:
            p_forward(nothing)
            p_across(nothing)
            p_finish(nothing)
            stats = statistics()
            get_wu.wait()
            hacc[...] = jnp.zeros_like(hacc)
            lax.fori_loop(0, chunks, lambda k, carry: (grow(k, False, *stats), carry)[1], 0)

        hid[...] = gelu(hacc[...]).astype(BF16)
        get_wd.wait()

        def part_of(q):
            first, last = splits[q]
            p16, got1, sum1, got2, sum2, got3 = reduces[6 * q : 6 * q + 6]
            span_l = range(first, last)

            def own_sum(d):
                return jnp.concatenate([t32[l, at_pack(d), :] for l in span_l], axis=1)

            def down():
                for k in range(chunks):
                    s = slice(wide * k + HEAD_DIM * first, wide * k + HEAD_DIM * last)
                    y = lax.dot_general(hid[...], wd_v[:, s], NN, preferred_element_type=F32)
                    for r in range(own_rows):
                        for l in span_l:
                            at = HEAD_DIM * (l - first)
                            t32[l, pl.ds(own_rows * k + r, n, stride=pack), :] = y[
                                n * r : n * (r + 1), at : at + HEAD_DIM
                            ]

            def copy1(m):
                i, j = far - 1 - m // near, near - 1 - m % near
                chip = xor(a, i, far) * near + xor(b, j, near)
                return chip, remote_copy(
                    p16.at[chip], got1.at[chip], rsend.at[q, 0, m], r1.at[q, chip], dev(a, b, 1 - c)
                )

            def hand(m):
                chip, copy = copy1(m)
                p16[chip] = own_sum(2 * chip + 1 - c).astype(BF16)
                copy.start()

            def pair(chip):
                remote_copy(got1.at[chip], got1.at[chip], rsend.at[q, 0, 0], r1.at[q, chip], me).wait_recv()
                return own_sum(2 * chip + c) + got1[chip].astype(F32)

            def copy_straight(j):
                a2, b2 = xor(a, far - 1, far), xor(b, j, near)
                chip = a2 * near + b2
                at = a * near + b
                return chip, remote_copy(
                    sum1.at[chip], got3.at[at], rsend.at[q, 3, j], r3.at[q, at], dev(a2, b2, c)
                )

            def straight(j):
                chip, copy = copy_straight(j)
                sum1[chip] = pair(chip).astype(BF16)
                copy.start()

            def copy2(m):
                i, j = far - 2 - m // (near - 1), near - 1 - m % (near - 1)
                a2, b2 = xor(a, i, far), xor(b, j, near)
                chip = a2 * near + b2
                at = a2 * near + b
                return chip, remote_copy(sum1.at[chip], got2.at[at], rsend.at[q, 1, m], r2.at[q, at], dev(a, b2, c))

            def second(m):
                chip, copy = copy2(m)
                sum1[chip] = pair(chip).astype(BF16)
                copy.start()

            def collect(i):
                a2 = xor(a, i, far)
                total = pair(a2 * near + b)
                for j in range(1, near):
                    at = a2 * near + xor(b, j, near)
                    remote_copy(got2.at[at], got2.at[at], rsend.at[q, 1, 0], r2.at[q, at], me).wait_recv()
                    total = total + got2[at].astype(F32)
                return a2, total

            def copy3(i):
                a2 = xor(a, i, far)
                at = a * near + b
                return remote_copy(sum2.at[a2], got3.at[at], rsend.at[q, 2, i], r3.at[q, at], dev(a2, b, c))

            def third(m):
                i = far - 1 - m
                a2, total = collect(i)
                sum2[a2] = total.astype(BF16)
                copy3(i).start()

            def last_sum():
                _, total = collect(0)
                for i in range(1, far):
                    for j in range(near if i == far - 1 else 1):
                        at = xor(a, i, far) * near + xor(b, j, near)
                        remote_copy(got3.at[at], got3.at[at], rsend.at[q, 2, 0], r3.at[q, at], me).wait_recv()
                        total = total + got3[at].astype(F32)
                s = slice(HEAD_DIM * first, HEAD_DIM * last)
                pack32[:, s] = own_pack[:, s] + gate_pack[:, s] * total

            def early_drain():
                loop(0, far * near, lambda m: copy1(m)[1].wait_send())

            def drain():
                loop(0, near, lambda j: copy_straight(j)[1].wait_send())
                loop(0, (far - 1) * (near - 1), lambda m: copy2(m)[1].wait_send())
                loop(1, far - 1, lambda i: copy3(i).wait_send())

            stages = [
                down,
                lambda: loop(0, far * near, hand),
                lambda: (loop(0, near, straight), loop(0, (far - 1) * (near - 1), second)),
                lambda: loop(1, far - 1, third),
                last_sum,
            ]
            return stages, early_drain, drain

        todo = [part_of(q) for q in range(len(splits))]
        for stages, _, _ in todo:
            stages[0]()
            stages[1]()
        for step in range(2, 5):
            for stages, _, _ in todo:
                stages[step]()
            if step == 2:
                p_drain()
                loop(1, n, lambda i: tell(i).wait_send())
                for _, early_drain, _ in todo:
                    early_drain()
                for k in range(chunks):
                    s = slice(wide * k, wide * (k + 1))
                    for r in range(own_rows):
                        at = own_rows * k + r
                        own_pack[at : at + 1, :] = res[pl.ds(me + n * r, 1), s]
                        gate_pack[at : at + 1, :] = mod_v[5:6, s]
        for k in range(chunks):
            s = slice(wide * k, wide * (k + 1))
            out[:, s] = pack32[own_rows * k : own_rows * (k + 1), :].astype(BF16)
        for _, _, drain in todo:
            drain()

    def vmem(shape, dtype):
        return pltpu.VMEM(shape, dtype)

    dma = pltpu.SemaphoreType.DMA
    chips = far * near
    packed = (pack, wide)
    return pl.pallas_call(
        body,
        out_shape=jax.ShapeDtypeStruct(tokens.shape, BF16),
        in_specs=[pl.BlockSpec(memory_space=pl.ANY)] * 8,
        out_specs=pl.BlockSpec(memory_space=pltpu.VMEM),
        scratch_shapes=[
            vmem(tokens.shape, BF16),
            vmem(modulation.shape, F32),
            vmem(gains.shape, F32),
            vmem(cache.shape, BF16),
            vmem(wq.shape, BF16),
            vmem(wo.shape, BF16),
            vmem(wu.shape, BF16),
            vmem(wd.shape, BF16),
            vmem((heads, n * pack, HEAD_DIM), F32),
            vmem(packed, F32),
            vmem((n,) + packed, BF16),
            vmem((rows, features), BF16),
            vmem((SLOT, width), F32),
            vmem((blocks, SLOT, wide), BF16),
            vmem((n, SLOT, wide), BF16),
            vmem((rows, 3 * cols), F32),
            vmem((gs, rows, 3 * cols), BF16),
            vmem((n, 2, rows), F32),
            vmem((n, 2, rows), F32),
            vmem((rows, wide), F32),
            vmem((far, 2, part_rows, wide), BF16),
            vmem((n,) + packed, BF16),
            vmem((rows, features), F32),
            vmem((rows, fl), F32),
            vmem((rows, fl), BF16),
            vmem(packed, F32),
            vmem(packed, F32),
            dma((8,)),
            dma((3, chips)),
            dma((n,)),
            dma((3, chips)),
            dma((n,)),
            dma((gs,)),
            dma((gs,)),
            dma((n,)),
            dma((n,)),
            dma((2, far)),
            dma((far, 2)),
            dma((3, chips)),
            dma((n,)),
            dma((n,)),
            dma((n,)),
            dma((len(splits), 4, chips)),
            dma((len(splits), chips)),
            dma((len(splits), chips)),
            dma((len(splits), chips)),
        ]
        + [
            vmem((lines, pack, HEAD_DIM * (last - first)), BF16)
            for first, last in splits
            for lines in (chips, chips, chips, chips, far, chips)
        ],
        compiler_params=pltpu.CompilerParams(
            collective_id=0, has_side_effects=True, vmem_limit_bytes=60 * 1024 * 1024
        ),
        name="block",
    )(tokens, modulation, wq, gains, cache, wo, wu, wd)


def solution(mesh):
    n = mesh.shape["seq"]
    in_specs = (
        P(("groups", "seq"), None),
        P(),
        P(None, None, "seq"),
        P(),
        P(None, None, ("groups", "seq"), None),
        P(None, "seq"),
        P(None, "seq"),
        P("seq", None),
    )
    out_specs = P(("groups", "seq"), None)

    def step(tokens, modulation, w_qkv, norm_gains, cache_kv, w_out, w_up, w_down):
        return fused(
            n,
            tokens,
            modulation,
            jnp.swapaxes(w_qkv, 1, 2),
            norm_gains,
            jnp.swapaxes(cache_kv, 1, 2),
            w_out.T,
            w_up.T,
            w_down,
        )

    return jax.shard_map(step, mesh=mesh, in_specs=in_specs, out_specs=out_specs, check_vma=False)
```

```python
import math

import jax
import jax.numpy as jnp
from jax import lax
from jax.experimental import pallas as pl
from jax.experimental.pallas import tpu as pltpu
from jax.sharding import PartitionSpec as P

HEAD_DIM = 128
HEADS = 20
SLOT = 16
MESH = pl.DeviceIdType.MESH
NT = (((1,), (1,)), ((), ()))
NN = (((1,), (0,)), ((), ()))
F32 = jnp.float32
BF16 = jnp.bfloat16


def factors(n):
    chips = n // 2
    near = 1
    while (2 * near) * (2 * near) <= chips:
        near *= 2
    return chips // near, near


def loop(low, high, fn):
    if high - low <= 8:
        for i in range(low, high):
            fn(i)
        return

    def step(i, c):
        fn(i)
        return c

    lax.fori_loop(low, high, step, 0)


def xor(value, k, size):
    total, bit = 0, 1
    while bit < size:
        digit = lax.rem(lax.div(value, bit), 2)
        other = (k // bit) % 2
        if isinstance(other, int):
            digit = 1 - digit if other else digit
        else:
            digit = lax.rem(digit + other, 2)
        total = total + bit * digit
        bit *= 2
    return total


def remote_copy(src, dst, send, recv, device):
    return pltpu.make_async_remote_copy(
        src_ref=src, dst_ref=dst, send_sem=send, recv_sem=recv, device_id={"seq": device}, device_id_type=MESH
    )


def fold(x):
    total = x[:, :128]
    for k in range(1, x.shape[1] // 128):
        total = total + x[:, 128 * k : 128 * (k + 1)]
    return total


def gelu(x):
    return 0.5 * x * (1.0 + jnp.tanh(math.sqrt(2.0 / math.pi) * (x + 0.044715 * (x * x * x))))


def fused(n, tokens, modulation, wq, gains, cache, wo, wu, wd):
    far, near = factors(n)
    own_rows, features = tokens.shape
    rows = n * own_rows
    width = HEADS * HEAD_DIM
    cols = wq.shape[1]
    wide = math.lcm(cols, HEAD_DIM)
    gs = wide // cols
    blocks = n // gs
    heads = wide // HEAD_DIM
    frames = cache.shape[2]
    held = frames * own_rows
    span = gs // (2 * near)
    part_rows = rows // (2 * span)
    oc = wo.shape[0]
    fl = wu.shape[0]
    chunks = features // wide
    splits = [(0, heads // 2), (heads // 2, heads)]
    pack = own_rows * chunks
    group = wide // oc
    scale = 1.0 / math.sqrt(HEAD_DIM)
    tall = -(-rows // 128) * 128
    assert held <= SLOT // 2 and rows // group == pack and gs % (2 * near) == 0 and far % blocks == 0

    def body(
        tok, mod, wq_h, gains_h, cache_h, wo_h, wu_h, wd_h, out,
        tok_v, mod_v, gains_v, cache_v, wq_v, wo_v, wu_v, wd_v,
        t32, pack32, gt, normed, c32, cown, kv, qacc, qk, sq, st, q32, att,
        gp, res, hacc, hid, own_pack, gate_pack,
        lsem, tsend, trecv, csend, crecv, qsend, qrecv, ssend, srecv, asend, arecv, psend, precv, usend, urecv,
        rsend, r1, r2, r3, *reduces,
    ):
        me = lax.axis_index("seq")
        a, b, c = lax.div(me, 2 * near), lax.rem(lax.div(me, 2), near), lax.rem(me, 2)
        block, place = lax.div(me, gs), lax.rem(me, gs)
        base = block * gs
        part = lax.rem(a, span) * 2 + c

        def dev(a2, b2, c2):
            return (a2 * near + b2) * 2 + c2

        def fetch(k, src, dst):
            copy = pltpu.make_async_copy(src, dst, lsem.at[k])
            copy.start()
            return copy

        barrier = pltpu.get_barrier_semaphore()

        partners = [dev(xor(a, i, far), b, c) for i in range(1, far)]
        partners += [dev(a, xor(b, j, near), c) for j in range(1, near)]
        partners += [dev(xor(a, far - 1, far), xor(b, j, near), c) for j in range(1, near)]
        partners += [dev(a, b, 1 - c)]
        for partner in partners:
            pl.semaphore_signal(barrier, inc=1, device_id={"seq": partner}, device_id_type=MESH)

        get_tok = fetch(0, tok, tok_v)
        get_cache = fetch(1, cache_h, cache_v)
        get_mod = fetch(2, mod, mod_v)
        get_gains = fetch(3, gains_h, gains_v)
        get_wq = fetch(4, wq_h, wq_v)
        get_wo = fetch(5, wo_h, wo_v)
        get_wu = fetch(6, wu_h, wu_v)
        get_wd = fetch(7, wd_h, wd_v)

        def at_pack(d):
            return pl.ds(pl.multiple_of(d * pack, 8), pack)

        def put(d, x):
            for l in range(heads):
                t32[l, at_pack(d), :] = x[:, HEAD_DIM * l : HEAD_DIM * (l + 1)]

        def take(d):
            return jnp.concatenate([t32[l, at_pack(d), :] for l in range(heads)], axis=1)

        def lanes(k):
            return pl.ds(pl.multiple_of(k * wide, wide), wide)

        get_tok.wait()
        for k in range(chunks):
            pack32[own_rows * k : own_rows * (k + 1), :] = tok_v[:, wide * k : wide * (k + 1)].astype(F32)
        put(me, pack32[...])
        gt[me] = pack32[...].astype(BF16)
        get_cache.wait()
        c32[...] = jnp.zeros_like(c32)
        for side in range(2):
            for r in range(own_rows):
                at = SLOT // 2 * side + frames * r
                c32[at : at + frames, :] = cache_v[side, r].astype(F32)
        for k in range(blocks):
            cown[k] = c32[:, wide * k : wide * (k + 1)].astype(BF16)
        kv[me] = c32[:, lanes(block)].astype(BF16)

        pl.semaphore_wait(barrier, len(partners))

        def gather(dst, send, recv, own_part=None):
            def far_copy(i):
                a2 = xor(a, i, far)
                src = dst.at[me] if own_part is None else own_part.at[lax.div(a2 * 2 * near, gs)]
                return remote_copy(src, dst.at[me], send.at[0, i], recv.at[me], dev(a2, b, c))

            def across_copy(j):
                b2 = xor(b, j, near)
                a2 = xor(a, far - 1, far)
                src = dst.at[me] if own_part is None else own_part.at[lax.div(a2 * 2 * near, gs)]
                at = (far - 1) * near + j
                return remote_copy(src, dst.at[me], send.at[1, at], recv.at[me], dev(a2, b2, c))

            def near_copy(i, j):
                row = dev(xor(a, i, far), b, c)
                return remote_copy(
                    dst.at[row], dst.at[row], send.at[1, i * near + j], recv.at[row], dev(a, xor(b, j, near), c)
                )

            def core_copy(i, j):
                row = dev(xor(a, i, far), xor(b, j, near), c)
                return remote_copy(dst.at[row], dst.at[row], send.at[2, i * near + j], recv.at[row], dev(a, b, 1 - c))

            def arrived(row):
                remote_copy(dst.at[row], dst.at[row], send.at[0, 0], recv.at[row], me).wait_recv()

            def begin():
                loop(1, far, lambda i: far_copy(far - 1 - i if i < far - 1 else i).start())
                loop(1, near, lambda j: across_copy(j).start())

            def begin_near():
                loop(1, near, lambda j: near_copy(0, j).start())
                core_copy(0, 0).start()

            def forward(use, low=1, high=far):
                def one(i):
                    row = dev(xor(a, i, far), b, c)
                    arrived(row)
                    if not isinstance(i, int) or i < far - 1:
                        loop(1, near, lambda j: near_copy(i, j).start())
                    core_copy(i, 0).start()
                    use(row)

                loop(low, high, one)

            def across(use, low=0, high=far * (near - 1)):
                def one(m):
                    i, j = m % far, 1 + m // far
                    row = dev(xor(a, i, far), xor(b, j, near), c)
                    arrived(row)
                    core_copy(i, j).start()
                    use(row)

                loop(low, high, one)

            def finish(use):
                def one(m):
                    row = dev(xor(a, m % far, far), xor(b, m // far, near), 1 - c)
                    arrived(row)
                    use(row)

                loop(0, far * near, one)

            def drain():
                loop(1, far, lambda i: far_copy(i).wait_send())
                loop(0, (far - 1) * (near - 1), lambda m: near_copy(m % (far - 1), 1 + m // (far - 1)).wait_send())
                loop(1, near, lambda j: across_copy(j).wait_send())
                loop(0, far * near, lambda m: core_copy(m % far, m // far).wait_send())

            return begin, begin_near, forward, across, finish, drain

        nothing = lambda row: None
        t_begin, t_near, t_forward, t_across, t_finish, t_drain = gather(gt, tsend, trecv)
        c_begin, c_near, c_forward, c_across, c_finish, c_drain = gather(kv, csend, crecv, cown)

        def ingest(row):
            put(row, gt[row].astype(F32))

        t_begin()
        t_near()
        c_begin()
        t_forward(ingest)
        t_across(ingest)
        c_near()
        c_forward(nothing)
        t_finish(ingest)

        def token_chunk(k):
            return jnp.concatenate(
                [
                    jnp.concatenate(
                        [t32[l, pl.ds(own_rows * k + r, n, stride=pack), :] for r in range(own_rows)], axis=0
                    )
                    for l in range(heads)
                ],
                axis=1,
            )

        def to_lines(first, second):
            x = jnp.where(lax.broadcasted_iota(jnp.int32, (rows, 128), 1) == 0, first, second)
            if tall > rows:
                x = jnp.concatenate([x, jnp.zeros((tall - rows, 128), F32)], axis=0)
            return x.T[:2, :rows]

        def to_columns(x):
            if tall > rows:
                x = jnp.concatenate([x, jnp.zeros((2, tall - rows), F32)], axis=1)
            return jnp.concatenate([x, jnp.zeros((6, tall), F32)], axis=0).T[:rows]

        def layer_norm(chunk, shift, gain):
            total = jnp.zeros((rows, 128), F32)
            for k in range(chunks):
                total = total + fold(chunk(k))
            mean = jnp.sum(total, axis=-1, keepdims=True) * (1.0 / features)
            total = jnp.zeros((rows, 128), F32)
            for k in range(chunks):
                center = chunk(k) - mean
                total = total + fold(center * center)
            inverse = lax.rsqrt(jnp.sum(total, axis=-1, keepdims=True) * (1.0 / features) + 1e-06)
            for k in range(chunks):
                s = slice(wide * k, wide * (k + 1))
                normed[:, s] = (
                    (chunk(k) - mean) * inverse * (1.0 + mod_v[gain : gain + 1, s]) + mod_v[shift : shift + 1, s]
                ).astype(BF16)

        get_mod.wait()
        layer_norm(token_chunk, 0, 1)

        get_wq.wait()
        depth = features // 4
        qacc[...] = jnp.zeros_like(qacc)

        def project(k, carry):
            s = pl.ds(pl.multiple_of(k * depth, depth), depth)
            x = normed[:, s]
            if cols % 16 == 0:
                qacc[...] += lax.dot_general(
                    x, wq_v[:, :, s].reshape(3 * cols, depth), NT, preferred_element_type=F32
                )
            else:
                for i in range(3):
                    qacc[:, cols * i : cols * (i + 1)] += lax.dot_general(
                        x, wq_v[i, :, s], NT, preferred_element_type=F32
                    )
            return carry

        lax.fori_loop(0, 4, project, 0)
        rounded = qacc[...].astype(BF16)
        qk[place] = rounded

        def peer(i):
            return remote_copy(
                qk.at[place], qk.at[place], qsend.at[i], qrecv.at[place], base + xor(place, i, gs)
            )

        loop(1, gs, lambda i: peer(gs - i).start())
        exact = rounded.astype(F32)
        square = exact * exact
        sq[me] = to_lines(
            jnp.sum(square[:, :cols], axis=-1, keepdims=True), jnp.sum(square[:, cols : 2 * cols], axis=-1, keepdims=True)
        )

        def spread(i):
            return remote_copy(sq.at[me], sq.at[me], ssend.at[i], srecv.at[me], lax.rem(me + i, n))

        loop(1, n, lambda i: spread(i).start())
        c_across(nothing)

        def squares_in(i):
            row = lax.rem(me + i, n)
            remote_copy(sq.at[row], sq.at[row], ssend.at[i], srecv.at[row], me).wait_recv()

        t_drain()
        loop(1, n, squares_in)
        both = lax.rsqrt(jnp.sum(sq[...], axis=0) * (1.0 / width) + 1e-06)
        inverse = to_columns(both)

        def peer_in(i):
            row = xor(place, i, gs)
            remote_copy(qk.at[row], qk.at[row], qsend.at[i], qrecv.at[row], me).wait_recv()

        loop(1, gs, peer_in)
        get_gains.wait()

        def whole(i):
            return jnp.concatenate([qk[p, :, cols * i : cols * (i + 1)].astype(F32) for p in range(gs)], axis=1)

        q32[...] = whole(0) * inverse[:, 0:1] * gains_v[0:1, lanes(block)]
        keys = (whole(1) * inverse[:, 1:2] * gains_v[1:2, lanes(block)]).astype(BF16)
        values = whole(2).astype(BF16)
        queries = q32[pl.ds(pl.multiple_of(part * part_rows, 8), part_rows), :].astype(BF16)

        c_finish(nothing)
        spot = lax.rem(lax.broadcasted_iota(jnp.int32, (part_rows, n * SLOT), 1), SLOT)
        columns = [slice(HEAD_DIM * h, HEAD_DIM * (h + 1)) for h in range(heads)]
        cached = [kv[:, :, s].reshape(n * SLOT, HEAD_DIM) for s in columns]
        scores = []
        for h, s in enumerate(columns):
            old = lax.dot_general(queries[:, s], cached[h], NT, preferred_element_type=F32) * scale
            new = lax.dot_general(queries[:, s], keys[:, s], NT, preferred_element_type=F32) * scale
            scores.append((jnp.where(spot < held, old, -jnp.inf), new))
        weights = []
        for old, new in scores:
            peak = jnp.maximum(jnp.max(old, axis=-1, keepdims=True), jnp.max(new, axis=-1, keepdims=True))
            old, new = jnp.exp(old - peak), jnp.exp(new - peak)
            total = jnp.sum(old, axis=-1, keepdims=True) + jnp.sum(new, axis=-1, keepdims=True)
            weights.append((pltpu.roll(old, SLOT // 2, axis=1).astype(BF16), new.astype(BF16), total))
        outs = []
        for h, s in enumerate(columns):
            old, new, total = weights[h]
            summed = lax.dot_general(old, cached[h], NN, preferred_element_type=F32) + lax.dot_general(
                new, values[:, s], NN, preferred_element_type=F32
            )
            outs.append((summed / total).astype(BF16))
        att[a, c] = jnp.concatenate(outs, axis=1)

        def att_far(i):
            return remote_copy(
                att.at[a, c], att.at[a, c], asend.at[0, i], arecv.at[a, c], dev(xor(a, i, far), b, c)
            )

        def att_core(i):
            a2 = xor(a, i, far)
            return remote_copy(
                att.at[a2, c], att.at[a2, c], asend.at[1, i], arecv.at[a2, c], dev(a, b, 1 - c)
            )

        def att_in(a2, c2):
            remote_copy(att.at[a2, c2], att.at[a2, c2], asend.at[0, 0], arecv.at[a2, c2], me).wait_recv()

        loop(1, far, lambda i: att_far(far - i).start())
        att_core(0).start()

        c_drain()
        loop(1, gs, lambda i: peer(i).wait_send())
        loop(1, n, lambda i: spread(i).wait_send())

        mine = lax.div(me, group)
        turn = lax.rem(wide - lax.rem(me, group) * oc, wide)

        def own_columns(x):
            return pltpu.roll(x, turn, axis=1)[:, :oc]

        own_tokens = own_columns(token_chunk(mine))
        own_gate = own_columns(jnp.broadcast_to(mod_v[2:3, lanes(mine)], (8, wide)))[0:1]

        def att_pass(i):
            att_in(xor(a, i, far), c)
            att_core(i).start()

        def head_block(first, s):
            x = att[pl.ds(first, span)].astype(F32).reshape(rows, wide).astype(BF16)
            return lax.dot_general(x, wo_v[:, s], NT, preferred_element_type=F32)

        get_wo.wait()
        projected = jnp.zeros((rows, oc), F32)
        if span == 1 and far <= 8:
            for i in range(far):
                if i == 0:
                    loop(1, far, att_pass)
                a2 = xor(a, i, far)
                att_in(a2, 1 - c)
                projected = projected + head_block(a2, lanes(a2))
        else:
            loop(1, far, att_pass)
            loop(0, far, lambda i: att_in(xor(a, i, far), 1 - c))
            for k in range(blocks):
                projected = projected + head_block(span * k, slice(wide * k, wide * (k + 1)))
        projected = projected.astype(BF16).astype(F32)
        gp[me] = jnp.concatenate([projected[pack * g : pack * (g + 1)] for g in range(group)], axis=1).astype(BF16)

        p_begin, p_near, p_forward, p_across, p_finish, p_drain = gather(gp, psend, precv)

        partly = own_tokens + own_gate * projected
        mean = jnp.sum(partly, axis=-1, keepdims=True) * (1.0 / oc)
        partly = partly - mean
        square = jnp.sum(partly * partly, axis=-1, keepdims=True)
        st[me] = to_lines(mean, square)

        def tell(i):
            return remote_copy(st.at[me], st.at[me], usend.at[i], urecv.at[me], lax.rem(me + i, n))

        loop(1, n, lambda i: tell(i).start())

        p_begin()
        p_near()
        loop(1, far, lambda i: att_far(i).wait_send())
        loop(0, far, lambda i: att_core(i).wait_send())

        def told(i):
            row = lax.rem(me + i, n)
            remote_copy(st.at[row], st.at[row], usend.at[i], urecv.at[row], me).wait_recv()

        def statistics():
            loop(1, n, told)
            means, squares = st[:, 0], st[:, 1]
            middle = jnp.sum(means, axis=0, keepdims=True) * (1.0 / n)
            apart = means - middle
            spread_ = jnp.sum(squares + oc * (apart * apart), axis=0, keepdims=True) * (1.0 / features)
            both = to_columns(jnp.concatenate([middle, lax.rsqrt(spread_ + 1e-06)], axis=0))
            return both[:, 0:1], both[:, 1:2]

        def residual_chunk(k):
            pieces = [gp[group * k + j].astype(F32) for j in range(group)]
            full = jnp.concatenate(
                [
                    jnp.concatenate([piece[:, oc * g : oc * (g + 1)] for piece in pieces], axis=1)
                    for g in range(group)
                ],
                axis=0,
            )
            return token_chunk(k) + mod_v[2:3, lanes(k)] * full

        def grow(k, first, middle, inverse):
            s = lanes(k)
            x = residual_chunk(k)
            res[:, s] = x
            x = ((x - middle) * inverse * (1.0 + mod_v[4:5, s]) + mod_v[3:4, s]).astype(BF16)
            y = lax.dot_general(x, wu_v[:, s], NT, preferred_element_type=F32)
            hacc[...] = y if first else hacc[...] + y

        if group == 2 and far == 4:

            def chunk_of(i, j, first=False):
                a2, b2 = xor(a, i, far), xor(b, j, near)
                row = dev(a2, b2, 1 - c)
                remote_copy(gp.at[row], gp.at[row], psend.at[0, 0], precv.at[row], me).wait_recv()
                grow(a2 * near + b2, first, *stats)

            p_forward(nothing, 1, 3)
            p_across(nothing, 0, 1)
            p_forward(nothing, 3, 4)
            stats = statistics()
            get_wu.wait()
            chunk_of(0, 0, True)
            chunk_of(1, 0)
            chunk_of(0, 1)
            p_across(nothing, 3, 4)
            chunk_of(2, 0)
            p_across(nothing, 1, 2)
            chunk_of(3, 0)
            p_across(nothing, 2, 3)
            chunk_of(3, 1)
            chunk_of(1, 1)
            chunk_of(2, 1)
        else:
            p_forward(nothing)
            p_across(nothing)
            p_finish(nothing)
            stats = statistics()
            get_wu.wait()
            hacc[...] = jnp.zeros_like(hacc)
            lax.fori_loop(0, chunks, lambda k, carry: (grow(k, False, *stats), carry)[1], 0)

        hid[...] = gelu(hacc[...]).astype(BF16)
        get_wd.wait()

        def part_of(q):
            first, last = splits[q]
            p16, got1, sum1, got2, sum2, got3 = reduces[6 * q : 6 * q + 6]
            span_l = range(first, last)

            def own_sum(d):
                return jnp.concatenate([t32[l, at_pack(d), :] for l in span_l], axis=1)

            def down():
                for k in range(chunks):
                    s = slice(wide * k + HEAD_DIM * first, wide * k + HEAD_DIM * last)
                    y = lax.dot_general(hid[...], wd_v[:, s], NN, preferred_element_type=F32)
                    for r in range(own_rows):
                        for l in span_l:
                            at = HEAD_DIM * (l - first)
                            t32[l, pl.ds(own_rows * k + r, n, stride=pack), :] = y[
                                n * r : n * (r + 1), at : at + HEAD_DIM
                            ]

            def copy1(m):
                i, j = far - 1 - m // near, near - 1 - m % near
                chip = xor(a, i, far) * near + xor(b, j, near)
                return chip, remote_copy(
                    p16.at[chip], got1.at[chip], rsend.at[q, 0, m], r1.at[q, chip], dev(a, b, 1 - c)
                )

            def hand(m):
                chip, copy = copy1(m)
                p16[chip] = own_sum(2 * chip + 1 - c).astype(BF16)
                copy.start()

            def pair(chip):
                remote_copy(got1.at[chip], got1.at[chip], rsend.at[q, 0, 0], r1.at[q, chip], me).wait_recv()
                return own_sum(2 * chip + c) + got1[chip].astype(F32)

            def copy_straight(j):
                a2, b2 = xor(a, far - 1, far), xor(b, j, near)
                chip = a2 * near + b2
                at = a * near + b
                return chip, remote_copy(
                    sum1.at[chip], got3.at[at], rsend.at[q, 3, j], r3.at[q, at], dev(a2, b2, c)
                )

            def straight(j):
                chip, copy = copy_straight(j)
                sum1[chip] = pair(chip).astype(BF16)
                copy.start()

            def copy2(m):
                i, j = far - 2 - m // (near - 1), near - 1 - m % (near - 1)
                a2, b2 = xor(a, i, far), xor(b, j, near)
                chip = a2 * near + b2
                at = a2 * near + b
                return chip, remote_copy(sum1.at[chip], got2.at[at], rsend.at[q, 1, m], r2.at[q, at], dev(a, b2, c))

            def second(m):
                chip, copy = copy2(m)
                sum1[chip] = pair(chip).astype(BF16)
                copy.start()

            def collect(i):
                a2 = xor(a, i, far)
                total = pair(a2 * near + b)
                for j in range(1, near):
                    at = a2 * near + xor(b, j, near)
                    remote_copy(got2.at[at], got2.at[at], rsend.at[q, 1, 0], r2.at[q, at], me).wait_recv()
                    total = total + got2[at].astype(F32)
                return a2, total

            def copy3(i):
                a2 = xor(a, i, far)
                at = a * near + b
                return remote_copy(sum2.at[a2], got3.at[at], rsend.at[q, 2, i], r3.at[q, at], dev(a2, b, c))

            def third(m):
                i = far - 1 - m
                a2, total = collect(i)
                sum2[a2] = total.astype(BF16)
                copy3(i).start()

            def last_sum():
                _, total = collect(0)
                for i in range(1, far):
                    for j in range(near if i == far - 1 else 1):
                        at = xor(a, i, far) * near + xor(b, j, near)
                        remote_copy(got3.at[at], got3.at[at], rsend.at[q, 2, 0], r3.at[q, at], me).wait_recv()
                        total = total + got3[at].astype(F32)
                s = slice(HEAD_DIM * first, HEAD_DIM * last)
                pack32[:, s] = own_pack[:, s] + gate_pack[:, s] * total

            def early_drain():
                loop(0, far * near, lambda m: copy1(m)[1].wait_send())

            def drain():
                loop(0, near, lambda j: copy_straight(j)[1].wait_send())
                loop(0, (far - 1) * (near - 1), lambda m: copy2(m)[1].wait_send())
                loop(1, far - 1, lambda i: copy3(i).wait_send())

            stages = [
                down,
                lambda: loop(0, far * near, hand),
                lambda: (loop(0, near, straight), loop(0, (far - 1) * (near - 1), second)),
                lambda: loop(1, far - 1, third),
                last_sum,
            ]
            return stages, early_drain, drain

        todo = [part_of(q) for q in range(len(splits))]
        for stages, _, _ in todo:
            stages[0]()
            stages[1]()
        for step in range(2, 5):
            for stages, _, _ in todo:
                stages[step]()
            if step == 2:
                p_drain()
                loop(1, n, lambda i: tell(i).wait_send())
                for _, early_drain, _ in todo:
                    early_drain()
                for k in range(chunks):
                    s = slice(wide * k, wide * (k + 1))
                    for r in range(own_rows):
                        at = own_rows * k + r
                        own_pack[at : at + 1, :] = res[pl.ds(me + n * r, 1), s]
                        gate_pack[at : at + 1, :] = mod_v[5:6, s]
        for k in range(chunks):
            s = slice(wide * k, wide * (k + 1))
            out[:, s] = pack32[own_rows * k : own_rows * (k + 1), :].astype(BF16)
        for _, _, drain in todo:
            drain()

    def vmem(shape, dtype):
        return pltpu.VMEM(shape, dtype)

    dma = pltpu.SemaphoreType.DMA
    chips = far * near
    packed = (pack, wide)
    return pl.pallas_call(
        body,
        out_shape=jax.ShapeDtypeStruct(tokens.shape, BF16),
        in_specs=[pl.BlockSpec(memory_space=pl.ANY)] * 8,
        out_specs=pl.BlockSpec(memory_space=pltpu.VMEM),
        scratch_shapes=[
            vmem(tokens.shape, BF16),
            vmem(modulation.shape, F32),
            vmem(gains.shape, F32),
            vmem(cache.shape, BF16),
            vmem(wq.shape, BF16),
            vmem(wo.shape, BF16),
            vmem(wu.shape, BF16),
            vmem(wd.shape, BF16),
            vmem((heads, n * pack, HEAD_DIM), F32),
            vmem(packed, F32),
            vmem((n,) + packed, BF16),
            vmem((rows, features), BF16),
            vmem((SLOT, width), F32),
            vmem((blocks, SLOT, wide), BF16),
            vmem((n, SLOT, wide), BF16),
            vmem((rows, 3 * cols), F32),
            vmem((gs, rows, 3 * cols), BF16),
            vmem((n, 2, rows), F32),
            vmem((n, 2, rows), F32),
            vmem((rows, wide), F32),
            vmem((far, 2, part_rows, wide), BF16),
            vmem((n,) + packed, BF16),
            vmem((rows, features), F32),
            vmem((rows, fl), F32),
            vmem((rows, fl), BF16),
            vmem(packed, F32),
            vmem(packed, F32),
            dma((8,)),
            dma((3, chips)),
            dma((n,)),
            dma((3, chips)),
            dma((n,)),
            dma((gs,)),
            dma((gs,)),
            dma((n,)),
            dma((n,)),
            dma((2, far)),
            dma((far, 2)),
            dma((3, chips)),
            dma((n,)),
            dma((n,)),
            dma((n,)),
            dma((len(splits), 4, chips)),
            dma((len(splits), chips)),
            dma((len(splits), chips)),
            dma((len(splits), chips)),
        ]
        + [
            vmem((lines, pack, HEAD_DIM * (last - first)), BF16)
            for first, last in splits
            for lines in (chips, chips, chips, chips, far, chips)
        ],
        compiler_params=pltpu.CompilerParams(
            collective_id=0, has_side_effects=True, vmem_limit_bytes=60 * 1024 * 1024
        ),
        name="block",
    )(tokens, modulation, wq, gains, cache, wo, wu, wd)


def solution(mesh):
    n = mesh.shape["seq"]
    in_specs = (
        P(("groups", "seq"), None),
        P(),
        P(None, None, "seq"),
        P(),
        P(None, None, ("groups", "seq"), None),
        P(None, "seq"),
        P(None, "seq"),
        P("seq", None),
    )
    out_specs = P(("groups", "seq"), None)

    def step(tokens, modulation, w_qkv, norm_gains, cache_kv, w_out, w_up, w_down):
        return fused(
            n,
            tokens,
            modulation,
            jnp.swapaxes(w_qkv, 1, 2),
            norm_gains,
            jnp.swapaxes(cache_kv, 1, 2),
            w_out.T,
            w_up.T,
            w_down,
        )

    return jax.shard_map(step, mesh=mesh, in_specs=in_specs, out_specs=out_specs, check_vma=False)
```

```python
import math

import jax
import jax.numpy as jnp
from jax import lax
from jax.experimental import pallas as pl
from jax.experimental.pallas import tpu as pltpu
from jax.sharding import PartitionSpec as P

HEAD_DIM = 128
HEADS = 20
SLOT = 16
MESH = pl.DeviceIdType.MESH
NT = (((1,), (1,)), ((), ()))
NN = (((1,), (0,)), ((), ()))
F32 = jnp.float32
BF16 = jnp.bfloat16


def factors(n):
    chips = n // 2
    near = 1
    while (2 * near) * (2 * near) <= chips:
        near *= 2
    return chips // near, near


def loop(low, high, fn):
    if high - low <= 8:
        for i in range(low, high):
            fn(i)
        return

    def step(i, c):
        fn(i)
        return c

    lax.fori_loop(low, high, step, 0)


def xor(value, k, size):
    total, bit = 0, 1
    while bit < size:
        digit = lax.rem(lax.div(value, bit), 2)
        other = (k // bit) % 2
        if isinstance(other, int):
            digit = 1 - digit if other else digit
        else:
            digit = lax.rem(digit + other, 2)
        total = total + bit * digit
        bit *= 2
    return total


def remote_copy(src, dst, send, recv, device):
    return pltpu.make_async_remote_copy(
        src_ref=src, dst_ref=dst, send_sem=send, recv_sem=recv, device_id={"seq": device}, device_id_type=MESH
    )


def fold(x):
    total = x[:, :128]
    for k in range(1, x.shape[1] // 128):
        total = total + x[:, 128 * k : 128 * (k + 1)]
    return total


def gelu(x):
    return 0.5 * x * (1.0 + jnp.tanh(math.sqrt(2.0 / math.pi) * (x + 0.044715 * (x * x * x))))


def fused(n, tokens, modulation, wq, gains, cache, wo, wu, wd):
    far, near = factors(n)
    own_rows, features = tokens.shape
    rows = n * own_rows
    width = HEADS * HEAD_DIM
    cols = wq.shape[1]
    wide = math.lcm(cols, HEAD_DIM)
    gs = wide // cols
    blocks = n // gs
    heads = wide // HEAD_DIM
    frames = cache.shape[2]
    held = frames * own_rows
    span = gs // (2 * near)
    part_rows = rows // (2 * span)
    oc = wo.shape[0]
    fl = wu.shape[0]
    chunks = features // wide
    splits = [(0, heads // 2), (heads // 2, heads)]
    pack = own_rows * chunks
    group = wide // oc
    scale = 1.0 / math.sqrt(HEAD_DIM)
    tall = -(-rows // 128) * 128
    assert held <= SLOT // 2 and rows // group == pack and gs % (2 * near) == 0 and far % blocks == 0

    def body(
        tok, mod, wq_h, gains_h, cache_h, wo_h, wu_h, wd_h, out,
        tok_v, mod_v, gains_v, cache_v, wq_v, wo_v, wu_v, wd_v,
        t32, pack32, gt, normed, c32, cown, kv, qacc, qk, sq, st, q32, att,
        gp, res, hacc, hid, own_pack, gate_pack,
        lsem, tsend, trecv, csend, crecv, qsend, qrecv, ssend, srecv, asend, arecv, psend, precv, usend, urecv,
        rsend, r1, r2, r3, *reduces,
    ):
        me = lax.axis_index("seq")
        a, b, c = lax.div(me, 2 * near), lax.rem(lax.div(me, 2), near), lax.rem(me, 2)
        block, place = lax.div(me, gs), lax.rem(me, gs)
        base = block * gs
        part = lax.rem(a, span) * 2 + c

        def dev(a2, b2, c2):
            return (a2 * near + b2) * 2 + c2

        def fetch(k, src, dst):
            copy = pltpu.make_async_copy(src, dst, lsem.at[k])
            copy.start()
            return copy

        barrier = pltpu.get_barrier_semaphore()

        partners = [dev(xor(a, i, far), b, c) for i in range(1, far)]
        partners += [dev(a, xor(b, j, near), c) for j in range(1, near)]
        partners += [dev(xor(a, far - 1, far), xor(b, j, near), c) for j in range(1, near)]
        partners += [dev(a, b, 1 - c)]
        for partner in partners:
            pl.semaphore_signal(barrier, inc=1, device_id={"seq": partner}, device_id_type=MESH)

        get_tok = fetch(0, tok, tok_v)
        get_cache = fetch(1, cache_h, cache_v)
        get_mod = fetch(2, mod, mod_v)
        get_gains = fetch(3, gains_h, gains_v)
        get_wq = fetch(4, wq_h, wq_v)
        get_wo = fetch(5, wo_h, wo_v)
        get_wu = fetch(6, wu_h, wu_v)
        get_wd = fetch(7, wd_h, wd_v)

        def at_pack(d):
            return pl.ds(pl.multiple_of(d * pack, 8), pack)

        def put(d, x):
            for l in range(heads):
                t32[l, at_pack(d), :] = x[:, HEAD_DIM * l : HEAD_DIM * (l + 1)]

        def take(d):
            return jnp.concatenate([t32[l, at_pack(d), :] for l in range(heads)], axis=1)

        def lanes(k):
            return pl.ds(pl.multiple_of(k * wide, wide), wide)

        get_tok.wait()
        for k in range(chunks):
            pack32[own_rows * k : own_rows * (k + 1), :] = tok_v[:, wide * k : wide * (k + 1)].astype(F32)
        put(me, pack32[...])
        gt[me] = pack32[...].astype(BF16)
        get_cache.wait()
        c32[...] = jnp.zeros_like(c32)
        for side in range(2):
            for r in range(own_rows):
                at = SLOT // 2 * side + frames * r
                c32[at : at + frames, :] = cache_v[side, r].astype(F32)
        for k in range(blocks):
            cown[k] = c32[:, wide * k : wide * (k + 1)].astype(BF16)
        kv[me] = c32[:, lanes(block)].astype(BF16)

        pl.semaphore_wait(barrier, len(partners))

        def gather(dst, send, recv, own_part=None):
            def far_copy(i):
                a2 = xor(a, i, far)
                src = dst.at[me] if own_part is None else own_part.at[lax.div(a2 * 2 * near, gs)]
                return remote_copy(src, dst.at[me], send.at[0, i], recv.at[me], dev(a2, b, c))

            def across_copy(j):
                b2 = xor(b, j, near)
                a2 = xor(a, far - 1, far)
                src = dst.at[me] if own_part is None else own_part.at[lax.div(a2 * 2 * near, gs)]
                at = (far - 1) * near + j
                return remote_copy(src, dst.at[me], send.at[1, at], recv.at[me], dev(a2, b2, c))

            def near_copy(i, j):
                row = dev(xor(a, i, far), b, c)
                return remote_copy(
                    dst.at[row], dst.at[row], send.at[1, i * near + j], recv.at[row], dev(a, xor(b, j, near), c)
                )

            def core_copy(i, j):
                row = dev(xor(a, i, far), xor(b, j, near), c)
                return remote_copy(dst.at[row], dst.at[row], send.at[2, i * near + j], recv.at[row], dev(a, b, 1 - c))

            def arrived(row):
                remote_copy(dst.at[row], dst.at[row], send.at[0, 0], recv.at[row], me).wait_recv()

            def begin():
                loop(1, far, lambda i: far_copy(far - 1 - i if i < far - 1 else i).start())
                loop(1, near, lambda j: across_copy(j).start())

            def begin_near():
                loop(1, near, lambda j: near_copy(0, j).start())
                core_copy(0, 0).start()

            def forward(use, low=1, high=far):
                def one(i):
                    row = dev(xor(a, i, far), b, c)
                    arrived(row)
                    if not isinstance(i, int) or i < far - 1:
                        loop(1, near, lambda j: near_copy(i, j).start())
                    core_copy(i, 0).start()
                    use(row)

                loop(low, high, one)

            def across(use, low=0, high=far * (near - 1)):
                def one(m):
                    i, j = m % far, 1 + m // far
                    row = dev(xor(a, i, far), xor(b, j, near), c)
                    arrived(row)
                    core_copy(i, j).start()
                    use(row)

                loop(low, high, one)

            def finish(use):
                def one(m):
                    row = dev(xor(a, m % far, far), xor(b, m // far, near), 1 - c)
                    arrived(row)
                    use(row)

                loop(0, far * near, one)

            def drain():
                loop(1, far, lambda i: far_copy(i).wait_send())
                loop(0, (far - 1) * (near - 1), lambda m: near_copy(m % (far - 1), 1 + m // (far - 1)).wait_send())
                loop(1, near, lambda j: across_copy(j).wait_send())
                loop(0, far * near, lambda m: core_copy(m % far, m // far).wait_send())

            return begin, begin_near, forward, across, finish, drain

        nothing = lambda row: None
        t_begin, t_near, t_forward, t_across, t_finish, t_drain = gather(gt, tsend, trecv)
        c_begin, c_near, c_forward, c_across, c_finish, c_drain = gather(kv, csend, crecv, cown)

        def ingest(row):
            put(row, gt[row].astype(F32))

        t_begin()
        t_near()
        c_begin()
        t_forward(nothing)
        t_across(nothing)
        c_near()
        c_forward(nothing)
        loop(1, far * near, lambda m: ingest(dev(xor(a, m % far, far), xor(b, m // far, near), c)))
        t_finish(ingest)

        def token_chunk(k):
            return jnp.concatenate(
                [
                    jnp.concatenate(
                        [t32[l, pl.ds(own_rows * k + r, n, stride=pack), :] for r in range(own_rows)], axis=0
                    )
                    for l in range(heads)
                ],
                axis=1,
            )

        def to_lines(first, second):
            x = jnp.where(lax.broadcasted_iota(jnp.int32, (rows, 128), 1) == 0, first, second)
            if tall > rows:
                x = jnp.concatenate([x, jnp.zeros((tall - rows, 128), F32)], axis=0)
            return x.T[:2, :rows]

        def to_columns(x):
            if tall > rows:
                x = jnp.concatenate([x, jnp.zeros((2, tall - rows), F32)], axis=1)
            return jnp.concatenate([x, jnp.zeros((6, tall), F32)], axis=0).T[:rows]

        def layer_norm(chunk, shift, gain):
            total = jnp.zeros((rows, 128), F32)
            for k in range(chunks):
                total = total + fold(chunk(k))
            mean = jnp.sum(total, axis=-1, keepdims=True) * (1.0 / features)
            total = jnp.zeros((rows, 128), F32)
            for k in range(chunks):
                center = chunk(k) - mean
                total = total + fold(center * center)
            inverse = lax.rsqrt(jnp.sum(total, axis=-1, keepdims=True) * (1.0 / features) + 1e-06)
            for k in range(chunks):
                s = slice(wide * k, wide * (k + 1))
                normed[:, s] = (
                    (chunk(k) - mean) * inverse * (1.0 + mod_v[gain : gain + 1, s]) + mod_v[shift : shift + 1, s]
                ).astype(BF16)

        get_mod.wait()
        layer_norm(token_chunk, 0, 1)

        get_wq.wait()
        depth = features // 4
        qacc[...] = jnp.zeros_like(qacc)

        def project(k, carry):
            s = pl.ds(pl.multiple_of(k * depth, depth), depth)
            x = normed[:, s]
            if cols % 16 == 0:
                qacc[...] += lax.dot_general(
                    x, wq_v[:, :, s].reshape(3 * cols, depth), NT, preferred_element_type=F32
                )
            else:
                for i in range(3):
                    qacc[:, cols * i : cols * (i + 1)] += lax.dot_general(
                        x, wq_v[i, :, s], NT, preferred_element_type=F32
                    )
            return carry

        lax.fori_loop(0, 4, project, 0)
        rounded = qacc[...].astype(BF16)
        qk[place] = rounded

        def peer(i):
            return remote_copy(
                qk.at[place], qk.at[place], qsend.at[i], qrecv.at[place], base + xor(place, i, gs)
            )

        loop(1, gs, lambda i: peer(gs - i).start())
        exact = rounded.astype(F32)
        square = exact * exact
        sq[me] = to_lines(
            jnp.sum(square[:, :cols], axis=-1, keepdims=True), jnp.sum(square[:, cols : 2 * cols], axis=-1, keepdims=True)
        )

        def spread(i):
            return remote_copy(sq.at[me], sq.at[me], ssend.at[i], srecv.at[me], lax.rem(me + i, n))

        loop(1, n, lambda i: spread(i).start())
        c_across(nothing)

        def squares_in(i):
            row = lax.rem(me + i, n)
            remote_copy(sq.at[row], sq.at[row], ssend.at[i], srecv.at[row], me).wait_recv()

        t_drain()
        loop(1, n, squares_in)
        both = lax.rsqrt(jnp.sum(sq[...], axis=0) * (1.0 / width) + 1e-06)
        inverse = to_columns(both)

        def peer_in(i):
            row = xor(place, i, gs)
            remote_copy(qk.at[row], qk.at[row], qsend.at[i], qrecv.at[row], me).wait_recv()

        loop(1, gs, peer_in)
        get_gains.wait()

        def whole(i):
            return jnp.concatenate([qk[p, :, cols * i : cols * (i + 1)].astype(F32) for p in range(gs)], axis=1)

        q32[...] = whole(0) * inverse[:, 0:1] * gains_v[0:1, lanes(block)]
        keys = (whole(1) * inverse[:, 1:2] * gains_v[1:2, lanes(block)]).astype(BF16)
        values = whole(2).astype(BF16)
        queries = q32[pl.ds(pl.multiple_of(part * part_rows, 8), part_rows), :].astype(BF16)

        c_finish(nothing)
        spot = lax.rem(lax.broadcasted_iota(jnp.int32, (part_rows, n * SLOT), 1), SLOT)
        columns = [slice(HEAD_DIM * h, HEAD_DIM * (h + 1)) for h in range(heads)]
        cached = [kv[:, :, s].reshape(n * SLOT, HEAD_DIM) for s in columns]
        scores = []
        for h, s in enumerate(columns):
            old = lax.dot_general(queries[:, s], cached[h], NT, preferred_element_type=F32) * scale
            new = lax.dot_general(queries[:, s], keys[:, s], NT, preferred_element_type=F32) * scale
            scores.append((jnp.where(spot < held, old, -jnp.inf), new))
        weights = []
        for old, new in scores:
            peak = jnp.maximum(jnp.max(old, axis=-1, keepdims=True), jnp.max(new, axis=-1, keepdims=True))
            old, new = jnp.exp(old - peak), jnp.exp(new - peak)
            total = jnp.sum(old, axis=-1, keepdims=True) + jnp.sum(new, axis=-1, keepdims=True)
            weights.append((pltpu.roll(old, SLOT // 2, axis=1).astype(BF16), new.astype(BF16), total))
        outs = []
        for h, s in enumerate(columns):
            old, new, total = weights[h]
            summed = lax.dot_general(old, cached[h], NN, preferred_element_type=F32) + lax.dot_general(
                new, values[:, s], NN, preferred_element_type=F32
            )
            outs.append((summed / total).astype(BF16))
        att[a, c] = jnp.concatenate(outs, axis=1)

        def att_far(i):
            return remote_copy(
                att.at[a, c], att.at[a, c], asend.at[0, i], arecv.at[a, c], dev(xor(a, i, far), b, c)
            )

        def att_core(i):
            a2 = xor(a, i, far)
            return remote_copy(
                att.at[a2, c], att.at[a2, c], asend.at[1, i], arecv.at[a2, c], dev(a, b, 1 - c)
            )

        def att_in(a2, c2):
            remote_copy(att.at[a2, c2], att.at[a2, c2], asend.at[0, 0], arecv.at[a2, c2], me).wait_recv()

        loop(1, far, lambda i: att_far(far - i).start())
        att_core(0).start()

        c_drain()
        loop(1, gs, lambda i: peer(i).wait_send())
        loop(1, n, lambda i: spread(i).wait_send())

        mine = lax.div(me, group)
        turn = lax.rem(wide - lax.rem(me, group) * oc, wide)

        def own_columns(x):
            return pltpu.roll(x, turn, axis=1)[:, :oc]

        own_tokens = own_columns(token_chunk(mine))
        own_gate = own_columns(jnp.broadcast_to(mod_v[2:3, lanes(mine)], (8, wide)))[0:1]

        def att_pass(i):
            att_in(xor(a, i, far), c)
            att_core(i).start()

        def head_block(first, s):
            x = att[pl.ds(first, span)].astype(F32).reshape(rows, wide).astype(BF16)
            return lax.dot_general(x, wo_v[:, s], NT, preferred_element_type=F32)

        get_wo.wait()
        projected = jnp.zeros((rows, oc), F32)
        if span == 1 and far <= 8:
            for i in range(far):
                if i == 0:
                    loop(1, far, att_pass)
                a2 = xor(a, i, far)
                att_in(a2, 1 - c)
                projected = projected + head_block(a2, lanes(a2))
        else:
            loop(1, far, att_pass)
            loop(0, far, lambda i: att_in(xor(a, i, far), 1 - c))
            for k in range(blocks):
                projected = projected + head_block(span * k, slice(wide * k, wide * (k + 1)))
        projected = projected.astype(BF16).astype(F32)
        gp[me] = jnp.concatenate([projected[pack * g : pack * (g + 1)] for g in range(group)], axis=1).astype(BF16)

        p_begin, p_near, p_forward, p_across, p_finish, p_drain = gather(gp, psend, precv)

        partly = own_tokens + own_gate * projected
        mean = jnp.sum(partly, axis=-1, keepdims=True) * (1.0 / oc)
        partly = partly - mean
        square = jnp.sum(partly * partly, axis=-1, keepdims=True)
        st[me] = to_lines(mean, square)

        def tell(i):
            return remote_copy(st.at[me], st.at[me], usend.at[i], urecv.at[me], lax.rem(me + i, n))

        loop(1, n, lambda i: tell(i).start())

        p_begin()
        p_near()
        loop(1, far, lambda i: att_far(i).wait_send())
        loop(0, far, lambda i: att_core(i).wait_send())

        def told(i):
            row = lax.rem(me + i, n)
            remote_copy(st.at[row], st.at[row], usend.at[i], urecv.at[row], me).wait_recv()

        def statistics():
            loop(1, n, told)
            means, squares = st[:, 0], st[:, 1]
            middle = jnp.sum(means, axis=0, keepdims=True) * (1.0 / n)
            apart = means - middle
            spread_ = jnp.sum(squares + oc * (apart * apart), axis=0, keepdims=True) * (1.0 / features)
            both = to_columns(jnp.concatenate([middle, lax.rsqrt(spread_ + 1e-06)], axis=0))
            return both[:, 0:1], both[:, 1:2]

        def residual_chunk(k):
            pieces = [gp[group * k + j].astype(F32) for j in range(group)]
            full = jnp.concatenate(
                [
                    jnp.concatenate([piece[:, oc * g : oc * (g + 1)] for piece in pieces], axis=1)
                    for g in range(group)
                ],
                axis=0,
            )
            return token_chunk(k) + mod_v[2:3, lanes(k)] * full

        def grow(k, first, middle, inverse):
            s = lanes(k)
            x = residual_chunk(k)
            res[:, s] = x
            x = ((x - middle) * inverse * (1.0 + mod_v[4:5, s]) + mod_v[3:4, s]).astype(BF16)
            y = lax.dot_general(x, wu_v[:, s], NT, preferred_element_type=F32)
            hacc[...] = y if first else hacc[...] + y

        if group == 2 and far == 4:

            def chunk_of(i, j, first=False):
                a2, b2 = xor(a, i, far), xor(b, j, near)
                row = dev(a2, b2, 1 - c)
                remote_copy(gp.at[row], gp.at[row], psend.at[0, 0], precv.at[row], me).wait_recv()
                grow(a2 * near + b2, first, *stats)

            p_forward(nothing, 1, 3)
            p_across(nothing, 0, 1)
            p_forward(nothing, 3, 4)
            stats = statistics()
            get_wu.wait()
            chunk_of(0, 0, True)
            chunk_of(1, 0)
            chunk_of(0, 1)
            p_across(nothing, 3, 4)
            chunk_of(2, 0)
            p_across(nothing, 1, 2)
            chunk_of(3, 0)
            p_across(nothing, 2, 3)
            chunk_of(3, 1)
            chunk_of(1, 1)
            chunk_of(2, 1)
        else:
            p_forward(nothing)
            p_across(nothing)
            p_finish(nothing)
            stats = statistics()
            get_wu.wait()
            hacc[...] = jnp.zeros_like(hacc)
            lax.fori_loop(0, chunks, lambda k, carry: (grow(k, False, *stats), carry)[1], 0)

        hid[...] = gelu(hacc[...]).astype(BF16)
        get_wd.wait()

        def part_of(q):
            first, last = splits[q]
            p16, got1, sum1, got2, sum2, got3 = reduces[6 * q : 6 * q + 6]
            span_l = range(first, last)

            def own_sum(d):
                return jnp.concatenate([t32[l, at_pack(d), :] for l in span_l], axis=1)

            def down():
                for k in range(chunks):
                    s = slice(wide * k + HEAD_DIM * first, wide * k + HEAD_DIM * last)
                    y = lax.dot_general(hid[...], wd_v[:, s], NN, preferred_element_type=F32)
                    for r in range(own_rows):
                        for l in span_l:
                            at = HEAD_DIM * (l - first)
                            t32[l, pl.ds(own_rows * k + r, n, stride=pack), :] = y[
                                n * r : n * (r + 1), at : at + HEAD_DIM
                            ]

            def copy1(m):
                i, j = far - 1 - m // near, near - 1 - m % near
                chip = xor(a, i, far) * near + xor(b, j, near)
                return chip, remote_copy(
                    p16.at[chip], got1.at[chip], rsend.at[q, 0, m], r1.at[q, chip], dev(a, b, 1 - c)
                )

            def hand(m):
                chip, copy = copy1(m)
                p16[chip] = own_sum(2 * chip + 1 - c).astype(BF16)
                copy.start()

            def pair(chip):
                remote_copy(got1.at[chip], got1.at[chip], rsend.at[q, 0, 0], r1.at[q, chip], me).wait_recv()
                return own_sum(2 * chip + c) + got1[chip].astype(F32)

            def copy_straight(j):
                a2, b2 = xor(a, far - 1, far), xor(b, j, near)
                chip = a2 * near + b2
                at = a * near + b
                return chip, remote_copy(
                    sum1.at[chip], got3.at[at], rsend.at[q, 3, j], r3.at[q, at], dev(a2, b2, c)
                )

            def straight(j):
                chip, copy = copy_straight(j)
                sum1[chip] = pair(chip).astype(BF16)
                copy.start()

            def copy2(m):
                i, j = far - 2 - m // (near - 1), near - 1 - m % (near - 1)
                a2, b2 = xor(a, i, far), xor(b, j, near)
                chip = a2 * near + b2
                at = a2 * near + b
                return chip, remote_copy(sum1.at[chip], got2.at[at], rsend.at[q, 1, m], r2.at[q, at], dev(a, b2, c))

            def second(m):
                chip, copy = copy2(m)
                sum1[chip] = pair(chip).astype(BF16)
                copy.start()

            def collect(i):
                a2 = xor(a, i, far)
                total = pair(a2 * near + b)
                for j in range(1, near):
                    at = a2 * near + xor(b, j, near)
                    remote_copy(got2.at[at], got2.at[at], rsend.at[q, 1, 0], r2.at[q, at], me).wait_recv()
                    total = total + got2[at].astype(F32)
                return a2, total

            def copy3(i):
                a2 = xor(a, i, far)
                at = a * near + b
                return remote_copy(sum2.at[a2], got3.at[at], rsend.at[q, 2, i], r3.at[q, at], dev(a2, b, c))

            def third(m):
                i = far - 1 - m
                a2, total = collect(i)
                sum2[a2] = total.astype(BF16)
                copy3(i).start()

            def last_sum():
                _, total = collect(0)
                for i in range(1, far):
                    for j in range(near if i == far - 1 else 1):
                        at = xor(a, i, far) * near + xor(b, j, near)
                        remote_copy(got3.at[at], got3.at[at], rsend.at[q, 2, 0], r3.at[q, at], me).wait_recv()
                        total = total + got3[at].astype(F32)
                s = slice(HEAD_DIM * first, HEAD_DIM * last)
                pack32[:, s] = own_pack[:, s] + gate_pack[:, s] * total

            def early_drain():
                loop(0, far * near, lambda m: copy1(m)[1].wait_send())

            def drain():
                loop(0, near, lambda j: copy_straight(j)[1].wait_send())
                loop(0, (far - 1) * (near - 1), lambda m: copy2(m)[1].wait_send())
                loop(1, far - 1, lambda i: copy3(i).wait_send())

            stages = [
                down,
                lambda: loop(0, far * near, hand),
                lambda: (loop(0, near, straight), loop(0, (far - 1) * (near - 1), second)),
                lambda: loop(1, far - 1, third),
                last_sum,
            ]
            return stages, early_drain, drain

        todo = [part_of(q) for q in range(len(splits))]
        for stages, _, _ in todo:
            stages[0]()
            stages[1]()
        for step in range(2, 5):
            for stages, _, _ in todo:
                stages[step]()
            if step == 2:
                p_drain()
                loop(1, n, lambda i: tell(i).wait_send())
                for _, early_drain, _ in todo:
                    early_drain()
                for k in range(chunks):
                    s = slice(wide * k, wide * (k + 1))
                    for r in range(own_rows):
                        at = own_rows * k + r
                        own_pack[at : at + 1, :] = res[pl.ds(me + n * r, 1), s]
                        gate_pack[at : at + 1, :] = mod_v[5:6, s]
        for k in range(chunks):
            s = slice(wide * k, wide * (k + 1))
            out[:, s] = pack32[own_rows * k : own_rows * (k + 1), :].astype(BF16)
        for _, _, drain in todo:
            drain()

    def vmem(shape, dtype):
        return pltpu.VMEM(shape, dtype)

    dma = pltpu.SemaphoreType.DMA
    chips = far * near
    packed = (pack, wide)
    return pl.pallas_call(
        body,
        out_shape=jax.ShapeDtypeStruct(tokens.shape, BF16),
        in_specs=[pl.BlockSpec(memory_space=pl.ANY)] * 8,
        out_specs=pl.BlockSpec(memory_space=pltpu.VMEM),
        scratch_shapes=[
            vmem(tokens.shape, BF16),
            vmem(modulation.shape, F32),
            vmem(gains.shape, F32),
            vmem(cache.shape, BF16),
            vmem(wq.shape, BF16),
            vmem(wo.shape, BF16),
            vmem(wu.shape, BF16),
            vmem(wd.shape, BF16),
            vmem((heads, n * pack, HEAD_DIM), F32),
            vmem(packed, F32),
            vmem((n,) + packed, BF16),
            vmem((rows, features), BF16),
            vmem((SLOT, width), F32),
            vmem((blocks, SLOT, wide), BF16),
            vmem((n, SLOT, wide), BF16),
            vmem((rows, 3 * cols), F32),
            vmem((gs, rows, 3 * cols), BF16),
            vmem((n, 2, rows), F32),
            vmem((n, 2, rows), F32),
            vmem((rows, wide), F32),
            vmem((far, 2, part_rows, wide), BF16),
            vmem((n,) + packed, BF16),
            vmem((rows, features), F32),
            vmem((rows, fl), F32),
            vmem((rows, fl), BF16),
            vmem(packed, F32),
            vmem(packed, F32),
            dma((8,)),
            dma((3, chips)),
            dma((n,)),
            dma((3, chips)),
            dma((n,)),
            dma((gs,)),
            dma((gs,)),
            dma((n,)),
            dma((n,)),
            dma((2, far)),
            dma((far, 2)),
            dma((3, chips)),
            dma((n,)),
            dma((n,)),
            dma((n,)),
            dma((len(splits), 4, chips)),
            dma((len(splits), chips)),
            dma((len(splits), chips)),
            dma((len(splits), chips)),
        ]
        + [
            vmem((lines, pack, HEAD_DIM * (last - first)), BF16)
            for first, last in splits
            for lines in (chips, chips, chips, chips, far, chips)
        ],
        compiler_params=pltpu.CompilerParams(
            collective_id=0, has_side_effects=True, vmem_limit_bytes=60 * 1024 * 1024
        ),
        name="block",
    )(tokens, modulation, wq, gains, cache, wo, wu, wd)


def solution(mesh):
    n = mesh.shape["seq"]
    in_specs = (
        P(("groups", "seq"), None),
        P(),
        P(None, None, "seq"),
        P(),
        P(None, None, ("groups", "seq"), None),
        P(None, "seq"),
        P(None, "seq"),
        P("seq", None),
    )
    out_specs = P(("groups", "seq"), None)

    def step(tokens, modulation, w_qkv, norm_gains, cache_kv, w_out, w_up, w_down):
        return fused(
            n,
            tokens,
            modulation,
            jnp.swapaxes(w_qkv, 1, 2),
            norm_gains,
            jnp.swapaxes(cache_kv, 1, 2),
            w_out.T,
            w_up.T,
            w_down,
        )

    return jax.shard_map(step, mesh=mesh, in_specs=in_specs, out_specs=out_specs, check_vma=False)
```

```python
import math

import jax
import jax.numpy as jnp
from jax import lax
from jax.experimental import pallas as pl
from jax.experimental.pallas import tpu as pltpu
from jax.sharding import PartitionSpec as P

HEAD_DIM = 128
HEADS = 20
SLOT = 16
MESH = pl.DeviceIdType.MESH
NT = (((1,), (1,)), ((), ()))
NN = (((1,), (0,)), ((), ()))
F32 = jnp.float32
BF16 = jnp.bfloat16


def factors(n):
    chips = n // 2
    near = 1
    while (2 * near) * (2 * near) <= chips:
        near *= 2
    return chips // near, near


def loop(low, high, fn):
    if high - low <= 16:
        for i in range(low, high):
            fn(i)
        return

    def step(i, c):
        fn(i)
        return c

    lax.fori_loop(low, high, step, 0)


def xor(value, k, size):
    total, bit = 0, 1
    while bit < size:
        digit = lax.rem(lax.div(value, bit), 2)
        other = (k // bit) % 2
        if isinstance(other, int):
            digit = 1 - digit if other else digit
        else:
            digit = lax.rem(digit + other, 2)
        total = total + bit * digit
        bit *= 2
    return total


def remote_copy(src, dst, send, recv, device):
    return pltpu.make_async_remote_copy(
        src_ref=src, dst_ref=dst, send_sem=send, recv_sem=recv, device_id={"seq": device}, device_id_type=MESH
    )


def fold(x):
    total = x[:, :128]
    for k in range(1, x.shape[1] // 128):
        total = total + x[:, 128 * k : 128 * (k + 1)]
    return total


def gelu(x):
    return 0.5 * x * (1.0 + jnp.tanh(math.sqrt(2.0 / math.pi) * (x + 0.044715 * (x * x * x))))


def fused(n, tokens, modulation, wq, gains, cache, wo, wu, wd):
    far, near = factors(n)
    own_rows, features = tokens.shape
    rows = n * own_rows
    width = HEADS * HEAD_DIM
    cols = wq.shape[1]
    wide = math.lcm(cols, HEAD_DIM)
    gs = wide // cols
    blocks = n // gs
    heads = wide // HEAD_DIM
    frames = cache.shape[2]
    held = frames * own_rows
    span = gs // (2 * near)
    part_rows = rows // (2 * span)
    oc = wo.shape[0]
    fl = wu.shape[0]
    chunks = features // wide
    splits = [(0, heads // 2), (heads // 2, heads)]
    pack = own_rows * chunks
    group = wide // oc
    scale = 1.0 / math.sqrt(HEAD_DIM)
    tall = -(-rows // 128) * 128
    assert held <= SLOT // 2 and rows // group == pack and gs % (2 * near) == 0 and far % blocks == 0

    def body(
        tok, mod, wq_h, gains_h, cache_h, wo_h, wu_h, wd_h, out,
        tok_v, mod_v, gains_v, cache_v, wq_v, wo_v, wu_v, wd_v,
        t32, pack32, gt, normed, c32, cown, kv, qacc, qk, sq, st, q32, att,
        gp, res, hacc, hid, own_pack, gate_pack,
        lsem, tsend, trecv, csend, crecv, qsend, qrecv, ssend, srecv, asend, arecv, psend, precv, usend, urecv,
        rsend, r1, r2, r3, *reduces,
    ):
        me = lax.axis_index("seq")
        a, b, c = lax.div(me, 2 * near), lax.rem(lax.div(me, 2), near), lax.rem(me, 2)
        block, place = lax.div(me, gs), lax.rem(me, gs)
        base = block * gs
        part = lax.rem(a, span) * 2 + c

        def dev(a2, b2, c2):
            return (a2 * near + b2) * 2 + c2

        def fetch(k, src, dst):
            copy = pltpu.make_async_copy(src, dst, lsem.at[k])
            copy.start()
            return copy

        barrier = pltpu.get_barrier_semaphore()

        partners = [dev(xor(a, i, far), b, c) for i in range(1, far)]
        partners += [dev(a, xor(b, j, near), c) for j in range(1, near)]
        partners += [dev(xor(a, far - 1, far), xor(b, j, near), c) for j in range(1, near)]
        partners += [dev(a, b, 1 - c)]
        for partner in partners:
            pl.semaphore_signal(barrier, inc=1, device_id={"seq": partner}, device_id_type=MESH)

        get_tok = fetch(0, tok, tok_v)
        get_cache = fetch(1, cache_h, cache_v)
        get_mod = fetch(2, mod, mod_v)
        get_gains = fetch(3, gains_h, gains_v)
        get_wq = fetch(4, wq_h, wq_v)
        get_wo = fetch(5, wo_h, wo_v)
        get_wu = fetch(6, wu_h, wu_v)
        get_wd = fetch(7, wd_h, wd_v)

        def at_pack(d):
            return pl.ds(pl.multiple_of(d * pack, 8), pack)

        def put(d, x):
            for l in range(heads):
                t32[l, at_pack(d), :] = x[:, HEAD_DIM * l : HEAD_DIM * (l + 1)]

        def take(d):
            return jnp.concatenate([t32[l, at_pack(d), :] for l in range(heads)], axis=1)

        def lanes(k):
            return pl.ds(pl.multiple_of(k * wide, wide), wide)

        get_tok.wait()
        for k in range(chunks):
            pack32[own_rows * k : own_rows * (k + 1), :] = tok_v[:, wide * k : wide * (k + 1)].astype(F32)
        put(me, pack32[...])
        gt[me] = pack32[...].astype(BF16)
        get_cache.wait()
        c32[...] = jnp.zeros_like(c32)
        for side in range(2):
            for r in range(own_rows):
                at = SLOT // 2 * side + frames * r
                c32[at : at + frames, :] = cache_v[side, r].astype(F32)
        for k in range(blocks):
            cown[k] = c32[:, wide * k : wide * (k + 1)].astype(BF16)
        kv[me] = c32[:, lanes(block)].astype(BF16)

        pl.semaphore_wait(barrier, len(partners))

        def gather(dst, send, recv, own_part=None):
            def far_copy(i):
                a2 = xor(a, i, far)
                src = dst.at[me] if own_part is None else own_part.at[lax.div(a2 * 2 * near, gs)]
                return remote_copy(src, dst.at[me], send.at[0, i], recv.at[me], dev(a2, b, c))

            def across_copy(j):
                b2 = xor(b, j, near)
                a2 = xor(a, far - 1, far)
                src = dst.at[me] if own_part is None else own_part.at[lax.div(a2 * 2 * near, gs)]
                at = (far - 1) * near + j
                return remote_copy(src, dst.at[me], send.at[1, at], recv.at[me], dev(a2, b2, c))

            def near_copy(i, j):
                row = dev(xor(a, i, far), b, c)
                return remote_copy(
                    dst.at[row], dst.at[row], send.at[1, i * near + j], recv.at[row], dev(a, xor(b, j, near), c)
                )

            def core_copy(i, j):
                row = dev(xor(a, i, far), xor(b, j, near), c)
                return remote_copy(dst.at[row], dst.at[row], send.at[2, i * near + j], recv.at[row], dev(a, b, 1 - c))

            def arrived(row):
                remote_copy(dst.at[row], dst.at[row], send.at[0, 0], recv.at[row], me).wait_recv()

            def begin():
                loop(1, far, lambda i: far_copy(far - 1 - i if i < far - 1 else i).start())
                loop(1, near, lambda j: across_copy(j).start())

            def begin_near():
                loop(1, near, lambda j: near_copy(0, j).start())
                core_copy(0, 0).start()

            def forward(use, low=1, high=far):
                def one(i):
                    row = dev(xor(a, i, far), b, c)
                    arrived(row)
                    if not isinstance(i, int) or i < far - 1:
                        loop(1, near, lambda j: near_copy(i, j).start())
                    core_copy(i, 0).start()
                    use(row)

                loop(low, high, one)

            def across(use, low=0, high=far * (near - 1)):
                def one(m):
                    i, j = m % far, 1 + m // far
                    row = dev(xor(a, i, far), xor(b, j, near), c)
                    arrived(row)
                    core_copy(i, j).start()
                    use(row)

                loop(low, high, one)

            def finish(use):
                def one(m):
                    row = dev(xor(a, m % far, far), xor(b, m // far, near), 1 - c)
                    arrived(row)
                    use(row)

                loop(0, far * near, one)

            def drain():
                loop(1, far, lambda i: far_copy(i).wait_send())
                loop(0, (far - 1) * (near - 1), lambda m: near_copy(m % (far - 1), 1 + m // (far - 1)).wait_send())
                loop(1, near, lambda j: across_copy(j).wait_send())
                loop(0, far * near, lambda m: core_copy(m % far, m // far).wait_send())

            return begin, begin_near, forward, across, finish, drain

        nothing = lambda row: None
        t_begin, t_near, t_forward, t_across, t_finish, t_drain = gather(gt, tsend, trecv)
        c_begin, c_near, c_forward, c_across, c_finish, c_drain = gather(kv, csend, crecv, cown)

        def ingest(row):
            put(row, gt[row].astype(F32))

        t_begin()
        t_near()
        c_begin()
        t_forward(ingest)
        t_across(ingest)
        c_near()
        c_forward(nothing)
        t_finish(ingest)

        def token_chunk(k):
            return jnp.concatenate(
                [
                    jnp.concatenate(
                        [t32[l, pl.ds(own_rows * k + r, n, stride=pack), :] for r in range(own_rows)], axis=0
                    )
                    for l in range(heads)
                ],
                axis=1,
            )

        def to_lines(first, second):
            x = jnp.where(lax.broadcasted_iota(jnp.int32, (rows, 128), 1) == 0, first, second)
            if tall > rows:
                x = jnp.concatenate([x, jnp.zeros((tall - rows, 128), F32)], axis=0)
            return x.T[:2, :rows]

        def to_columns(x):
            if tall > rows:
                x = jnp.concatenate([x, jnp.zeros((2, tall - rows), F32)], axis=1)
            return jnp.concatenate([x, jnp.zeros((6, tall), F32)], axis=0).T[:rows]

        def layer_norm(chunk, shift, gain):
            total = jnp.zeros((rows, 128), F32)
            for k in range(chunks):
                total = total + fold(chunk(k))
            mean = jnp.sum(total, axis=-1, keepdims=True) * (1.0 / features)
            total = jnp.zeros((rows, 128), F32)
            for k in range(chunks):
                center = chunk(k) - mean
                total = total + fold(center * center)
            inverse = lax.rsqrt(jnp.sum(total, axis=-1, keepdims=True) * (1.0 / features) + 1e-06)
            for k in range(chunks):
                s = slice(wide * k, wide * (k + 1))
                normed[:, s] = (
                    (chunk(k) - mean) * inverse * (1.0 + mod_v[gain : gain + 1, s]) + mod_v[shift : shift + 1, s]
                ).astype(BF16)

        get_mod.wait()
        layer_norm(token_chunk, 0, 1)

        get_wq.wait()
        depth = features // 4
        qacc[...] = jnp.zeros_like(qacc)

        def project(k, carry):
            s = pl.ds(pl.multiple_of(k * depth, depth), depth)
            x = normed[:, s]
            if cols % 16 == 0:
                qacc[...] += lax.dot_general(
                    x, wq_v[:, :, s].reshape(3 * cols, depth), NT, preferred_element_type=F32
                )
            else:
                for i in range(3):
                    qacc[:, cols * i : cols * (i + 1)] += lax.dot_general(
                        x, wq_v[i, :, s], NT, preferred_element_type=F32
                    )
            return carry

        lax.fori_loop(0, 4, project, 0)
        rounded = qacc[...].astype(BF16)
        qk[place] = rounded

        def peer(i):
            return remote_copy(
                qk.at[place], qk.at[place], qsend.at[i], qrecv.at[place], base + xor(place, i, gs)
            )

        loop(1, gs, lambda i: peer(gs - i).start())
        exact = rounded.astype(F32)
        square = exact * exact
        sq[me] = to_lines(
            jnp.sum(square[:, :cols], axis=-1, keepdims=True), jnp.sum(square[:, cols : 2 * cols], axis=-1, keepdims=True)
        )

        def spread(i):
            return remote_copy(sq.at[me], sq.at[me], ssend.at[i], srecv.at[me], lax.rem(me + i, n))

        loop(1, n, lambda i: spread(i).start())
        c_across(nothing)

        def squares_in(i):
            row = lax.rem(me + i, n)
            remote_copy(sq.at[row], sq.at[row], ssend.at[i], srecv.at[row], me).wait_recv()

        t_drain()
        loop(1, n, squares_in)
        both = lax.rsqrt(jnp.sum(sq[...], axis=0) * (1.0 / width) + 1e-06)
        inverse = to_columns(both)

        def peer_in(i):
            row = xor(place, i, gs)
            remote_copy(qk.at[row], qk.at[row], qsend.at[i], qrecv.at[row], me).wait_recv()

        loop(1, gs, peer_in)
        get_gains.wait()

        def whole(i):
            return jnp.concatenate([qk[p, :, cols * i : cols * (i + 1)].astype(F32) for p in range(gs)], axis=1)

        q32[...] = whole(0) * inverse[:, 0:1] * gains_v[0:1, lanes(block)]
        keys = (whole(1) * inverse[:, 1:2] * gains_v[1:2, lanes(block)]).astype(BF16)
        values = whole(2).astype(BF16)
        queries = q32[pl.ds(pl.multiple_of(part * part_rows, 8), part_rows), :].astype(BF16)

        c_finish(nothing)
        spot = lax.rem(lax.broadcasted_iota(jnp.int32, (part_rows, n * SLOT), 1), SLOT)
        columns = [slice(HEAD_DIM * h, HEAD_DIM * (h + 1)) for h in range(heads)]
        cached = [kv[:, :, s].reshape(n * SLOT, HEAD_DIM) for s in columns]
        scores = []
        for h, s in enumerate(columns):
            old = lax.dot_general(queries[:, s], cached[h], NT, preferred_element_type=F32) * scale
            new = lax.dot_general(queries[:, s], keys[:, s], NT, preferred_element_type=F32) * scale
            scores.append((jnp.where(spot < held, old, -jnp.inf), new))
        weights = []
        for old, new in scores:
            peak = jnp.maximum(jnp.max(old, axis=-1, keepdims=True), jnp.max(new, axis=-1, keepdims=True))
            old, new = jnp.exp(old - peak), jnp.exp(new - peak)
            total = jnp.sum(old, axis=-1, keepdims=True) + jnp.sum(new, axis=-1, keepdims=True)
            weights.append((pltpu.roll(old, SLOT // 2, axis=1).astype(BF16), new.astype(BF16), total))
        outs = []
        for h, s in enumerate(columns):
            old, new, total = weights[h]
            summed = lax.dot_general(old, cached[h], NN, preferred_element_type=F32) + lax.dot_general(
                new, values[:, s], NN, preferred_element_type=F32
            )
            outs.append((summed / total).astype(BF16))
        att[a, c] = jnp.concatenate(outs, axis=1)

        def att_far(i):
            return remote_copy(
                att.at[a, c], att.at[a, c], asend.at[0, i], arecv.at[a, c], dev(xor(a, i, far), b, c)
            )

        def att_core(i):
            a2 = xor(a, i, far)
            return remote_copy(
                att.at[a2, c], att.at[a2, c], asend.at[1, i], arecv.at[a2, c], dev(a, b, 1 - c)
            )

        def att_in(a2, c2):
            remote_copy(att.at[a2, c2], att.at[a2, c2], asend.at[0, 0], arecv.at[a2, c2], me).wait_recv()

        loop(1, far, lambda i: att_far(far - i).start())
        att_core(0).start()

        c_drain()
        loop(1, gs, lambda i: peer(i).wait_send())
        loop(1, n, lambda i: spread(i).wait_send())

        mine = lax.div(me, group)
        turn = lax.rem(wide - lax.rem(me, group) * oc, wide)

        def own_columns(x):
            return pltpu.roll(x, turn, axis=1)[:, :oc]

        own_tokens = own_columns(token_chunk(mine))
        own_gate = own_columns(jnp.broadcast_to(mod_v[2:3, lanes(mine)], (8, wide)))[0:1]

        def att_pass(i):
            att_in(xor(a, i, far), c)
            att_core(i).start()

        def head_block(first, s):
            x = att[pl.ds(first, span)].astype(F32).reshape(rows, wide).astype(BF16)
            return lax.dot_general(x, wo_v[:, s], NT, preferred_element_type=F32)

        get_wo.wait()
        projected = jnp.zeros((rows, oc), F32)
        if span == 1 and far <= 8:
            for i in range(far):
                if i == 0:
                    loop(1, far, att_pass)
                a2 = xor(a, i, far)
                att_in(a2, 1 - c)
                projected = projected + head_block(a2, lanes(a2))
        else:
            loop(1, far, att_pass)
            loop(0, far, lambda i: att_in(xor(a, i, far), 1 - c))
            for k in range(blocks):
                projected = projected + head_block(span * k, slice(wide * k, wide * (k + 1)))
        projected = projected.astype(BF16).astype(F32)
        gp[me] = jnp.concatenate([projected[pack * g : pack * (g + 1)] for g in range(group)], axis=1).astype(BF16)

        p_begin, p_near, p_forward, p_across, p_finish, p_drain = gather(gp, psend, precv)

        partly = own_tokens + own_gate * projected
        mean = jnp.sum(partly, axis=-1, keepdims=True) * (1.0 / oc)
        partly = partly - mean
        square = jnp.sum(partly * partly, axis=-1, keepdims=True)
        st[me] = to_lines(mean, square)

        def tell(i):
            return remote_copy(st.at[me], st.at[me], usend.at[i], urecv.at[me], lax.rem(me + i, n))

        loop(1, n, lambda i: tell(i).start())

        p_begin()
        p_near()
        loop(1, far, lambda i: att_far(i).wait_send())
        loop(0, far, lambda i: att_core(i).wait_send())

        def told(i):
            row = lax.rem(me + i, n)
            remote_copy(st.at[row], st.at[row], usend.at[i], urecv.at[row], me).wait_recv()

        def statistics():
            loop(1, n, told)
            means, squares = st[:, 0], st[:, 1]
            middle = jnp.sum(means, axis=0, keepdims=True) * (1.0 / n)
            apart = means - middle
            spread_ = jnp.sum(squares + oc * (apart * apart), axis=0, keepdims=True) * (1.0 / features)
            both = to_columns(jnp.concatenate([middle, lax.rsqrt(spread_ + 1e-06)], axis=0))
            return both[:, 0:1], both[:, 1:2]

        def residual_chunk(k):
            pieces = [gp[group * k + j].astype(F32) for j in range(group)]
            full = jnp.concatenate(
                [
                    jnp.concatenate([piece[:, oc * g : oc * (g + 1)] for piece in pieces], axis=1)
                    for g in range(group)
                ],
                axis=0,
            )
            return token_chunk(k) + mod_v[2:3, lanes(k)] * full

        def grow(k, first, middle, inverse):
            s = lanes(k)
            x = residual_chunk(k)
            res[:, s] = x
            x = ((x - middle) * inverse * (1.0 + mod_v[4:5, s]) + mod_v[3:4, s]).astype(BF16)
            y = lax.dot_general(x, wu_v[:, s], NT, preferred_element_type=F32)
            hacc[...] = y if first else hacc[...] + y

        if group == 2 and far == 4:

            def chunk_of(i, j, first=False):
                a2, b2 = xor(a, i, far), xor(b, j, near)
                row = dev(a2, b2, 1 - c)
                remote_copy(gp.at[row], gp.at[row], psend.at[0, 0], precv.at[row], me).wait_recv()
                grow(a2 * near + b2, first, *stats)

            p_forward(nothing, 1, 3)
            p_across(nothing, 0, 1)
            p_forward(nothing, 3, 4)
            stats = statistics()
            get_wu.wait()
            chunk_of(0, 0, True)
            chunk_of(1, 0)
            chunk_of(0, 1)
            p_across(nothing, 3, 4)
            chunk_of(2, 0)
            p_across(nothing, 1, 2)
            chunk_of(3, 0)
            p_across(nothing, 2, 3)
            chunk_of(3, 1)
            chunk_of(1, 1)
            chunk_of(2, 1)
        else:
            p_forward(nothing)
            p_across(nothing)
            p_finish(nothing)
            stats = statistics()
            get_wu.wait()
            hacc[...] = jnp.zeros_like(hacc)
            lax.fori_loop(0, chunks, lambda k, carry: (grow(k, False, *stats), carry)[1], 0)

        hid[...] = gelu(hacc[...]).astype(BF16)
        get_wd.wait()

        def part_of(q):
            first, last = splits[q]
            p16, got1, sum1, got2, sum2, got3 = reduces[6 * q : 6 * q + 6]
            span_l = range(first, last)

            def own_sum(d):
                return jnp.concatenate([t32[l, at_pack(d), :] for l in span_l], axis=1)

            def down():
                for k in range(chunks):
                    s = slice(wide * k + HEAD_DIM * first, wide * k + HEAD_DIM * last)
                    y = lax.dot_general(hid[...], wd_v[:, s], NN, preferred_element_type=F32)
                    for r in range(own_rows):
                        for l in span_l:
                            at = HEAD_DIM * (l - first)
                            t32[l, pl.ds(own_rows * k + r, n, stride=pack), :] = y[
                                n * r : n * (r + 1), at : at + HEAD_DIM
                            ]

            def copy1(m):
                i, j = far - 1 - m // near, near - 1 - m % near
                chip = xor(a, i, far) * near + xor(b, j, near)
                return chip, remote_copy(
                    p16.at[chip], got1.at[chip], rsend.at[q, 0, m], r1.at[q, chip], dev(a, b, 1 - c)
                )

            def hand(m):
                chip, copy = copy1(m)
                p16[chip] = own_sum(2 * chip + 1 - c).astype(BF16)
                copy.start()

            def pair(chip):
                remote_copy(got1.at[chip], got1.at[chip], rsend.at[q, 0, 0], r1.at[q, chip], me).wait_recv()
                return own_sum(2 * chip + c) + got1[chip].astype(F32)

            def copy_straight(j):
                a2, b2 = xor(a, far - 1, far), xor(b, j, near)
                chip = a2 * near + b2
                at = a * near + b
                return chip, remote_copy(
                    sum1.at[chip], got3.at[at], rsend.at[q, 3, j], r3.at[q, at], dev(a2, b2, c)
                )

            def straight(j):
                chip, copy = copy_straight(j)
                sum1[chip] = pair(chip).astype(BF16)
                copy.start()

            def copy2(m):
                i, j = far - 2 - m // (near - 1), near - 1 - m % (near - 1)
                a2, b2 = xor(a, i, far), xor(b, j, near)
                chip = a2 * near + b2
                at = a2 * near + b
                return chip, remote_copy(sum1.at[chip], got2.at[at], rsend.at[q, 1, m], r2.at[q, at], dev(a, b2, c))

            def second(m):
                chip, copy = copy2(m)
                sum1[chip] = pair(chip).astype(BF16)
                copy.start()

            def collect(i):
                a2 = xor(a, i, far)
                total = pair(a2 * near + b)
                for j in range(1, near):
                    at = a2 * near + xor(b, j, near)
                    remote_copy(got2.at[at], got2.at[at], rsend.at[q, 1, 0], r2.at[q, at], me).wait_recv()
                    total = total + got2[at].astype(F32)
                return a2, total

            def copy3(i):
                a2 = xor(a, i, far)
                at = a * near + b
                return remote_copy(sum2.at[a2], got3.at[at], rsend.at[q, 2, i], r3.at[q, at], dev(a2, b, c))

            def third(m):
                i = far - 1 - m
                a2, total = collect(i)
                sum2[a2] = total.astype(BF16)
                copy3(i).start()

            def last_sum():
                _, total = collect(0)
                for i in range(1, far):
                    for j in range(near if i == far - 1 else 1):
                        at = xor(a, i, far) * near + xor(b, j, near)
                        remote_copy(got3.at[at], got3.at[at], rsend.at[q, 2, 0], r3.at[q, at], me).wait_recv()
                        total = total + got3[at].astype(F32)
                s = slice(HEAD_DIM * first, HEAD_DIM * last)
                pack32[:, s] = own_pack[:, s] + gate_pack[:, s] * total

            def early_drain():
                loop(0, far * near, lambda m: copy1(m)[1].wait_send())

            def drain():
                loop(0, near, lambda j: copy_straight(j)[1].wait_send())
                loop(0, (far - 1) * (near - 1), lambda m: copy2(m)[1].wait_send())
                loop(1, far - 1, lambda i: copy3(i).wait_send())

            stages = [
                down,
                lambda: loop(0, far * near, hand),
                lambda: (loop(0, near, straight), loop(0, (far - 1) * (near - 1), second)),
                lambda: loop(1, far - 1, third),
                last_sum,
            ]
            return stages, early_drain, drain

        todo = [part_of(q) for q in range(len(splits))]
        for stages, _, _ in todo:
            stages[0]()
            stages[1]()
        for step in range(2, 5):
            for stages, _, _ in todo:
                stages[step]()
            if step == 2:
                p_drain()
                loop(1, n, lambda i: tell(i).wait_send())
                for _, early_drain, _ in todo:
                    early_drain()
                for k in range(chunks):
                    s = slice(wide * k, wide * (k + 1))
                    for r in range(own_rows):
                        at = own_rows * k + r
                        own_pack[at : at + 1, :] = res[pl.ds(me + n * r, 1), s]
                        gate_pack[at : at + 1, :] = mod_v[5:6, s]
        for k in range(chunks):
            s = slice(wide * k, wide * (k + 1))
            out[:, s] = pack32[own_rows * k : own_rows * (k + 1), :].astype(BF16)
        for _, _, drain in todo:
            drain()

    def vmem(shape, dtype):
        return pltpu.VMEM(shape, dtype)

    dma = pltpu.SemaphoreType.DMA
    chips = far * near
    packed = (pack, wide)
    return pl.pallas_call(
        body,
        out_shape=jax.ShapeDtypeStruct(tokens.shape, BF16),
        in_specs=[pl.BlockSpec(memory_space=pl.ANY)] * 8,
        out_specs=pl.BlockSpec(memory_space=pltpu.VMEM),
        scratch_shapes=[
            vmem(tokens.shape, BF16),
            vmem(modulation.shape, F32),
            vmem(gains.shape, F32),
            vmem(cache.shape, BF16),
            vmem(wq.shape, BF16),
            vmem(wo.shape, BF16),
            vmem(wu.shape, BF16),
            vmem(wd.shape, BF16),
            vmem((heads, n * pack, HEAD_DIM), F32),
            vmem(packed, F32),
            vmem((n,) + packed, BF16),
            vmem((rows, features), BF16),
            vmem((SLOT, width), F32),
            vmem((blocks, SLOT, wide), BF16),
            vmem((n, SLOT, wide), BF16),
            vmem((rows, 3 * cols), F32),
            vmem((gs, rows, 3 * cols), BF16),
            vmem((n, 2, rows), F32),
            vmem((n, 2, rows), F32),
            vmem((rows, wide), F32),
            vmem((far, 2, part_rows, wide), BF16),
            vmem((n,) + packed, BF16),
            vmem((rows, features), F32),
            vmem((rows, fl), F32),
            vmem((rows, fl), BF16),
            vmem(packed, F32),
            vmem(packed, F32),
            dma((8,)),
            dma((3, chips)),
            dma((n,)),
            dma((3, chips)),
            dma((n,)),
            dma((gs,)),
            dma((gs,)),
            dma((n,)),
            dma((n,)),
            dma((2, far)),
            dma((far, 2)),
            dma((3, chips)),
            dma((n,)),
            dma((n,)),
            dma((n,)),
            dma((len(splits), 4, chips)),
            dma((len(splits), chips)),
            dma((len(splits), chips)),
            dma((len(splits), chips)),
        ]
        + [
            vmem((lines, pack, HEAD_DIM * (last - first)), BF16)
            for first, last in splits
            for lines in (chips, chips, chips, chips, far, chips)
        ],
        compiler_params=pltpu.CompilerParams(
            collective_id=0, has_side_effects=True, vmem_limit_bytes=60 * 1024 * 1024
        ),
        name="block",
    )(tokens, modulation, wq, gains, cache, wo, wu, wd)


def solution(mesh):
    n = mesh.shape["seq"]
    in_specs = (
        P(("groups", "seq"), None),
        P(),
        P(None, None, "seq"),
        P(),
        P(None, None, ("groups", "seq"), None),
        P(None, "seq"),
        P(None, "seq"),
        P("seq", None),
    )
    out_specs = P(("groups", "seq"), None)

    def step(tokens, modulation, w_qkv, norm_gains, cache_kv, w_out, w_up, w_down):
        return fused(
            n,
            tokens,
            modulation,
            jnp.swapaxes(w_qkv, 1, 2),
            norm_gains,
            jnp.swapaxes(cache_kv, 1, 2),
            w_out.T,
            w_up.T,
            w_down,
        )

    return jax.shard_map(step, mesh=mesh, in_specs=in_specs, out_specs=out_specs, check_vma=False)
```
